128 devices in a mesh: section: 2 (over core), grid: 64 (over z, x, y).
Axes of the slice: x: 4, y: 4, z: 4, core: 2. Of those that a mesh axis runs over, the one named last changes fastest.
Arguments:
- visibilities: float32 [2, 6144, 2, 2, 16, 128], P('section', 'grid'), may hold values from -6 to 6
- uv_coords: float32 [6144, 2, 128], P('grid'), may hold values from -8 to 8
- w_terms: float32 [6144], P('grid'), may hold values from -40 to 40
- stations: int32 [2, 6144], P(None, 'grid'), may hold values from 0 to 511
- tile_ids: int32 [6144], P('grid'), may hold values from 0 to 16383, as said below
- owner_map: int32 [16384], replicated, may hold values from 0 to 16383, as said below
- jones_gains: float32 [512, 128], replicated, may hold values from -4.2 to 4.2
Outputs:
- grid_tiles: float32 [2, 16384, 2048], P('section', 'grid')
The draws below stay inside these ranges and needn't reach their ends.
Inputs may be any that keep to these rules, and one draw needn't show every extreme that they name: `tile_ids`: of the 96 subgrids of one index of grid, at most 4 have tiles held by any one index of grid (index owner_map[tile] // 256), and these lie on at most 2 distinct tiles. `owner_map`: each of 0 to 16383 exactly once.
All inputs are finite; a program needn't handle non-finite values.
Results may differ from the reference program's by a relative error of at most 0.0036.
Values sent between devices are 32-bit elements; how exact they have to be, the bound alone decides.
No kernel may reach another device: no remote copies, remote signals or barrier semaphores. Data moves between devices by JAX's collectives and lax.ppermute only.
A program may use at most 128 MiB of HBM per device.

```python
import math
import jax
import jax.numpy as jnp
from jax import lax

SUBGRID = 32
CHAN = 16
TSG = 128
STATIONS = 512
SUB_DEV = 96
TILES_DEV = 256
SUBGRIDS = 6144
TILES = 16384
CAP = 4


def tile_layout(key):
    base_key = jax.random.fold_in(key, 11)
    perm_key, hot_key, offset_key, order_key = jax.random.split(base_key, 4)
    grid_count = SUBGRIDS // SUB_DEV
    held_tile = jax.random.permutation(perm_key, TILES).astype(jnp.int32)
    owner_table = jnp.zeros((TILES,), jnp.int32).at[held_tile].set(jnp.arange(TILES, dtype=jnp.int32))
    hot_owner = jax.random.randint(hot_key, (), 0, grid_count)
    offsets = jax.random.randint(offset_key, (grid_count, grid_count), 0, TILES_DEV)
    spread = max(CAP // 3, 1)
    item_rank = jnp.arange(SUB_DEV, dtype=jnp.int32)
    is_hot = item_rank < CAP
    later_rank = jnp.maximum(item_rank - CAP, 0)
    other_rank = later_rank % (grid_count - 1)
    owner_rank = jnp.where(is_hot, hot_owner, (hot_owner + 1 + other_rank) % grid_count)
    place_step = jnp.where(is_hot, item_rank % spread, later_rank // (grid_count - 1))
    column = jnp.where(is_hot, 0, other_rank + 1)
    slot_index = (offsets[:, column] + place_step[None, :]) % TILES_DEV
    position = owner_rank[None, :] * TILES_DEV + slot_index
    order_keys = jax.random.split(order_key, grid_count)
    shuffles = jax.vmap(lambda one_key: jax.random.permutation(one_key, SUB_DEV))(order_keys)
    position = jnp.take_along_axis(position, shuffles, axis=1)
    return (held_tile[position.reshape(-1)].astype(jnp.int32), owner_table)


def draw_tile_ids(key, part):
    return tile_layout(key)[0]


def draw_owner_map(key, part):
    return tile_layout(key)[1]


def touch_ends(values, own_key, low, largest):
    dims = values.shape
    place = [jax.random.randint(jax.random.fold_in(own_key, axis), (), 0, dims[axis]) for axis in range(len(dims))]
    values = values.at[tuple(place)].set(low)
    longest = dims.index(max(dims))
    place[longest] = (place[longest] + 1) % dims[longest]
    return values.at[tuple(place)].set(largest)


def steps_of(stream_key, shape, cuts, smallest, largest):
    gain = 1.0
    for axis_at, shards_of in cuts:
        heights = jax.random.uniform(jax.random.fold_in(jax.random.fold_in(stream_key, 6), axis_at), (shards_of,), jnp.float32, smallest / len(cuts), largest / len(cuts))
        gain = gain * jnp.repeat(jnp.exp(heights), shape[axis_at] // shards_of).reshape((-1,) + (1,) * (len(shape) - 1 - axis_at))
    return gain


def bell_draw(own_key, extent, deviation, reach, cuts=(), kind=jnp.bfloat16):
    array = deviation * jax.random.normal(own_key, extent, jnp.float32)
    if cuts:
        array = array * steps_of(own_key, extent, cuts, -0.22, 0.18)
    return jnp.clip(array, -reach, reach).astype(kind)


def setup_inputs(seed: int = 0) -> dict:
    streams_of = jax.random.split(jax.random.key(seed), 8)
    return {
        "visibilities": bell_draw(streams_of[0], (2, SUBGRIDS, 2, 2, CHAN, TSG), 1.0, 6.0, ((0, 2), (1, 64)), jnp.float32),
        "uv_coords": jnp.clip(jax.random.uniform(streams_of[1], (SUBGRIDS, 2, TSG), jnp.float32, -8.0, 8.0) * steps_of(streams_of[1], (SUBGRIDS, 2, TSG), ((0, 64),), -0.4, 0.0), -8.0, 8.0),
        "w_terms": jnp.clip(jax.random.uniform(streams_of[2], (SUBGRIDS,), jnp.float32, -40.0, 40.0) * steps_of(streams_of[2], (SUBGRIDS,), ((0, 64),), -0.4, 0.0), -40.0, 40.0),
        "stations": touch_ends(jax.random.randint(streams_of[3], (2, SUBGRIDS), 0, STATIONS), jax.random.fold_in(streams_of[3], 1), 0, STATIONS - 1).astype(jnp.int32),
        "tile_ids": draw_tile_ids(jax.random.fold_in(streams_of[7], 71), 0),
        "owner_map": draw_owner_map(jax.random.fold_in(streams_of[7], 71), 0),
        "jones_gains": bell_draw(streams_of[6], (STATIONS, CHAN * 8), 0.7, 4.2, (), jnp.float32),
    }


def station_gains(station_pair, jones_gains):
    table_rows = jones_gains.shape[0]
    picked = (station_pair.reshape(-1)[:, None] == jnp.arange(table_rows, dtype=jnp.int32)[None, :]).astype(jnp.float32)
    looked = jnp.dot(picked, jones_gains, precision=lax.Precision.HIGHEST, preferred_element_type=jnp.float32)
    return looked.reshape(2, station_pair.shape[1], jones_gains.shape[1] // 8, 2, 2, 2)

def jones_term(vis_rows, gain_p, gain_q):
    total_real = jnp.zeros(vis_rows.shape[:1] + vis_rows.shape[3:], jnp.float32)
    total_imag = jnp.zeros(vis_rows.shape[:1] + vis_rows.shape[3:], jnp.float32)
    for d in range(2):
        coef_real = (gain_p[..., 0] * gain_q[:, :, d, 0] + gain_p[..., 1] * gain_q[:, :, d, 1])[..., None]
        coef_imag = (gain_p[..., 1] * gain_q[:, :, d, 0] - gain_p[..., 0] * gain_q[:, :, d, 1])[..., None]
        vis_real = vis_rows[:, d, 0]
        vis_imag = vis_rows[:, d, 1]
        total_real = total_real + coef_real * vis_real - coef_imag * vis_imag
        total_imag = total_imag + coef_real * vis_imag + coef_imag * vis_real
    return jnp.stack([total_real, total_imag], 1)

def subgrid_tiles(corrected, coords, w_group):
    groups = corrected.shape[0]
    samples = corrected.shape[2]
    steps_t = coords.shape[2]
    chan_count = samples // steps_t
    side = SUBGRID
    freq_scale = 1.0 + jnp.arange(chan_count, dtype=jnp.float32) / (4.0 * chan_count)
    cell_pos = (coords[:, :, None, :] * freq_scale[None, None, :, None]).reshape(groups, 2, samples)
    pixel_pos = jnp.arange(side, dtype=jnp.float32) - side // 2
    phase_angle = 2.0 * jnp.pi / side * cell_pos[:, :, None, :] * pixel_pos[None, None, :, None]
    wave_real = jnp.cos(phase_angle)
    wave_imag = jnp.sin(phase_angle)
    vis_real = corrected[:, 0][:, None, :]
    vis_imag = corrected[:, 1][:, None, :]
    weighted = jnp.concatenate([wave_real[:, 0] * vis_real - wave_imag[:, 0] * vis_imag, wave_real[:, 0] * vis_imag + wave_imag[:, 0] * vis_real], 1).astype(jnp.bfloat16)
    basis = jnp.concatenate([wave_real[:, 1], wave_imag[:, 1]], 1).astype(jnp.bfloat16)
    product = jnp.einsum('nxk,nyk->nxy', weighted.astype(jnp.float32), basis.astype(jnp.float32))
    image_real = product[:, :side, :side] - product[:, side:, side:]
    image_imag = product[:, :side, side:] + product[:, side:, :side]
    taper_line = jnp.cos(jnp.pi * pixel_pos / (side + 4.0))
    sine_pos = 0.6 * pixel_pos / side
    n_term = jnp.sqrt(1.0 - sine_pos[:, None] ** 2 - sine_pos[None, :] ** 2) - 1.0
    w_phase = 2.0 * jnp.pi * w_group[:, None, None] * n_term[None]
    norm_scale = taper_line[:, None] * taper_line[None, :] / math.sqrt(samples)
    turn_real = jnp.cos(w_phase) * norm_scale
    turn_imag = jnp.sin(w_phase) * norm_scale
    field_real = image_real * turn_real - image_imag * turn_imag
    field_imag = image_real * turn_imag + image_imag * turn_real
    dft_angle = -2.0 * jnp.pi / side * pixel_pos[:, None] * pixel_pos[None, :]
    dft_real = jnp.cos(dft_angle)
    dft_imag = jnp.sin(dft_angle)
    highest = lax.Precision.HIGHEST

    def apply_right(values, matrix):
        return jnp.einsum('nxy,ly->nxl', values, matrix, precision=highest)

    def apply_left(matrix, values):
        return jnp.einsum('jx,nxl->njl', matrix, values, precision=highest)
    half_real = apply_right(field_real, dft_real) - apply_right(field_imag, dft_imag)
    half_imag = apply_right(field_real, dft_imag) + apply_right(field_imag, dft_real)
    uv_real = apply_left(dft_real, half_real) - apply_left(dft_imag, half_imag)
    uv_imag = apply_left(dft_real, half_imag) + apply_left(dft_imag, half_real)
    return jnp.concatenate([uv_real, uv_imag], 1).reshape(groups, 2 * side * side) / side

def reference(visibilities, uv_coords, w_terms, stations, tile_ids, owner_map, jones_gains):
    groups = SUBGRIDS // 32
    vis_grouped = jnp.swapaxes(visibilities.reshape(2, groups, 32, 2, 2, CHAN, TSG), 0, 1)
    coord_grouped = uv_coords.reshape(groups, 32, 2, TSG)
    w_grouped = w_terms.reshape(groups, 32)
    station_grouped = jnp.swapaxes(stations.reshape(2, groups, 32), 0, 1)

    def grid_group(packed):
        vis_group, coord_group, w_group, station_group = packed
        gain_sets = station_gains(station_group, jones_gains)
        polar_tiles = []
        for polar_index in range(2):
            corrected = jones_term(vis_group[0], gain_sets[0][:, :, polar_index, 0], gain_sets[1][:, :, polar_index])
            corrected = corrected + jones_term(vis_group[1], gain_sets[0][:, :, polar_index, 1], gain_sets[1][:, :, polar_index])
            corrected = corrected.reshape(32, 2, CHAN * TSG)
            polar_tiles.append(subgrid_tiles(corrected, coord_group, w_group))
        return jnp.stack(polar_tiles, 0)
    tiles_out = lax.map(grid_group, (vis_grouped, coord_grouped, w_grouped, station_grouped))
    uv_sub = jnp.swapaxes(tiles_out, 0, 1).reshape(2, SUBGRIDS, 2 * SUBGRID * SUBGRID)
    positions = owner_map[tile_ids]
    return jnp.zeros((2, TILES, 2 * SUBGRID * SUBGRID), jnp.float32).at[:, positions].add(uv_sub)
```

```python
import math

import numpy as np
import jax
import jax.numpy as jnp
from jax import lax
from jax.experimental import pallas as pl
from jax.experimental.pallas import tpu as pltpu
from jax.sharding import PartitionSpec as P

SIDE = 32
HALF = 16
CHUNKS = 2
GROUP = 4

PIXELS = np.concatenate([np.arange(16), -1 - np.arange(16)]).astype(np.float64)


def fit_even(function, reach, terms):
    nodes = np.cos(np.pi * (np.arange(64) + 0.5) / 64)
    square = (nodes + 1.0) / 2.0 * reach * reach
    cheb = np.polynomial.chebyshev.chebfit(nodes, function(np.sqrt(square)), terms - 1)
    poly = np.polynomial.chebyshev.cheb2poly(cheb)
    shift = np.polynomial.polynomial.Polynomial(poly)(
        np.polynomial.polynomial.Polynomial([-1.0, 2.0 / (reach * reach)])
    )
    return [float(np.float32(value)) for value in shift.coef]


def sinc_turns(scale):
    return lambda x: np.where(x > 0, np.sin(scale * x) / np.maximum(x, 1e-30), scale)


HALF_SIN = fit_even(sinc_turns(np.pi), 0.5, 6)
HALF_COS = fit_even(lambda x: np.cos(np.pi * x), 0.5, 6)
STEP_SIN = fit_even(sinc_turns(2 * np.pi), 0.0625, 4)
STEP_COS = fit_even(lambda x: np.cos(2 * np.pi * x), 0.0625, 4)


def horner(coefs, square):
    total = square * coefs[-1] + coefs[-2]
    for value in coefs[-3::-1]:
        total = total * square + value
    return total


def sincos_half(x):
    square = x * x
    half_sin = x * horner(HALF_SIN, square)
    half_cos = horner(HALF_COS, square)
    twice = half_sin + half_sin
    return twice * half_cos, 1.0 - twice * half_sin


def sincos_step(x):
    square = x * x
    return x * horner(STEP_SIN, square), horner(STEP_COS, square)


def spread(ref, g, k, c):
    line = ref[g, k, pl.ds(c, 8, stride=0), :]
    return jnp.concatenate([line, line], 0)


def split_hi_lo(values):
    high = values.astype(jnp.bfloat16)
    low = (values - high.astype(jnp.float32)).astype(jnp.bfloat16)
    return high, low


def np_split(values):
    high = np.asarray(values, np.float32).astype(jnp.bfloat16)
    low = (np.asarray(values, np.float32) - high.astype(np.float32)).astype(jnp.bfloat16)
    return high, low


def tables(samples):
    lane = np.arange(128)
    lane_ri, lane_pol, lane_pix = lane // 64, (lane // 32) % 2, lane % 32
    row_p = PIXELS[:, None]
    lane_p = PIXELS[lane_pix][None, :]
    sine_row, sine_lane = 0.6 * row_p / SIDE, 0.6 * lane_p / SIDE
    n_term = np.sqrt(1.0 - sine_row**2 - sine_lane**2) - 1.0
    taper = np.cos(np.pi * row_p / (SIDE + 4.0)) * np.cos(np.pi * lane_p / (SIDE + 4.0))
    norm = taper / math.sqrt(samples) / SIDE
    signed = norm * np.where(lane_ri == 0, -1.0, 1.0)[None, :]
    pixel_tables = np.stack([n_term, norm, signed]).astype(np.float32)

    freq = np.arange(SIDE) - SIDE // 2
    angle = 2.0 * np.pi / SIDE * PIXELS[:, None] * freq[None, :]
    cos_t, sin_t = np.cos(angle), np.sin(angle)
    right = np.zeros((2, 2, 32, 2, 2, 2, 32))
    for pol in range(2):
        re_re, re_im = cos_t, -sin_t
        im_re, im_im = sin_t, cos_t
        right[0, pol, :, 0, 0, pol, :] = re_re
        right[0, pol, :, 0, 1, pol, :] = re_im
        right[1, pol, :, 0, 0, pol, :] = im_re
        right[1, pol, :, 0, 1, pol, :] = im_im
        right[0, pol, :, 1, 0, pol, :] = re_im
        right[0, pol, :, 1, 1, pol, :] = -re_re
        right[1, pol, :, 1, 0, pol, :] = im_im
        right[1, pol, :, 1, 1, pol, :] = -im_re
    right_high, right_low = np_split(right.reshape(128, 256))
    right_all = np.concatenate([right_high, right_high, right_low], 0)

    order = np.arange(SIDE).reshape(8, 4).T.reshape(-1)
    angle = 2.0 * np.pi / SIDE * freq[order][:, None] * PIXELS[None, :]
    left = np.concatenate([np.cos(angle), np.sin(angle)], 1)
    left_high, left_low = np_split(left)
    left_all = np.concatenate([left_high, left_high, left_low], 1)
    return pixel_tables, right_all, left_all


def prep_kernel(section_ref, stations_ref, tile_ref, owner_ref, jones_ref, coef_ref, row_ref, slot_ref,
                p_rows, q_rows, turned, first_ref):
    section = section_ref[0]
    sub_count = stations_ref.shape[1]
    half = sub_count // 2
    tiles_dev = owner_ref.shape[0] // (slot_ref.shape[0] // 2)
    p_rows[...] = jnp.zeros_like(p_rows)
    q_rows[...] = jnp.zeros_like(q_rows)

    def fetch(step, carry):
        item = section * half + step
        p_rows[pl.ds(step, 1), :] = jones_ref[pl.ds(stations_ref[0, item], 1), :]
        q_rows[pl.ds(step, 1), :] = jones_ref[pl.ds(stations_ref[1, item], 1), :]
        return carry

    lax.fori_loop(0, half, fetch, 0)
    lane = lax.broadcasted_iota(jnp.int32, (128, 128), 1)
    odd = (lane & 1) == 1
    high_pair = (lane & 2) == 2

    def swap_one(x):
        return jnp.where(odd, pltpu.roll(x, 1, 1), pltpu.roll(x, 127, 1))

    def swap_two(x):
        return jnp.where(high_pair, pltpu.roll(x, 2, 1), pltpu.roll(x, 126, 1))

    gain_p = p_rows[...]
    gain_p_turned = swap_one(gain_p)
    for kind in range(2):
        gain_q = q_rows[...] if kind == 0 else swap_two(q_rows[...])
        straight = gain_p * gain_q
        crossed = gain_p_turned * gain_q
        real = straight + swap_one(straight)
        imag = swap_one(crossed) - crossed
        turned[...] = jnp.where(odd, imag, real).T
        for place in range(8):
            coef_ref[kind * 8 + place] = turned[pl.ds(place, 16, stride=8), :]

    def clear(step, carry):
        slot_ref[2 * step] = -1
        slot_ref[2 * step + 1] = -1
        return carry

    lax.fori_loop(0, slot_ref.shape[0] // 2, clear, 0)

    def place_item(item, carry):
        position = owner_ref[tile_ref[item]]
        target = position // tiles_dev
        slot = position % tiles_dev
        first = slot_ref[2 * target]
        rank = jnp.where((first == -1) | (first == slot), 0, 1)
        slot_ref[2 * target + rank] = slot
        row_ref[item] = 2 * target + rank
        return carry

    lax.fori_loop(0, sub_count, place_item, 0)


def grid_kernel(chunk_size, chunk, section_ref, w_ref, coef_ref, own_ref, peer_ref, uv_ref, pixel_ref, right_ref,
                left_ref, mine_ref, other_ref, bcast):
    section = section_ref[0]
    step = pl.program_id(0)
    base = chunk * chunk_size + step * GROUP
    half = w_ref.shape[0] // 2
    lane = lax.broadcasted_iota(jnp.int32, (16, 128), 1)
    lane8 = lax.broadcasted_iota(jnp.int32, (8, 128), 1)
    upper = (lane & 16) == 16
    sign = jnp.where(upper, -1.0, 1.0)
    re_lane = lane < 64
    sign_p = jnp.where(re_lane, -sign, sign)
    sign_q = jnp.where(re_lane, -1.0, 1.0)
    q_index = (lax.broadcasted_iota(jnp.int32, (16, 128), 0).astype(jnp.float32) + 0.5) / SIDE
    chan = lax.broadcasted_iota(jnp.int32, (16, 128), 0).astype(jnp.float32)
    chan_half = (1.0 + chan / 64.0) / (2.0 * SIDE)
    shift = lax.rem(128 - base, 128)

    coefs = {}
    for kind in range(2):
        for pol in range(2):
            for row in range(2):
                for part in range(2):
                    place = kind * 8 + (pol ^ section) * 4 + (row ^ section) * 2 + part
                    coefs[kind, pol, row, part] = pltpu.roll(coef_ref[place], shift, 1)

    fields = []
    for g in range(GROUP):
        corr = [[None, None], [None, None]]
        for row in range(2):
            for kind in range(2):
                column = (row ^ section) ^ kind
                if row == 0:
                    vis = [own_ref[0, g, column, 0], own_ref[0, g, column, 1]]
                else:
                    vis = [peer_ref[g, column, 0], peer_ref[g, column, 1]]
                for pol in range(2):
                    cr = jnp.broadcast_to(coefs[kind, pol, row, 0][:, g : g + 1], (16, 128))
                    ci = jnp.broadcast_to(coefs[kind, pol, row, 1][:, g : g + 1], (16, 128))
                    real = cr * vis[0] - ci * vis[1]
                    imag = cr * vis[1] + ci * vis[0]
                    if corr[pol][0] is None:
                        corr[pol] = [real, imag]
                    else:
                        corr[pol] = [corr[pol][0] + real, corr[pol][1] + imag]
        u_row = jnp.broadcast_to(uv_ref[g, 0:1, :], (16, 128))
        v_row = jnp.broadcast_to(uv_ref[g, 1:2, :], (16, 128))
        turn_sin, turn_cos = sincos_half((u_row + v_row) * chan_half)
        for pol in range(2):
            real, imag = corr[pol]
            bcast[g, pol] = real * turn_cos + imag * turn_sin
            bcast[g, 2 + pol] = imag * turn_cos - real * turn_sin

        waves = []
        for cell in (u_row, v_row):
            turns = cell * q_index
            sin_0, cos_0 = sincos_half(turns - jnp.round(turns))
            sin_d, cos_d = sincos_step(turns * (1.0 / 64.0))
            cos_1 = cos_0 * cos_d - sin_0 * sin_d
            sin_1 = sin_0 * cos_d + cos_0 * sin_d
            waves.append([cos_0, sin_0, cos_1, sin_1, cos_d + cos_d])
        total = None
        for pair in range(8):
            left_parts, right_parts = [], []
            for c in (2 * pair, 2 * pair + 1):
                cos_u, sin_u = waves[0][0], waves[0][1]
                cos_v, sin_v = waves[1][0], waves[1][1]
                left_parts.append(jnp.concatenate([cos_u.astype(jnp.bfloat16), sin_u.astype(jnp.bfloat16)], 0))
                pieces = []
                for k in range(4):
                    line = spread(bcast, g, k, c)
                    pieces.append((cos_v * line).astype(jnp.bfloat16))
                    pieces.append((sin_v * line).astype(jnp.bfloat16))
                right_parts.append(jnp.concatenate(pieces, 0))
                for wave in waves:
                    cos_0, sin_0, cos_1, sin_1, twice = wave
                    wave[0], wave[1] = cos_1, sin_1
                    if c < 14:
                        wave[2], wave[3] = twice * cos_1 - cos_0, twice * sin_1 - sin_0
            part = lax.dot_general(
                jnp.concatenate(left_parts, 1),
                jnp.concatenate(right_parts, 1),
                (((1,), (1,)), ((), ())),
                preferred_element_type=jnp.float32,
            )
            total = part if total is None else total + part

        x_rows, y_rows = total[:16], total[16:]
        x_cos = jnp.where(upper, pltpu.roll(x_rows, 16, 1), x_rows)
        x_sin = jnp.where(upper, x_rows, pltpu.roll(x_rows, 112, 1))
        y_cos = jnp.where(upper, pltpu.roll(y_rows, 16, 1), y_rows)
        y_sin = jnp.where(upper, y_rows, pltpu.roll(y_rows, 112, 1))
        even = x_cos + sign_p * pltpu.roll(x_sin, 64, 1)
        oddp = sign_q * pltpu.roll(y_cos, 64, 1) - sign * y_sin
        image = jnp.concatenate([even + oddp, even - oddp], 0)

        w_turns = w_ref[section * half + base + g] * pixel_ref[0]
        w_sin, w_cos = sincos_half(w_turns - jnp.round(w_turns))
        fields.append(
            image * (w_cos * pixel_ref[1]) + pltpu.roll(image, 64, 1) * (w_sin * pixel_ref[2])
        )

    high, low = split_hi_lo(jnp.concatenate(fields, 0))
    rows = jnp.dot(
        jnp.concatenate([high, low, high], 1), right_ref[...], preferred_element_type=jnp.float32
    )
    for g in range(GROUP):
        high, low = split_hi_lo(rows[g * 32 : (g + 1) * 32])
        stack = jnp.concatenate(
            [high[:, :128], high[:, 128:], low[:, :128], low[:, 128:], high[:, :128], high[:, 128:]], 0
        )
        uv = jnp.dot(left_ref[...], stack, preferred_element_type=jnp.float32)
        part = [uv[k * 8 : (k + 1) * 8] for k in range(4)]
        below = lane8 < 64
        quarter = (lane8 & 32) == 32
        a0 = jnp.where(below, part[0], pltpu.roll(part[2], 64, 1))
        a2 = jnp.where(below, pltpu.roll(part[0], 64, 1), part[2])
        a1 = jnp.where(below, part[1], pltpu.roll(part[3], 64, 1))
        a3 = jnp.where(below, pltpu.roll(part[1], 64, 1), part[3])
        mine_ref[g, 0:8, :] = jnp.where(quarter, pltpu.roll(a1, 32, 1), a0)
        other_ref[g, 0:8, :] = jnp.where(quarter, a1, pltpu.roll(a0, 96, 1))
        mine_ref[g, 8:16, :] = jnp.where(quarter, pltpu.roll(a3, 32, 1), a2)
        other_ref[g, 8:16, :] = jnp.where(quarter, a3, pltpu.roll(a2, 96, 1))


def pack_kernel(section_ref, row_ref, *refs):
    count = (len(refs) - 1) // 2
    packed = refs[-1]
    section = section_ref[0]
    half = row_ref.shape[0] // 2
    packed[...] = jnp.zeros_like(packed)
    for side in range(2):
        start = (section ^ side) * half
        for part in range(count):
            values = refs[side * count + part]
            size = values.shape[0]
            offset = start + part * size

            def add(item, carry, values=values, offset=offset):
                row = row_ref[offset + item]
                packed[row] = packed[row] + values[item]
                return carry

            lax.fori_loop(0, size, add, 0)


def unpack_kernel(slot_ref, received_ref, out_ref, acc):
    tiles_dev = out_ref.shape[0]
    acc[...] = jnp.zeros_like(acc)

    def add(item, carry):
        slot = slot_ref[item]
        start = pl.multiple_of(jnp.where(slot < 0, tiles_dev, slot) * 16, 16)
        acc[pl.ds(start, 16), :] = acc[pl.ds(start, 16), :] + received_ref[item]
        return carry

    lax.fori_loop(0, slot_ref.shape[0], add, 0)

    def turn(block, carry):
        top = pl.multiple_of(block * 8, 8)
        for column in range(16):
            out_ref[pl.ds(top, 8), column * 128 : (column + 1) * 128] = acc[
                pl.ds(top * 16 + column, 8, stride=16), :
            ]
        return carry

    lax.fori_loop(0, tiles_dev // 8, turn, 0)


SMEM = pl.BlockSpec(memory_space=pltpu.SMEM)
VMEM = pl.BlockSpec(memory_space=pltpu.VMEM)


def prep(section, stations, tile_ids, owner_map, jones_gains, grid_size):
    return pl.pallas_call(
        prep_kernel,
        out_shape=(
            jax.ShapeDtypeStruct((16, 16, 128), jnp.float32),
            jax.ShapeDtypeStruct(tile_ids.shape, jnp.int32),
            jax.ShapeDtypeStruct((2 * grid_size,), jnp.int32),
        ),
        in_specs=[SMEM, SMEM, SMEM, SMEM, VMEM],
        out_specs=(VMEM, SMEM, SMEM),
        scratch_shapes=[pltpu.VMEM((128, 128), jnp.float32)] * 3 + [pltpu.SMEM((8,), jnp.int32)],
        cost_estimate=pl.CostEstimate(flops=10_000_000, bytes_accessed=500_000, transcendentals=0),
        name="prep",
    )(section, stations, tile_ids, owner_map, jones_gains)


def grid_chunk(chunk, chunk_size, half, section, w_terms, coefs, visibilities, peer, uv_coords, constants):
    per_half = half // GROUP
    offset = chunk * chunk_size // GROUP

    def fixed(shape):
        return pl.BlockSpec(shape, lambda i, s, w: (0,) * len(shape))

    out = jax.ShapeDtypeStruct((chunk_size, 16, 128), jnp.float32)
    return pl.pallas_call(
        lambda *refs: grid_kernel(chunk_size, chunk, *refs),
        out_shape=(out, out),
        grid_spec=pltpu.PrefetchScalarGridSpec(
            num_scalar_prefetch=2,
            grid=(chunk_size // GROUP,),
            in_specs=[
                fixed((16, 16, 128)),
                pl.BlockSpec(
                    (1, GROUP, 2, 2, 16, 128), lambda i, s, w: (0, s[0] * per_half + offset + i, 0, 0, 0, 0)
                ),
                pl.BlockSpec((GROUP, 2, 2, 16, 128), lambda i, s, w: (i, 0, 0, 0, 0)),
                pl.BlockSpec((GROUP, 2, 128), lambda i, s, w: (s[0] * per_half + offset + i, 0, 0)),
                fixed((3, 32, 128)),
                fixed((384, 256)),
                fixed((32, 192)),
            ],
            out_specs=[pl.BlockSpec((GROUP, 16, 128), lambda i, s, w: (i, 0, 0))] * 2,
            scratch_shapes=[pltpu.VMEM((GROUP, 4, 16, 128), jnp.float32)],
        ),
        cost_estimate=pl.CostEstimate(
            flops=chunk_size * 300_000_000, bytes_accessed=chunk_size * 100_000, transcendentals=0
        ),
        name="grid_chunk",
    )(section, w_terms, coefs, visibilities, peer, uv_coords, *constants)


def shards(visibilities, uv_coords, w_terms, stations, tile_ids, owner_map, jones_gains):
    sub_count = visibilities.shape[1]
    samples = visibilities.shape[4] * visibilities.shape[5]
    half = sub_count // 2
    chunk_size = half // CHUNKS
    grid_size = lax.axis_size("grid")
    tiles_dev = owner_map.shape[0] // grid_size
    section_index = lax.axis_index("section").astype(jnp.int32)
    section = section_index.reshape(1)
    swap = [(0, 1), (1, 0)]

    peers = []
    for chunk in range(CHUNKS):
        start = (1 - section_index) * half + chunk * chunk_size
        rows = lax.dynamic_slice_in_dim(visibilities[0], start, chunk_size, 0)
        peers.append(lax.ppermute(rows, "section", swap))

    coefs, row_index, slots = prep(section, stations, tile_ids, owner_map, jones_gains, grid_size)
    every_slot = lax.all_to_all(
        slots.reshape(grid_size, 2), "grid", split_axis=0, concat_axis=0, tiled=True
    ).reshape(-1)

    constants = [jnp.asarray(table) for table in tables(samples)]
    mine, theirs = [], []
    for chunk in range(CHUNKS):
        kept, other = grid_chunk(
            chunk, chunk_size, half, section, w_terms, coefs, visibilities, peers[chunk], uv_coords, constants
        )
        mine.append(kept)
        theirs.append(lax.ppermute(other, "section", swap))

    packed = pl.pallas_call(
        pack_kernel,
        out_shape=jax.ShapeDtypeStruct((2 * grid_size, 16, 128), jnp.float32),
        in_specs=[SMEM, SMEM] + [VMEM] * (2 * CHUNKS),
        out_specs=VMEM,
        name="pack",
    )(section, row_index, *mine, *theirs)
    received = lax.all_to_all(
        packed.reshape(grid_size, 2, 16, 128), "grid", split_axis=0, concat_axis=0, tiled=True
    ).reshape(2 * grid_size, 16, 128)
    tiles = pl.pallas_call(
        unpack_kernel,
        out_shape=jax.ShapeDtypeStruct((tiles_dev, 2048), jnp.float32),
        in_specs=[SMEM, VMEM],
        out_specs=VMEM,
        scratch_shapes=[pltpu.VMEM(((tiles_dev + 1) * 16, 128), jnp.float32)],
        name="unpack",
    )(every_slot, received)
    return tiles[None]


def solution(mesh):
    in_specs = (
        P("section", "grid", None, None, None, None),
        P("grid", None, None),
        P("grid"),
        P(None, "grid"),
        P("grid"),
        P(),
        P(),
    )
    out_specs = P("section", "grid", None)
    return jax.shard_map(shards, mesh=mesh, in_specs=in_specs, out_specs=out_specs, check_vma=False)
```

```python
import math

import numpy as np
import jax
import jax.numpy as jnp
from jax import lax
from jax.experimental import pallas as pl
from jax.experimental.pallas import tpu as pltpu
from jax.sharding import PartitionSpec as P

SIDE = 32
CHUNKS = (48,)
GROUP = 4

PIXELS = np.concatenate([np.arange(16), -1 - np.arange(16)]).astype(np.float64)


def fit_even(function, reach, terms):
    nodes = np.cos(np.pi * (np.arange(64) + 0.5) / 64)
    square = (nodes + 1.0) / 2.0 * reach * reach
    cheb = np.polynomial.chebyshev.chebfit(nodes, function(np.sqrt(square)), terms - 1)
    poly = np.polynomial.chebyshev.cheb2poly(cheb)
    shift = np.polynomial.polynomial.Polynomial(poly)(
        np.polynomial.polynomial.Polynomial([-1.0, 2.0 / (reach * reach)])
    )
    return [float(np.float32(value)) for value in shift.coef]


def sinc_turns(scale):
    return lambda x: np.where(x > 0, np.sin(scale * x) / np.maximum(x, 1e-30), scale)


HALF_SIN = fit_even(sinc_turns(np.pi), 0.5, 5)
HALF_COS = fit_even(lambda x: np.cos(np.pi * x), 0.5, 6)
STEP_SIN = fit_even(sinc_turns(2 * np.pi), 0.0625, 3)
STEP_COS = fit_even(lambda x: np.cos(2 * np.pi * x), 0.0625, 4)


def horner(coefs, square):
    total = square * coefs[-1] + coefs[-2]
    for value in coefs[-3::-1]:
        total = total * square + value
    return total


def sincos_half(x):
    square = x * x
    half_sin = x * horner(HALF_SIN, square)
    half_cos = horner(HALF_COS, square)
    twice = half_sin + half_sin
    return twice * half_cos, 1.0 - twice * half_sin


def sincos_turns(x):
    return sincos_half(x - jnp.round(x))


def sincos_step(x):
    square = x * x
    return x * horner(STEP_SIN, square), horner(STEP_COS, square)


def spread(ref, row):
    return ref[pl.ds(row, 8, stride=0), :]


def split_hi_lo(values):
    high = values.astype(jnp.bfloat16)
    low = (values - high.astype(jnp.float32)).astype(jnp.bfloat16)
    return high, low


def np_split(values):
    high = np.asarray(values, np.float32).astype(jnp.bfloat16)
    low = (np.asarray(values, np.float32) - high.astype(np.float32)).astype(jnp.bfloat16)
    return high, low


def tables(samples):
    row_p = PIXELS[:, None]
    lane_p = np.tile(PIXELS, GROUP)[None, :]
    sine_row, sine_lane = 0.6 * row_p / SIDE, 0.6 * lane_p / SIDE
    n_term = np.sqrt(1.0 - sine_row**2 - sine_lane**2) - 1.0
    taper = np.cos(np.pi * row_p / (SIDE + 4.0)) * np.cos(np.pi * lane_p / (SIDE + 4.0))
    pixel_tables = np.stack([n_term, taper / math.sqrt(samples) / SIDE]).astype(np.float32)

    freq = np.arange(SIDE) - SIDE // 2
    angle = 2.0 * np.pi / SIDE * PIXELS[:, None] * freq[None, :]
    cos_t = np.kron(np.eye(GROUP), np.cos(angle))
    sin_t = np.kron(np.eye(GROUP), np.sin(angle))
    high, low = np_split(np.block([[cos_t, -sin_t], [sin_t, cos_t]]))
    right_all = np.concatenate([high, high, low], 0)

    order = np.arange(SIDE).reshape(8, 4).T.reshape(-1)
    angle = 2.0 * np.pi / SIDE * freq[order][:, None] * PIXELS[None, :]
    high, low = np_split(np.block([[np.cos(angle), np.sin(angle)], [-np.sin(angle), np.cos(angle)]]))
    left_all = np.concatenate([high, high, low], 1)
    return pixel_tables, right_all, left_all


def swap_groups(parts, low_half, odd_quarter):
    a0 = jnp.where(low_half, parts[0], pltpu.roll(parts[2], 64, 1))
    a2 = jnp.where(low_half, pltpu.roll(parts[0], 64, 1), parts[2])
    a1 = jnp.where(low_half, parts[1], pltpu.roll(parts[3], 64, 1))
    a3 = jnp.where(low_half, pltpu.roll(parts[1], 64, 1), parts[3])
    return [
        jnp.where(odd_quarter, pltpu.roll(a1, 32, 1), a0),
        jnp.where(odd_quarter, a1, pltpu.roll(a0, 96, 1)),
        jnp.where(odd_quarter, pltpu.roll(a3, 32, 1), a2),
        jnp.where(odd_quarter, a3, pltpu.roll(a2, 96, 1)),
    ]


def gains_kernel(section_ref, stations_ref, jones_ref, coef_ref, p_rows, q_rows, turned):
    section = section_ref[0]
    half = stations_ref.shape[1] // 2
    p_rows[...] = jnp.zeros_like(p_rows)
    q_rows[...] = jnp.zeros_like(q_rows)

    def fetch(step, carry):
        for k in range(8):
            item = section * half + step * 8 + k
            p_rows[pl.ds(step * 8 + k, 1), :] = jones_ref[pl.ds(stations_ref[0, item], 1), :]
            q_rows[pl.ds(step * 8 + k, 1), :] = jones_ref[pl.ds(stations_ref[1, item], 1), :]
        return carry

    lax.fori_loop(0, half // 8, fetch, 0)
    lane = lax.broadcasted_iota(jnp.int32, (128, 128), 1)
    odd = (lane & 1) == 1
    high_pair = (lane & 2) == 2

    def swap_one(x):
        return jnp.where(odd, pltpu.roll(x, 1, 1), pltpu.roll(x, 127, 1))

    def swap_two(x):
        return jnp.where(high_pair, pltpu.roll(x, 2, 1), pltpu.roll(x, 126, 1))

    gain_p = p_rows[...]
    gain_p_turned = swap_one(gain_p)
    for kind in range(2):
        gain_q = q_rows[...] if kind == 0 else swap_two(q_rows[...])
        straight = gain_p * gain_q
        crossed = gain_p_turned * gain_q
        real = straight + swap_one(straight)
        imag = swap_one(crossed) - crossed
        turned[...] = jnp.where(odd, imag, real).T
        for place in range(8):
            coef_ref[kind * 8 + place] = turned[pl.ds(place, 16, stride=8), :]


def index_kernel(tile_ref, owner_ref, row_ref, slot_ref):
    sub_count = tile_ref.shape[0]
    tiles_dev = owner_ref.shape[0] // (slot_ref.shape[0] // 2)
    shift = tiles_dev.bit_length() - 1
    assert tiles_dev == 1 << shift

    def clear(step, carry):
        for k in range(4):
            slot_ref[step * 4 + k] = -1
        return carry

    lax.fori_loop(0, slot_ref.shape[0] // 4, clear, 0)

    def place_item(step, carry):
        for k in range(8):
            item = step * 8 + k
            position = owner_ref[tile_ref[item]]
            target = 2 * (position >> shift)
            slot = position & (tiles_dev - 1)
            first = slot_ref[target]
            row = target + jnp.where((first == -1) | (first == slot), 0, 1)
            slot_ref[row] = slot
            row_ref[item] = row
        return carry

    lax.fori_loop(0, sub_count // 8, place_item, 0)


def grid_kernel(chunk_start, section_ref, w_ref, coef_ref, own_ref, peer_ref, uv_ref, pixel_ref, right_ref, left_ref,
                mine_ref, other_ref, bcast, rolled, wave_rows, totals):
    section = section_ref[0]
    groups = mine_ref.shape[0] // GROUP
    half = w_ref.shape[0] // 2
    lane = lax.broadcasted_iota(jnp.int32, (8, 128), 1)
    sub_lane = lax.broadcasted_iota(jnp.int32, (8, 128), 0).astype(jnp.float32)

    def gridding(group):
        first = group * GROUP
        shift = lax.rem(128 - (chunk_start + first), 128)
        for place in range(16):
            rolled[place] = pltpu.roll(coef_ref[place], shift, 1)
        cells = uv_ref[pl.ds(pl.multiple_of(section * (2 * half) + 2 * (chunk_start + first), 8), 8), :]
        wave_rows[0:8], wave_rows[8:16] = sincos_turns(cells * (8.0 / SIDE))
        wave_rows[16:24], wave_rows[24:32] = sincos_step(cells * (8.0 / (64.0 * SIDE)))
        sums = cells + pltpu.roll(cells, 7, 0)
        wave_rows[32:40], wave_rows[40:48] = sincos_step(sums * (8.0 / (128.0 * SIDE)))
        wave_rows[48:56] = cells
        for g in range(GROUP):
            corr = [None, None]
            for row in range(2):
                for kind in range(2):
                    column = (row ^ section) ^ kind
                    source = own_ref if row == 0 else peer_ref
                    vis_real = source[first + g, column, 0]
                    vis_imag = source[first + g, column, 1]
                    for pol in range(2):
                        place = kind * 8 + (pol ^ section) * 4 + (row ^ section) * 2
                        cr = jnp.broadcast_to(rolled[place][:, g : g + 1], (16, 128))
                        ci = jnp.broadcast_to(rolled[place + 1][:, g : g + 1], (16, 128))
                        real = cr * vis_real - ci * vis_imag
                        imag = cr * vis_imag + ci * vis_real
                        if corr[pol] is None:
                            corr[pol] = [real, imag]
                        else:
                            corr[pol] = [corr[pol][0] + real, corr[pol][1] + imag]
            u_row = spread(wave_rows, 48 + 2 * g)
            v_row = spread(wave_rows, 49 + 2 * g)
            turn_sin, turn_cos = sincos_half((u_row + v_row) * ((1.0 + sub_lane / 64.0) / (2.0 * SIDE)))
            step_sin, step_cos = spread(wave_rows, 32 + 2 * g), spread(wave_rows, 40 + 2 * g)
            turn_sin, turn_cos = (
                jnp.concatenate([turn_sin, turn_sin * step_cos + turn_cos * step_sin], 0),
                jnp.concatenate([turn_cos, turn_cos * step_cos - turn_sin * step_sin], 0),
            )
            for pol in range(2):
                real, imag = corr[pol]
                bcast[g, pol * 16 : pol * 16 + 16] = real * turn_cos + imag * turn_sin
                bcast[g, 32 + pol * 16 : 48 + pol * 16] = imag * turn_cos - real * turn_sin

            waves = []
            for axis, cell in enumerate((u_row, v_row)):
                turns = cell * ((sub_lane + 0.5) / SIDE)
                sin_0, cos_0 = sincos_turns(turns)
                sin_d, cos_d = sincos_step(turns * (1.0 / 64.0))
                place = 2 * g + axis
                up_sin, up_cos = spread(wave_rows, place), spread(wave_rows, 8 + place)
                upd_sin, upd_cos = spread(wave_rows, 16 + place), spread(wave_rows, 24 + place)
                cos_0, sin_0, cos_d, sin_d = (
                    jnp.stack([cos_0, cos_0 * up_cos - sin_0 * up_sin]),
                    jnp.stack([sin_0, sin_0 * up_cos + cos_0 * up_sin]),
                    jnp.stack([cos_d, cos_d * upd_cos - sin_d * upd_sin]),
                    jnp.stack([sin_d, sin_d * upd_cos + cos_d * upd_sin]),
                )
                cos_1 = cos_0 * cos_d - sin_0 * sin_d
                sin_1 = sin_0 * cos_d + cos_0 * sin_d
                waves.append([cos_0, sin_0, cos_1, sin_1, cos_d + cos_d])
            total = None
            for pair in range(8):
                left_parts, right_parts = [], []
                for c in (2 * pair, 2 * pair + 1):
                    cos_u, sin_u = waves[0][0], waves[0][1]
                    cos_v, sin_v = waves[1][0], waves[1][1]
                    left_parts.append(jnp.concatenate([cos_u, sin_u], 0).reshape(32, 128))
                    pieces = []
                    for k in range(4):
                        line = spread(bcast.at[g], 16 * k + c)[None]
                        pieces.append((cos_v * line).reshape(16, 128))
                        pieces.append((sin_v * line).reshape(16, 128))
                    right_parts.append(jnp.concatenate(pieces, 0))
                    for wave in waves:
                        cos_0, sin_0, cos_1, sin_1, twice = wave
                        wave[0], wave[1] = cos_1, sin_1
                        if c < 14:
                            wave[2], wave[3] = twice * cos_1 - cos_0, twice * sin_1 - sin_0
                part = lax.dot_general(
                    jnp.concatenate(left_parts, 1).astype(jnp.bfloat16),
                    jnp.concatenate(right_parts, 1).astype(jnp.bfloat16),
                    (((1,), (1,)), ((), ())),
                    preferred_element_type=jnp.float32,
                )
                total = part if total is None else total + part
            totals[group & 1, g] = total

    def imaging(group):
        first = group * GROUP
        lane32 = lax.broadcasted_iota(jnp.int32, (32, 128), 1)
        lane16 = lax.broadcasted_iota(jnp.int32, (16, 128), 1)
        sums = swap_groups(
            [totals[group & 1, g] for g in range(GROUP)], lane32 < 64, (lane32 & 32) == 32
        )
        upper = (lane16 & 16) == 16
        sign = jnp.where(upper, -1.0, 1.0)
        w_first = section * half + chunk_start + first
        w_row = jnp.where(
            lane < 64,
            jnp.where(lane < 32, w_ref[w_first], w_ref[w_first + 1]),
            jnp.where(lane < 96, w_ref[w_first + 2], w_ref[w_first + 3]),
        )
        w_turns = pixel_ref[0].reshape(4, 8, 128) * w_row[None]
        w_sin, w_cos = sincos_turns(w_turns.reshape(32, 128))
        w_sin, w_cos = w_sin * pixel_ref[1], w_cos * pixel_ref[1]
        fields = []
        for pol in range(2):
            cos_part, sin_part = [], []
            for value in (sums[pol][:16], sums[2 + pol][:16], sums[pol][16:], sums[2 + pol][16:]):
                cos_part.append(jnp.where(upper, pltpu.roll(value, 16, 1), value))
                sin_part.append(sign * jnp.where(upper, value, pltpu.roll(value, 112, 1)))
            even_re = cos_part[0] - sin_part[1]
            even_im = cos_part[1] + sin_part[0]
            odd_re = cos_part[3] + sin_part[2]
            odd_im = cos_part[2] - sin_part[3]
            image_re = jnp.concatenate([even_re - odd_re, even_re + odd_re], 0)
            image_im = jnp.concatenate([even_im + odd_im, even_im - odd_im], 0)
            fields.append(
                jnp.concatenate(
                    [image_re * w_cos - image_im * w_sin, image_re * w_sin + image_im * w_cos], 1
                )
            )
        high, low = split_hi_lo(jnp.concatenate(fields, 0))
        rows = jnp.dot(
            jnp.concatenate([high, low, high], 1), right_ref[...], preferred_element_type=jnp.float32
        )
        high, low = split_hi_lo(rows)
        for pol, out_ref in enumerate((mine_ref, other_ref)):
            top = slice(pol * 32, pol * 32 + 32)
            stack = jnp.concatenate(
                [high[top, :128], high[top, 128:], low[top, :128], low[top, 128:], high[top, :128], high[top, 128:]],
                0,
            )
            uv = jnp.dot(left_ref[...], stack, preferred_element_type=jnp.float32)
            for part in range(2):
                parts = swap_groups(
                    [uv[part * 32 + k * 8 : part * 32 + k * 8 + 8] for k in range(4)], lane < 64, (lane & 32) == 32
                )
                for g in range(GROUP):
                    out_ref[first + g, part * 8 : part * 8 + 8, :] = parts[g]

    gridding(0)

    def both(group, carry):
        imaging(group - 1)
        gridding(group)
        return carry

    lax.fori_loop(1, groups, both, 0)
    imaging(groups - 1)


def pack_kernel(section_ref, row_ref, slot_ref, *refs):
    packed = refs[-1]
    section = section_ref[0]
    half = row_ref.shape[0] // 2
    width = packed.shape[0] // (slot_ref.shape[0] // 2)
    packed[...] = jnp.zeros_like(packed)
    lane = lax.broadcasted_iota(jnp.int32, (1, 128), 1)

    def note(step, carry):
        for k in range(2):
            target = step * 2 + k
            slots = jnp.where(lane == 0, slot_ref[2 * target], slot_ref[2 * target + 1])
            packed[pl.ds(target * width + width - 1, 1), :] = slots.astype(jnp.float32)
        return carry

    lax.fori_loop(0, slot_ref.shape[0] // 4, note, 0)
    add_rows(row_ref, section * half, width, refs[:-1], packed)


def pack_more_kernel(section_ref, row_ref, *refs):
    packed = refs[-1]
    half = row_ref.shape[0] // 2
    packed[...] = refs[0][...]
    add_rows(row_ref, (1 - section_ref[0]) * half, 33, refs[1:-1], packed)


def add_rows(row_ref, start, width, sources, packed):
    for values in sources:

        def add(step, carry, values=values, start=start):
            for k in range(4):
                item = step * 4 + k
                row = row_ref[start + item]
                top = (row >> 1) * width + (row & 1) * 16
                packed[pl.ds(top, 16), :] = packed[pl.ds(top, 16), :] + values[item]
            return carry

        lax.fori_loop(0, values.shape[0] // 4, add, 0)
        start = start + values.shape[0]


def unpack_kernel(received_ref, out_ref):
    tiles_dev = out_ref.shape[0]
    sources = received_ref.shape[0] // 33
    slots = received_ref[pl.ds(32, sources, stride=33), :].T
    row = jnp.concatenate([slots[0:1, :], slots[1:2, :]], 1)
    tile = lax.broadcasted_iota(jnp.int32, (tiles_dev, 2 * sources), 0).astype(jnp.float32)
    picked = jnp.where(tile == row, 1.0, 0.0).astype(jnp.bfloat16)
    picked = jnp.concatenate([picked, picked], 1)
    for pair in range(8):
        columns = []
        for column in (2 * pair, 2 * pair + 1):
            values = jnp.concatenate(
                [received_ref[pl.ds(16 * rank + column, sources, stride=33), :] for rank in range(2)], 0
            )
            columns.append(jnp.concatenate(split_hi_lo(values), 0))
        out_ref[:, pair * 256 : (pair + 1) * 256] = jnp.dot(
            picked, jnp.concatenate(columns, 1), preferred_element_type=jnp.float32
        )


SMEM = pl.BlockSpec(memory_space=pltpu.SMEM)
VMEM = pl.BlockSpec(memory_space=pltpu.VMEM)


def call(kernel, name, out_shape, in_specs, out_specs, scratch=(), flops=1_000_000, moved=1_000_000, mib=8):
    return pl.pallas_call(
        kernel,
        out_shape=out_shape,
        in_specs=in_specs,
        out_specs=out_specs,
        scratch_shapes=list(scratch),
        compiler_params=pltpu.CompilerParams(vmem_limit_bytes=mib * 1024 * 1024),
        cost_estimate=pl.CostEstimate(flops=flops, bytes_accessed=moved, transcendentals=0),
        name=name,
    )


def shards(visibilities, uv_coords, w_terms, stations, tile_ids, owner_map, jones_gains):
    sub_count = visibilities.shape[1]
    samples = visibilities.shape[4] * visibilities.shape[5]
    half = sub_count // 2
    grid_size = lax.axis_size("grid")
    tiles_dev = owner_map.shape[0] // grid_size
    section_index = lax.axis_index("section").astype(jnp.int32)
    section = section_index.reshape(1)
    swap = [(0, 1), (1, 0)]
    shape_f32 = lambda *shape: jax.ShapeDtypeStruct(shape, jnp.float32)
    shape_i32 = lambda *shape: jax.ShapeDtypeStruct(shape, jnp.int32)

    own, peers, start = [], [], 0
    for size in CHUNKS:
        rows = lax.dynamic_slice_in_dim(visibilities[0], (1 - section_index) * half + start, size, 0)
        peers.append(lax.ppermute(rows, "section", swap))
        start += size
    start = 0
    for size in CHUNKS:
        own.append(lax.dynamic_slice_in_dim(visibilities[0], section_index * half + start, size, 0))
        start += size

    coefs = call(
        gains_kernel, "gains", shape_f32(16, 16, 128), [SMEM, SMEM, VMEM], VMEM,
        [pltpu.VMEM((128, 128), jnp.float32)] * 3,
    )(section, stations, jones_gains)
    row_index, slots = call(
        index_kernel, "index", (shape_i32(sub_count), shape_i32(2 * grid_size)), [SMEM, SMEM], (SMEM, SMEM)
    )(tile_ids, owner_map)

    constants = [jnp.asarray(table) for table in tables(samples)]
    uv_rows = uv_coords.reshape(2 * sub_count, uv_coords.shape[2])
    mine, theirs, start = [], [], 0
    for chunk, size in enumerate(CHUNKS):
        kept, other = call(
            lambda *refs, start=start: grid_kernel(start, *refs),
            "grid_chunk",
            (shape_f32(size, 16, 128),) * 2,
            [SMEM, SMEM] + [VMEM] * 7,
            (VMEM, VMEM),
            [
                pltpu.VMEM((GROUP, 64, 128), jnp.float32),
                pltpu.VMEM((16, 16, 128), jnp.float32),
                pltpu.VMEM((56, 128), jnp.float32),
                pltpu.VMEM((2, GROUP, 32, 128), jnp.float32),
            ],
            flops=size * 300_000_000,
            moved=size * 100_000,
            mib=12,
        )(section, w_terms, coefs, own[chunk], peers[chunk], uv_rows, *constants)
        mine.append(kept)
        theirs.append(lax.ppermute(other, "section", swap))
        start += size

    packed_shape = shape_f32(33 * grid_size, 128)
    packed = call(
        pack_kernel, "pack", packed_shape, [SMEM] * 3 + [VMEM] * len(CHUNKS), VMEM, flops=100_000_000
    )(section, row_index, slots, *mine)
    packed = call(
        pack_more_kernel, "pack_more", packed_shape, [SMEM] * 2 + [VMEM] * (1 + len(CHUNKS)), VMEM
    )(section, row_index, packed, *theirs)
    received = lax.all_to_all(
        packed.reshape(grid_size, 1, 33 * 128), "grid", split_axis=0, concat_axis=0, tiled=True
    ).reshape(33 * grid_size, 128)
    tiles = call(unpack_kernel, "unpack", shape_f32(tiles_dev, 2048), [VMEM], VMEM)(received)
    return tiles[None]


def solution(mesh):
    in_specs = (
        P("section", "grid", None, None, None, None),
        P("grid", None, None),
        P("grid"),
        P(None, "grid"),
        P("grid"),
        P(),
        P(),
    )
    out_specs = P("section", "grid", None)
    return jax.shard_map(shards, mesh=mesh, in_specs=in_specs, out_specs=out_specs, check_vma=False)
```

```python
import math

import numpy as np
import jax
import jax.numpy as jnp
from jax import lax
from jax.experimental import pallas as pl
from jax.experimental.pallas import tpu as pltpu
from jax.sharding import PartitionSpec as P

SIDE = 32
CHUNKS = (48,)
GROUP = 4

PIXELS = np.concatenate([np.arange(16), -1 - np.arange(16)]).astype(np.float64)


def fit_even(function, reach, terms):
    nodes = np.cos(np.pi * (np.arange(64) + 0.5) / 64)
    square = (nodes + 1.0) / 2.0 * reach * reach
    cheb = np.polynomial.chebyshev.chebfit(nodes, function(np.sqrt(square)), terms - 1)
    poly = np.polynomial.chebyshev.cheb2poly(cheb)
    shift = np.polynomial.polynomial.Polynomial(poly)(
        np.polynomial.polynomial.Polynomial([-1.0, 2.0 / (reach * reach)])
    )
    return [float(np.float32(value)) for value in shift.coef]


def sinc_turns(scale):
    return lambda x: np.where(x > 0, np.sin(scale * x) / np.maximum(x, 1e-30), scale)


HALF_SIN = fit_even(sinc_turns(np.pi), 0.5, 5)
HALF_COS = fit_even(lambda x: np.cos(np.pi * x), 0.5, 6)
STEP_SIN = fit_even(sinc_turns(2 * np.pi), 0.0625, 3)
STEP_COS = fit_even(lambda x: np.cos(2 * np.pi * x), 0.0625, 4)


def horner(coefs, square):
    total = square * coefs[-1] + coefs[-2]
    for value in coefs[-3::-1]:
        total = total * square + value
    return total


def sincos_half(x):
    square = x * x
    half_sin = x * horner(HALF_SIN, square)
    half_cos = horner(HALF_COS, square)
    twice = half_sin + half_sin
    return twice * half_cos, 1.0 - twice * half_sin


def sincos_turns(x):
    return sincos_half(x - jnp.round(x))


def sincos_step(x):
    square = x * x
    return x * horner(STEP_SIN, square), horner(STEP_COS, square)


def spread(ref, row):
    return ref[pl.ds(row, 8, stride=0), :]


def split_hi_lo(values):
    high = values.astype(jnp.bfloat16)
    low = (values - high.astype(jnp.float32)).astype(jnp.bfloat16)
    return high, low


def np_split(values):
    high = np.asarray(values, np.float32).astype(jnp.bfloat16)
    low = (np.asarray(values, np.float32) - high.astype(np.float32)).astype(jnp.bfloat16)
    return high, low


def tables(samples):
    row_p = PIXELS[:, None]
    lane_p = np.tile(PIXELS, GROUP)[None, :]
    sine_row, sine_lane = 0.6 * row_p / SIDE, 0.6 * lane_p / SIDE
    n_term = np.sqrt(1.0 - sine_row**2 - sine_lane**2) - 1.0
    taper = np.cos(np.pi * row_p / (SIDE + 4.0)) * np.cos(np.pi * lane_p / (SIDE + 4.0))
    pixel_tables = np.stack([n_term, taper / math.sqrt(samples) / SIDE]).astype(np.float32)

    freq = np.arange(SIDE) - SIDE // 2
    angle = 2.0 * np.pi / SIDE * PIXELS[:, None] * freq[None, :]
    cos_t = np.kron(np.eye(GROUP), np.cos(angle))
    sin_t = np.kron(np.eye(GROUP), np.sin(angle))
    high, low = np_split(np.block([[cos_t, -sin_t], [sin_t, cos_t]]))
    right_all = np.concatenate([high, high, low], 0)

    order = np.arange(SIDE).reshape(8, 4).T.reshape(-1)
    angle = 2.0 * np.pi / SIDE * freq[order][:, None] * PIXELS[None, :]
    high, low = np_split(np.block([[np.cos(angle), np.sin(angle)], [-np.sin(angle), np.cos(angle)]]))
    left_all = np.concatenate([high, high, low], 1)
    return pixel_tables, right_all, left_all


def swap_groups(parts, low_half, odd_quarter):
    a0 = jnp.where(low_half, parts[0], pltpu.roll(parts[2], 64, 1))
    a2 = jnp.where(low_half, pltpu.roll(parts[0], 64, 1), parts[2])
    a1 = jnp.where(low_half, parts[1], pltpu.roll(parts[3], 64, 1))
    a3 = jnp.where(low_half, pltpu.roll(parts[1], 64, 1), parts[3])
    return [
        jnp.where(odd_quarter, pltpu.roll(a1, 32, 1), a0),
        jnp.where(odd_quarter, a1, pltpu.roll(a0, 96, 1)),
        jnp.where(odd_quarter, pltpu.roll(a3, 32, 1), a2),
        jnp.where(odd_quarter, a3, pltpu.roll(a2, 96, 1)),
    ]


def prep_kernel(section_ref, stations_ref, tile_ref, owner_any, jones_ref, vis_any, coef_ref, own_ref, row_ref, slot_ref,
                p_rows, q_rows, turned, owner_ref, sems):
    section = section_ref[0]
    sub_count = tile_ref.shape[0]
    half = sub_count // 2
    owner_copy = pltpu.make_async_copy(owner_any, owner_ref, sems.at[0])
    owner_copy.start()
    own_copy = pltpu.make_async_copy(vis_any.at[0, pl.ds(section * half, half)], own_ref, sems.at[1])
    own_copy.start()

    p_rows[...] = jnp.zeros_like(p_rows)
    q_rows[...] = jnp.zeros_like(q_rows)

    def fetch(step, carry):
        for k in range(8):
            item = section * half + step * 8 + k
            p_rows[pl.ds(step * 8 + k, 1), :] = jones_ref[pl.ds(stations_ref[0, item], 1), :]
            q_rows[pl.ds(step * 8 + k, 1), :] = jones_ref[pl.ds(stations_ref[1, item], 1), :]
        return carry

    lax.fori_loop(0, half // 8, fetch, 0)
    lane = lax.broadcasted_iota(jnp.int32, (128, 128), 1)
    odd = (lane & 1) == 1
    high_pair = (lane & 2) == 2

    def swap_one(x):
        return jnp.where(odd, pltpu.roll(x, 1, 1), pltpu.roll(x, 127, 1))

    def swap_two(x):
        return jnp.where(high_pair, pltpu.roll(x, 2, 1), pltpu.roll(x, 126, 1))

    gain_p = p_rows[...]
    gain_p_turned = swap_one(gain_p)
    for kind in range(2):
        gain_q = q_rows[...] if kind == 0 else swap_two(q_rows[...])
        straight = gain_p * gain_q
        crossed = gain_p_turned * gain_q
        real = straight + swap_one(straight)
        imag = swap_one(crossed) - crossed
        turned[...] = jnp.where(odd, imag, real).T
        for place in range(8):
            coef_ref[kind * 8 + place] = turned[pl.ds(place, 16, stride=8), :]

    tiles_dev = owner_ref.shape[0] // (slot_ref.shape[0] // 2)
    shift = tiles_dev.bit_length() - 1
    assert tiles_dev == 1 << shift

    def clear(step, carry):
        for k in range(4):
            slot_ref[step * 4 + k] = -1
        return carry

    lax.fori_loop(0, slot_ref.shape[0] // 4, clear, 0)
    owner_copy.wait()

    def place_item(step, carry):
        positions = [owner_ref[tile_ref[step * 8 + k]] for k in range(8)]
        for k, position in enumerate(positions):
            target = 2 * (position >> shift)
            slot = position & (tiles_dev - 1)
            first = slot_ref[target]
            row = target + jnp.where((first == -1) | (first == slot), 0, 1)
            slot_ref[row] = slot
            row_ref[step * 8 + k] = row
        return carry

    lax.fori_loop(0, sub_count // 8, place_item, 0)
    own_copy.wait()


def grid_kernel(chunk_start, section_ref, w_ref, coef_ref, own_ref, peer_ref, uv_ref, pixel_ref, right_ref, left_ref,
                mine_ref, other_ref, bcast, rolled, wave_rows, totals, finished):
    section = section_ref[0]
    groups = mine_ref.shape[0] // GROUP
    half = w_ref.shape[0] // 2
    lane = lax.broadcasted_iota(jnp.int32, (8, 128), 1)
    sub_lane = lax.broadcasted_iota(jnp.int32, (8, 128), 0).astype(jnp.float32)

    def gridding(group):
        first = group * GROUP
        shift = lax.rem(128 - (chunk_start + first), 128)
        for place in range(16):
            rolled[place] = pltpu.roll(coef_ref[place], shift, 1)
        cells = uv_ref[pl.ds(pl.multiple_of(section * (2 * half) + 2 * (chunk_start + first), 8), 8), :]
        wave_rows[0:8], wave_rows[8:16] = sincos_turns(cells * (8.0 / SIDE))
        wave_rows[16:24], wave_rows[24:32] = sincos_step(cells * (8.0 / (64.0 * SIDE)))
        sums = cells + pltpu.roll(cells, 7, 0)
        wave_rows[32:40], wave_rows[40:48] = sincos_step(sums * (8.0 / (128.0 * SIDE)))
        wave_rows[48:56] = cells
        for g in range(GROUP):
            corr = [None, None]
            for row in range(2):
                for kind in range(2):
                    column = (row ^ section) ^ kind
                    source = own_ref if row == 0 else peer_ref
                    at = first + g + (chunk_start if row == 0 else 0)
                    vis_real = source[at, column, 0]
                    vis_imag = source[at, column, 1]
                    for pol in range(2):
                        place = kind * 8 + (pol ^ section) * 4 + (row ^ section) * 2
                        cr = jnp.broadcast_to(rolled[place][:, g : g + 1], (16, 128))
                        ci = jnp.broadcast_to(rolled[place + 1][:, g : g + 1], (16, 128))
                        real = cr * vis_real - ci * vis_imag
                        imag = cr * vis_imag + ci * vis_real
                        if corr[pol] is None:
                            corr[pol] = [real, imag]
                        else:
                            corr[pol] = [corr[pol][0] + real, corr[pol][1] + imag]
            u_row = spread(wave_rows, 48 + 2 * g)
            v_row = spread(wave_rows, 49 + 2 * g)
            turn_sin, turn_cos = sincos_half((u_row + v_row) * ((1.0 + sub_lane / 64.0) / (2.0 * SIDE)))
            step_sin, step_cos = spread(wave_rows, 32 + 2 * g), spread(wave_rows, 40 + 2 * g)
            turn_sin, turn_cos = (
                jnp.concatenate([turn_sin, turn_sin * step_cos + turn_cos * step_sin], 0),
                jnp.concatenate([turn_cos, turn_cos * step_cos - turn_sin * step_sin], 0),
            )
            for pol in range(2):
                real, imag = corr[pol]
                bcast[g, pol * 16 : pol * 16 + 16] = real * turn_cos + imag * turn_sin
                bcast[g, 32 + pol * 16 : 48 + pol * 16] = imag * turn_cos - real * turn_sin
            yield

            waves = []
            for axis, cell in enumerate((u_row, v_row)):
                turns = cell * ((sub_lane + 0.5) / SIDE)
                sin_0, cos_0 = sincos_turns(turns)
                sin_d, cos_d = sincos_step(turns * (1.0 / 64.0))
                place = 2 * g + axis
                up_sin, up_cos = spread(wave_rows, place), spread(wave_rows, 8 + place)
                upd_sin, upd_cos = spread(wave_rows, 16 + place), spread(wave_rows, 24 + place)
                cos_0, sin_0, cos_d, sin_d = (
                    jnp.stack([cos_0, cos_0 * up_cos - sin_0 * up_sin]),
                    jnp.stack([sin_0, sin_0 * up_cos + cos_0 * up_sin]),
                    jnp.stack([cos_d, cos_d * upd_cos - sin_d * upd_sin]),
                    jnp.stack([sin_d, sin_d * upd_cos + cos_d * upd_sin]),
                )
                cos_1 = cos_0 * cos_d - sin_0 * sin_d
                sin_1 = sin_0 * cos_d + cos_0 * sin_d
                waves.append([cos_0, sin_0, cos_1, sin_1, cos_d + cos_d])
            yield
            total = None
            for pair in range(8):
                left_parts, right_parts = [], []
                for c in (2 * pair, 2 * pair + 1):
                    cos_u, sin_u = waves[0][0], waves[0][1]
                    cos_v, sin_v = waves[1][0], waves[1][1]
                    left_parts.append(jnp.concatenate([cos_u, sin_u], 0).reshape(32, 128))
                    pieces = []
                    for k in range(4):
                        line = spread(bcast.at[g], 16 * k + c)[None]
                        pieces.append((cos_v * line).reshape(16, 128))
                        pieces.append((sin_v * line).reshape(16, 128))
                    right_parts.append(jnp.concatenate(pieces, 0))
                    for wave in waves:
                        cos_0, sin_0, cos_1, sin_1, twice = wave
                        wave[0], wave[1] = cos_1, sin_1
                        if c < 14:
                            wave[2], wave[3] = twice * cos_1 - cos_0, twice * sin_1 - sin_0
                part = lax.dot_general(
                    jnp.concatenate(left_parts, 1).astype(jnp.bfloat16),
                    jnp.concatenate(right_parts, 1).astype(jnp.bfloat16),
                    (((1,), (1,)), ((), ())),
                    preferred_element_type=jnp.float32,
                )
                total = part if total is None else total + part
                yield
            totals[g] = total

    def imaging(group):
        first = group * GROUP
        lane16 = lax.broadcasted_iota(jnp.int32, (16, 128), 1)
        upper = (lane16 & 16) == 16
        sign = jnp.where(upper, -1.0, 1.0)
        low_half, odd_quarter = lane16 < 64, (lane16 & 32) == 32
        w_first = section * half + chunk_start + first
        w_row = jnp.where(
            lane < 64,
            jnp.where(lane < 32, w_ref[w_first], w_ref[w_first + 1]),
            jnp.where(lane < 96, w_ref[w_first + 2], w_ref[w_first + 3]),
        )
        w_row = jnp.concatenate([w_row, w_row], 0)
        turned = []
        for k in range(2):
            rows = slice(k * 16, k * 16 + 16)
            w_sin, w_cos = sincos_turns(pixel_ref[0, rows] * w_row)
            turned.append((w_sin * pixel_ref[1, rows], w_cos * pixel_ref[1, rows]))
            yield
        parts = []
        for k in range(2):
            sums = swap_groups(
                [finished[g, k * 16 : k * 16 + 16] for g in range(GROUP)], low_half, odd_quarter
            )
            yield
            for value in sums:
                parts.append(
                    (
                        jnp.where(upper, pltpu.roll(value, 16, 1), value),
                        sign * jnp.where(upper, value, pltpu.roll(value, 112, 1)),
                    )
                )
                yield
        fields = []
        for pol in range(2):
            xa, xb, ya, yb = parts[pol], parts[2 + pol], parts[4 + pol], parts[6 + pol]
            even_re, even_im = xa[0] - xb[1], xb[0] + xa[1]
            odd_re, odd_im = yb[0] + ya[1], ya[0] - yb[1]
            for k in range(2):
                w_sin, w_cos = turned[k]
                image_re = even_re - odd_re if k == 0 else even_re + odd_re
                image_im = even_im + odd_im if k == 0 else even_im - odd_im
                fields.append(
                    jnp.concatenate(
                        [image_re * w_cos - image_im * w_sin, image_re * w_sin + image_im * w_cos], 1
                    )
                )
                yield
        pieces = []
        for field in fields:
            high, low = split_hi_lo(field)
            pieces.append(jnp.concatenate([high, low, high], 1))
            yield
        rows = jnp.dot(jnp.concatenate(pieces, 0), right_ref[...], preferred_element_type=jnp.float32)
        yield
        for pol, out_ref in enumerate((mine_ref, other_ref)):
            high, low = split_hi_lo(rows[pol * 32 : pol * 32 + 32])
            stack = jnp.concatenate(
                [high[:, :128], high[:, 128:], low[:, :128], low[:, 128:], high[:, :128], high[:, 128:]], 0
            )
            yield
            uv = jnp.dot(left_ref[...], stack, preferred_element_type=jnp.float32)
            yield
            for part in range(2):
                outs = swap_groups(
                    [uv[part * 32 + k * 8 : part * 32 + k * 8 + 8] for k in range(4)], lane < 64, (lane & 32) == 32
                )
                for g in range(GROUP):
                    out_ref[first + g, part * 8 : part * 8 + 8, :] = outs[g]
                yield

    def run(work):
        for _ in work:
            pass

    run(gridding(0))

    def both(group, carry):
        finished[...] = totals[...]
        run(imaging(group - 1))
        run(gridding(group))
        return carry

    lax.fori_loop(1, groups, both, 0)
    finished[...] = totals[...]
    run(imaging(groups - 1))


def pack_kernel(section_ref, row_ref, slot_ref, *refs):
    packed = refs[-1]
    section = section_ref[0]
    half = row_ref.shape[0] // 2
    width = packed.shape[0] // (slot_ref.shape[0] // 2)
    packed[...] = jnp.zeros_like(packed)
    lane = lax.broadcasted_iota(jnp.int32, (1, 128), 1)

    def note(step, carry):
        for k in range(2):
            target = step * 2 + k
            slots = jnp.where(lane == 0, slot_ref[2 * target], slot_ref[2 * target + 1])
            packed[pl.ds(target * width + width - 1, 1), :] = slots.astype(jnp.float32)
        return carry

    lax.fori_loop(0, slot_ref.shape[0] // 4, note, 0)
    add_rows(row_ref, section * half, width, refs[:-1], packed)


def pack_more_kernel(section_ref, row_ref, *refs):
    packed = refs[-1]
    half = row_ref.shape[0] // 2
    packed[...] = refs[0][...]
    add_rows(row_ref, (1 - section_ref[0]) * half, 33, refs[1:-1], packed)


def add_rows(row_ref, start, width, sources, packed):
    for values in sources:

        def add(step, carry, values=values, start=start):
            for k in range(4):
                item = step * 4 + k
                row = row_ref[start + item]
                top = (row >> 1) * width + (row & 1) * 16
                packed[pl.ds(top, 16), :] = packed[pl.ds(top, 16), :] + values[item]
            return carry

        lax.fori_loop(0, values.shape[0] // 4, add, 0)
        start = start + values.shape[0]


def unpack_kernel(received_ref, out_ref):
    tiles_dev = out_ref.shape[0]
    sources = received_ref.shape[0] // 33
    slots = received_ref[pl.ds(32, sources, stride=33), :].T
    row = jnp.concatenate([slots[0:1, :], slots[1:2, :]], 1)
    tile = lax.broadcasted_iota(jnp.int32, (tiles_dev, 2 * sources), 0).astype(jnp.float32)
    picked = jnp.where(tile == row, 1.0, 0.0).astype(jnp.bfloat16)
    picked = jnp.concatenate([picked, picked], 1)
    for pair in range(8):
        columns = []
        for column in (2 * pair, 2 * pair + 1):
            values = jnp.concatenate(
                [received_ref[pl.ds(16 * rank + column, sources, stride=33), :] for rank in range(2)], 0
            )
            columns.append(jnp.concatenate(split_hi_lo(values), 0))
        out_ref[:, pair * 256 : (pair + 1) * 256] = jnp.dot(
            picked, jnp.concatenate(columns, 1), preferred_element_type=jnp.float32
        )


SMEM = pl.BlockSpec(memory_space=pltpu.SMEM)
VMEM = pl.BlockSpec(memory_space=pltpu.VMEM)
ANY = pl.BlockSpec(memory_space=pl.ANY)


def call(kernel, name, out_shape, in_specs, out_specs, scratch=(), flops=1_000_000, moved=1_000_000, mib=8):
    return pl.pallas_call(
        kernel,
        out_shape=out_shape,
        in_specs=in_specs,
        out_specs=out_specs,
        scratch_shapes=list(scratch),
        compiler_params=pltpu.CompilerParams(vmem_limit_bytes=mib * 1024 * 1024),
        cost_estimate=pl.CostEstimate(flops=flops, bytes_accessed=moved, transcendentals=0),
        name=name,
    )


def shards(visibilities, uv_coords, w_terms, stations, tile_ids, owner_map, jones_gains):
    sub_count = visibilities.shape[1]
    samples = visibilities.shape[4] * visibilities.shape[5]
    half = sub_count // 2
    grid_size = lax.axis_size("grid")
    tiles_dev = owner_map.shape[0] // grid_size
    section_index = lax.axis_index("section").astype(jnp.int32)
    section = section_index.reshape(1)
    swap = [(0, 1), (1, 0)]
    shape_f32 = lambda *shape: jax.ShapeDtypeStruct(shape, jnp.float32)
    shape_i32 = lambda *shape: jax.ShapeDtypeStruct(shape, jnp.int32)

    peers, start = [], 0
    for size in CHUNKS:
        rows = lax.dynamic_slice_in_dim(visibilities[0], (1 - section_index) * half + start, size, 0)
        peers.append(lax.ppermute(rows, "section", swap))
        start += size
    coefs, own, row_index, slots = call(
        prep_kernel,
        "prep",
        (
            shape_f32(16, 16, 128),
            shape_f32(half, *visibilities.shape[2:]),
            shape_i32(sub_count),
            shape_i32(2 * grid_size),
        ),
        [SMEM, SMEM, SMEM, ANY, VMEM, ANY],
        (VMEM, VMEM, SMEM, SMEM),
        [pltpu.VMEM((128, 128), jnp.float32)] * 3
        + [pltpu.SMEM(owner_map.shape, jnp.int32), pltpu.SemaphoreType.DMA((2,))],
    )(section, stations, tile_ids, owner_map, jones_gains, visibilities)

    constants = [jnp.asarray(table) for table in tables(samples)]
    uv_rows = uv_coords.reshape(2 * sub_count, uv_coords.shape[2])
    mine, theirs, start = [], [], 0
    for chunk, size in enumerate(CHUNKS):
        kept, other = call(
            lambda *refs, start=start: grid_kernel(start, *refs),
            "grid_chunk",
            (shape_f32(size, 16, 128),) * 2,
            [SMEM, SMEM] + [VMEM] * 7,
            (VMEM, VMEM),
            [
                pltpu.VMEM((GROUP, 64, 128), jnp.float32),
                pltpu.VMEM((16, 16, 128), jnp.float32),
                pltpu.VMEM((56, 128), jnp.float32),
                pltpu.VMEM((GROUP, 32, 128), jnp.float32),
                pltpu.VMEM((GROUP, 32, 128), jnp.float32),
            ],
            flops=size * 300_000_000,
            moved=size * 100_000,
            mib=12,
        )(section, w_terms, coefs, own, peers[chunk], uv_rows, *constants)
        mine.append(kept)
        theirs.append(lax.ppermute(other, "section", swap))
        start += size

    packed_shape = shape_f32(33 * grid_size, 128)
    packed = call(
        pack_kernel, "pack", packed_shape, [SMEM] * 3 + [VMEM] * len(CHUNKS), VMEM, flops=100_000_000
    )(section, row_index, slots, *mine)
    packed = call(
        pack_more_kernel, "pack_more", packed_shape, [SMEM] * 2 + [VMEM] * (1 + len(CHUNKS)), VMEM
    )(section, row_index, packed, *theirs)
    received = lax.all_to_all(
        packed.reshape(grid_size, 1, 33 * 128), "grid", split_axis=0, concat_axis=0, tiled=True
    ).reshape(33 * grid_size, 128)
    tiles = call(unpack_kernel, "unpack", shape_f32(tiles_dev, 2048), [VMEM], VMEM)(received)
    return tiles[None]


def solution(mesh):
    in_specs = (
        P("section", "grid", None, None, None, None),
        P("grid", None, None),
        P("grid"),
        P(None, "grid"),
        P("grid"),
        P(),
        P(),
    )
    out_specs = P("section", "grid", None)
    return jax.shard_map(shards, mesh=mesh, in_specs=in_specs, out_specs=out_specs, check_vma=False)
```

```python
import math

import numpy as np
import jax
import jax.numpy as jnp
from jax import lax
from jax.experimental import pallas as pl
from jax.experimental.pallas import tpu as pltpu
from jax.sharding import PartitionSpec as P

SIDE = 32
CHUNKS = (48,)
GROUP = 4

PIXELS = np.concatenate([np.arange(16), -1 - np.arange(16)]).astype(np.float64)


def fit_even(function, reach, terms):
    nodes = np.cos(np.pi * (np.arange(64) + 0.5) / 64)
    square = (nodes + 1.0) / 2.0 * reach * reach
    cheb = np.polynomial.chebyshev.chebfit(nodes, function(np.sqrt(square)), terms - 1)
    poly = np.polynomial.chebyshev.cheb2poly(cheb)
    shift = np.polynomial.polynomial.Polynomial(poly)(
        np.polynomial.polynomial.Polynomial([-1.0, 2.0 / (reach * reach)])
    )
    return [float(np.float32(value)) for value in shift.coef]


def sinc_turns(scale):
    return lambda x: np.where(x > 0, np.sin(scale * x) / np.maximum(x, 1e-30), scale)


HALF_SIN = fit_even(sinc_turns(np.pi), 0.5, 5)
HALF_COS = fit_even(lambda x: np.cos(np.pi * x), 0.5, 6)
STEP_SIN = fit_even(sinc_turns(2 * np.pi), 0.0625, 3)
STEP_COS = fit_even(lambda x: np.cos(2 * np.pi * x), 0.0625, 4)


def horner(coefs, square):
    total = square * coefs[-1] + coefs[-2]
    for value in coefs[-3::-1]:
        total = total * square + value
    return total


def sincos_half(x):
    square = x * x
    half_sin = x * horner(HALF_SIN, square)
    half_cos = horner(HALF_COS, square)
    twice = half_sin + half_sin
    return twice * half_cos, 1.0 - twice * half_sin


def sincos_turns(x):
    return sincos_half(x - jnp.round(x))


def sincos_step(x):
    square = x * x
    return x * horner(STEP_SIN, square), horner(STEP_COS, square)


def spread(ref, row):
    return ref[pl.ds(row, 8, stride=0), :]


def split_hi_lo(values):
    high = values.astype(jnp.bfloat16)
    low = (values - high.astype(jnp.float32)).astype(jnp.bfloat16)
    return high, low


def np_split(values):
    high = np.asarray(values, np.float32).astype(jnp.bfloat16)
    low = (np.asarray(values, np.float32) - high.astype(np.float32)).astype(jnp.bfloat16)
    return high, low


def tables(samples):
    row_p = PIXELS[:, None]
    lane_p = np.tile(PIXELS, GROUP)[None, :]
    sine_row, sine_lane = 0.6 * row_p / SIDE, 0.6 * lane_p / SIDE
    n_term = np.sqrt(1.0 - sine_row**2 - sine_lane**2) - 1.0
    taper = np.cos(np.pi * row_p / (SIDE + 4.0)) * np.cos(np.pi * lane_p / (SIDE + 4.0))
    pixel_tables = np.stack([n_term, taper / math.sqrt(samples) / SIDE]).astype(np.float32)

    freq = np.arange(SIDE) - SIDE // 2
    angle = 2.0 * np.pi / SIDE * PIXELS[:, None] * freq[None, :]
    cos_t = np.kron(np.eye(GROUP), np.cos(angle))
    sin_t = np.kron(np.eye(GROUP), np.sin(angle))
    high, low = np_split(np.block([[cos_t, -sin_t], [sin_t, cos_t]]))
    right_all = np.concatenate([high, high, low], 0)

    order = np.arange(SIDE).reshape(8, 4).T.reshape(-1)
    angle = 2.0 * np.pi / SIDE * freq[order][:, None] * PIXELS[None, :]
    high, low = np_split(np.block([[np.cos(angle), np.sin(angle)], [-np.sin(angle), np.cos(angle)]]))
    left_all = np.concatenate([high, high, low], 1)
    return pixel_tables, right_all, left_all


def swap_groups(parts, low_half, odd_quarter):
    a0 = jnp.where(low_half, parts[0], pltpu.roll(parts[2], 64, 1))
    a2 = jnp.where(low_half, pltpu.roll(parts[0], 64, 1), parts[2])
    a1 = jnp.where(low_half, parts[1], pltpu.roll(parts[3], 64, 1))
    a3 = jnp.where(low_half, pltpu.roll(parts[1], 64, 1), parts[3])
    return [
        jnp.where(odd_quarter, pltpu.roll(a1, 32, 1), a0),
        jnp.where(odd_quarter, a1, pltpu.roll(a0, 96, 1)),
        jnp.where(odd_quarter, pltpu.roll(a3, 32, 1), a2),
        jnp.where(odd_quarter, a3, pltpu.roll(a2, 96, 1)),
    ]


def prep_kernel(section_ref, stations_ref, jones_ref, *refs):
    count = (len(refs) - 4) // 2
    for source, target in zip(refs[:count], refs[count + 1 : 2 * count + 1]):
        target[...] = source[...]
    coef_ref, (p_rows, q_rows, turned) = refs[count], refs[2 * count + 1 :]
    section = section_ref[0]
    half = stations_ref.shape[1] // 2

    p_rows[...] = jnp.zeros_like(p_rows)
    q_rows[...] = jnp.zeros_like(q_rows)

    def fetch(step, carry):
        for k in range(8):
            item = section * half + step * 8 + k
            p_rows[pl.ds(step * 8 + k, 1), :] = jones_ref[pl.ds(stations_ref[0, item], 1), :]
            q_rows[pl.ds(step * 8 + k, 1), :] = jones_ref[pl.ds(stations_ref[1, item], 1), :]
        return carry

    lax.fori_loop(0, half // 8, fetch, 0)
    lane = lax.broadcasted_iota(jnp.int32, (128, 128), 1)
    odd = (lane & 1) == 1
    high_pair = (lane & 2) == 2

    def swap_one(x):
        return jnp.where(odd, pltpu.roll(x, 1, 1), pltpu.roll(x, 127, 1))

    def swap_two(x):
        return jnp.where(high_pair, pltpu.roll(x, 2, 1), pltpu.roll(x, 126, 1))

    gain_p = p_rows[...]
    gain_p_turned = swap_one(gain_p)
    for kind in range(2):
        gain_q = q_rows[...] if kind == 0 else swap_two(q_rows[...])
        straight = gain_p * gain_q
        crossed = gain_p_turned * gain_q
        real = straight + swap_one(straight)
        imag = swap_one(crossed) - crossed
        turned[...] = jnp.where(odd, imag, real).T
        for place in range(8):
            coef_ref[kind * 8 + place] = turned[pl.ds(place, 16, stride=8), :]


def clear_slots(slot_ref):
    for target in range(slot_ref.shape[0]):
        slot_ref[target] = -1


def place_items(first, count, tile_ref, owner_ref, row_ref, slot_ref):
    tiles_dev = owner_ref.shape[0] * 128 // (slot_ref.shape[0] // 2)
    shift = tiles_dev.bit_length() - 1
    assert tiles_dev == 1 << shift
    for k in range(count):
        item = jnp.minimum(first + k, tile_ref.shape[0] - 1)
        tile = tile_ref[item]
        position = owner_ref[tile >> 7, tile & 127]
        target = 2 * (position >> shift)
        slot = position & (tiles_dev - 1)
        known = slot_ref[target]
        row = target + jnp.where((known == -1) | (known == slot), 0, 1)
        slot_ref[row] = slot
        row_ref[item] = row


def grid_kernel(chunk_start, placing, section_ref, w_ref, coef_ref, own_ref, peer_ref, uv_ref, pixel_ref, right_ref,
                left_ref, *refs):
    if placing:
        tile_ref, owner_any, mine_ref, other_ref, row_ref, slot_ref = refs[:6]
        owner_ref, owner_sem = refs[-2:]
        owner_copy = pltpu.make_async_copy(owner_any, owner_ref, owner_sem)
        owner_copy.start()
        clear_slots(slot_ref)
    else:
        mine_ref, other_ref = refs[:2]
    start = 6 if placing else 2
    bcast_all, rolled_all, rows_all, totals, finished = refs[start : start + 5]
    section = section_ref[0]
    groups = mine_ref.shape[0] // GROUP
    half = w_ref.shape[0] // 2
    lane = lax.broadcasted_iota(jnp.int32, (8, 128), 1)
    sub_lane = lax.broadcasted_iota(jnp.int32, (8, 128), 0).astype(jnp.float32)

    def gridding(group, side):
        first = group * GROUP
        bcast, rolled, wave_rows = bcast_all.at[side], rolled_all.at[side], rows_all.at[side]
        shift = lax.rem(128 - (chunk_start + first), 128)
        for place in range(16):
            rolled[place] = pltpu.roll(coef_ref[place], shift, 1)
        cells = uv_ref[pl.ds(pl.multiple_of(section * (2 * half) + 2 * (chunk_start + first), 8), 8), :]
        wave_rows[0:8], wave_rows[8:16] = sincos_turns(cells * (8.0 / SIDE))
        wave_rows[16:24], wave_rows[24:32] = sincos_step(cells * (8.0 / (64.0 * SIDE)))
        sums = cells + pltpu.roll(cells, 7, 0)
        wave_rows[32:40], wave_rows[40:48] = sincos_step(sums * (8.0 / (128.0 * SIDE)))
        wave_rows[48:56] = cells
        for g in range(GROUP):
            corr = [None, None]
            for row in range(2):
                for kind in range(2):
                    column = (row ^ section) ^ kind
                    source = own_ref if row == 0 else peer_ref
                    at = first + g + (section * half + chunk_start if row == 0 else 0)
                    vis_real = source[at, column, 0]
                    vis_imag = source[at, column, 1]
                    for pol in range(2):
                        place = kind * 8 + (pol ^ section) * 4 + (row ^ section) * 2
                        cr = jnp.broadcast_to(rolled[place][:, g : g + 1], (16, 128))
                        ci = jnp.broadcast_to(rolled[place + 1][:, g : g + 1], (16, 128))
                        real = cr * vis_real - ci * vis_imag
                        imag = cr * vis_imag + ci * vis_real
                        if corr[pol] is None:
                            corr[pol] = [real, imag]
                        else:
                            corr[pol] = [corr[pol][0] + real, corr[pol][1] + imag]
            u_row = spread(wave_rows, 48 + 2 * g)
            v_row = spread(wave_rows, 49 + 2 * g)
            turn_sin, turn_cos = sincos_half((u_row + v_row) * ((1.0 + sub_lane / 64.0) / (2.0 * SIDE)))
            step_sin, step_cos = spread(wave_rows, 32 + 2 * g), spread(wave_rows, 40 + 2 * g)
            turn_sin, turn_cos = (
                jnp.concatenate([turn_sin, turn_sin * step_cos + turn_cos * step_sin], 0),
                jnp.concatenate([turn_cos, turn_cos * step_cos - turn_sin * step_sin], 0),
            )
            for pol in range(2):
                real, imag = corr[pol]
                bcast[g, pol * 16 : pol * 16 + 16] = real * turn_cos + imag * turn_sin
                bcast[g, 32 + pol * 16 : 48 + pol * 16] = imag * turn_cos - real * turn_sin
            yield

            waves = []
            for axis, cell in enumerate((u_row, v_row)):
                turns = cell * ((sub_lane + 0.5) / SIDE)
                sin_0, cos_0 = sincos_turns(turns)
                sin_d, cos_d = sincos_step(turns * (1.0 / 64.0))
                place = 2 * g + axis
                up_sin, up_cos = spread(wave_rows, place), spread(wave_rows, 8 + place)
                upd_sin, upd_cos = spread(wave_rows, 16 + place), spread(wave_rows, 24 + place)
                cos_0, sin_0, cos_d, sin_d = (
                    jnp.stack([cos_0, cos_0 * up_cos - sin_0 * up_sin]),
                    jnp.stack([sin_0, sin_0 * up_cos + cos_0 * up_sin]),
                    jnp.stack([cos_d, cos_d * upd_cos - sin_d * upd_sin]),
                    jnp.stack([sin_d, sin_d * upd_cos + cos_d * upd_sin]),
                )
                cos_1 = cos_0 * cos_d - sin_0 * sin_d
                sin_1 = sin_0 * cos_d + cos_0 * sin_d
                waves.append([cos_0, sin_0, cos_1, sin_1, cos_d + cos_d])
            yield
            total = None
            for pair in range(8):
                left_parts, right_parts = [], []
                for c in (2 * pair, 2 * pair + 1):
                    cos_u, sin_u = waves[0][0], waves[0][1]
                    cos_v, sin_v = waves[1][0], waves[1][1]
                    left_parts.append(jnp.concatenate([cos_u, sin_u], 0).reshape(32, 128))
                    pieces = []
                    for k in range(4):
                        line = spread(bcast.at[g], 16 * k + c)[None]
                        pieces.append((cos_v * line).reshape(16, 128))
                        pieces.append((sin_v * line).reshape(16, 128))
                    right_parts.append(jnp.concatenate(pieces, 0))
                    for wave in waves:
                        cos_0, sin_0, cos_1, sin_1, twice = wave
                        wave[0], wave[1] = cos_1, sin_1
                        if c < 14:
                            wave[2], wave[3] = twice * cos_1 - cos_0, twice * sin_1 - sin_0
                part = lax.dot_general(
                    jnp.concatenate(left_parts, 1).astype(jnp.bfloat16),
                    jnp.concatenate(right_parts, 1).astype(jnp.bfloat16),
                    (((1,), (1,)), ((), ())),
                    preferred_element_type=jnp.float32,
                )
                total = part if total is None else total + part
                yield
            totals[side, g] = total

    def imaging(group, side):
        first = group * GROUP
        lane16 = lax.broadcasted_iota(jnp.int32, (16, 128), 1)
        upper = (lane16 & 16) == 16
        sign = jnp.where(upper, -1.0, 1.0)
        low_half, odd_quarter = lane16 < 64, (lane16 & 32) == 32
        w_first = section * half + chunk_start + first
        w_row = jnp.where(
            lane < 64,
            jnp.where(lane < 32, w_ref[w_first], w_ref[w_first + 1]),
            jnp.where(lane < 96, w_ref[w_first + 2], w_ref[w_first + 3]),
        )
        w_row = jnp.concatenate([w_row, w_row], 0)
        turned = []
        for k in range(2):
            rows = slice(k * 16, k * 16 + 16)
            w_sin, w_cos = sincos_turns(pixel_ref[0, rows] * w_row)
            turned.append((w_sin * pixel_ref[1, rows], w_cos * pixel_ref[1, rows]))
            yield
        parts = []
        for k in range(2):
            sums = swap_groups(
                [finished[side, g, k * 16 : k * 16 + 16] for g in range(GROUP)], low_half, odd_quarter
            )
            yield
            for value in sums:
                parts.append(
                    (
                        jnp.where(upper, pltpu.roll(value, 16, 1), value),
                        sign * jnp.where(upper, value, pltpu.roll(value, 112, 1)),
                    )
                )
                yield
        fields = []
        for pol in range(2):
            xa, xb, ya, yb = parts[pol], parts[2 + pol], parts[4 + pol], parts[6 + pol]
            even_re, even_im = xa[0] - xb[1], xb[0] + xa[1]
            odd_re, odd_im = yb[0] + ya[1], ya[0] - yb[1]
            for k in range(2):
                w_sin, w_cos = turned[k]
                image_re = even_re - odd_re if k == 0 else even_re + odd_re
                image_im = even_im + odd_im if k == 0 else even_im - odd_im
                fields.append(
                    jnp.concatenate(
                        [image_re * w_cos - image_im * w_sin, image_re * w_sin + image_im * w_cos], 1
                    )
                )
                yield
        pieces = []
        for field in fields:
            high, low = split_hi_lo(field)
            pieces.append(jnp.concatenate([high, low, high], 1))
            yield
        rows = jnp.dot(jnp.concatenate(pieces, 0), right_ref[...], preferred_element_type=jnp.float32)
        yield
        for pol, out_ref in enumerate((mine_ref, other_ref)):
            high, low = split_hi_lo(rows[pol * 32 : pol * 32 + 32])
            stack = jnp.concatenate(
                [high[:, :128], high[:, 128:], low[:, :128], low[:, 128:], high[:, :128], high[:, 128:]], 0
            )
            yield
            uv = jnp.dot(left_ref[...], stack, preferred_element_type=jnp.float32)
            yield
            for part in range(2):
                outs = swap_groups(
                    [uv[part * 32 + k * 8 : part * 32 + k * 8 + 8] for k in range(4)], lane < 64, (lane & 32) == 32
                )
                for g in range(GROUP):
                    out_ref[first + g, part * 8 : part * 8 + 8, :] = outs[g]
                yield

    def run(work):
        for _ in work:
            pass

    def image_pair(pair):
        finished[...] = totals[...]
        second = imaging(2 * pair + 1, 1)
        for _ in imaging(2 * pair, 0):
            next(second)
        run(second)

    def grid_pair(pair):
        run(gridding(2 * pair, 0))
        run(gridding(2 * pair + 1, 1))

    pairs = groups // 2
    grid_pair(0)
    if placing:
        owner_copy.wait()
        each = -(-tile_ref.shape[0] // (pairs - 1))

    def both(pair, carry):
        if placing:
            place_items((pair - 1) * each, each, tile_ref, owner_ref, row_ref, slot_ref)
        image_pair(pair - 1)
        grid_pair(pair)
        return carry

    lax.fori_loop(1, pairs, both, 0)
    image_pair(pairs - 1)


def pack_kernel(section_ref, row_ref, slot_ref, *refs):
    packed = refs[-1]
    section = section_ref[0]
    half = row_ref.shape[0] // 2
    width = packed.shape[0] // (slot_ref.shape[0] // 2)
    packed[...] = jnp.zeros_like(packed)
    lane = lax.broadcasted_iota(jnp.int32, (1, 128), 1)

    def note(step, carry):
        for k in range(2):
            target = step * 2 + k
            slots = jnp.where(lane == 0, slot_ref[2 * target], slot_ref[2 * target + 1])
            packed[pl.ds(target * width + width - 1, 1), :] = slots.astype(jnp.float32)
        return carry

    lax.fori_loop(0, slot_ref.shape[0] // 4, note, 0)
    start = section * half
    for values in refs[: len(CHUNKS)]:
        add_rows(row_ref, start, width, values, packed)
        start = start + values.shape[0]
    start = (1 - section) * half
    for values in refs[len(CHUNKS) : -1]:
        add_rows(row_ref, start, width, values, packed)
        start = start + values.shape[0]


def pack_more_kernel(section_ref, row_ref, before_ref, values, packed):
    half = row_ref.shape[0] // 2
    packed[...] = before_ref[...]
    add_rows(row_ref, (2 - section_ref[0]) * half - values.shape[0], 33, values, packed)


def add_rows(row_ref, start, width, values, packed):
    def add(step, carry):
        for k in range(4):
            item = step * 4 + k
            row = row_ref[start + item]
            top = (row >> 1) * width + (row & 1) * 16
            packed[pl.ds(top, 16), :] = packed[pl.ds(top, 16), :] + values[item]
        return carry

    lax.fori_loop(0, values.shape[0] // 4, add, 0)


def unpack_kernel(received_ref, out_ref):
    tiles_dev = out_ref.shape[0]
    sources = received_ref.shape[0] // 33
    slots = received_ref[pl.ds(32, sources, stride=33), :].T
    row = jnp.concatenate([slots[0:1, :], slots[1:2, :]], 1)
    tile = lax.broadcasted_iota(jnp.int32, (tiles_dev, 2 * sources), 0).astype(jnp.float32)
    picked = jnp.where(tile == row, 1.0, 0.0).astype(jnp.bfloat16)
    picked = jnp.concatenate([picked, picked], 1)
    for pair in range(8):
        columns = []
        for column in (2 * pair, 2 * pair + 1):
            values = jnp.concatenate(
                [received_ref[pl.ds(16 * rank + column, sources, stride=33), :] for rank in range(2)], 0
            )
            columns.append(jnp.concatenate(split_hi_lo(values), 0))
        out_ref[:, pair * 256 : (pair + 1) * 256] = jnp.dot(
            picked, jnp.concatenate(columns, 1), preferred_element_type=jnp.float32
        )


SMEM = pl.BlockSpec(memory_space=pltpu.SMEM)
VMEM = pl.BlockSpec(memory_space=pltpu.VMEM)
HBM = pl.BlockSpec(memory_space=pltpu.HBM)


def call(kernel, name, out_shape, in_specs, out_specs, scratch=(), flops=1_000_000, moved=1_000_000, mib=8):
    return pl.pallas_call(
        kernel,
        out_shape=out_shape,
        in_specs=in_specs,
        out_specs=out_specs,
        scratch_shapes=list(scratch),
        compiler_params=pltpu.CompilerParams(vmem_limit_bytes=mib * 1024 * 1024),
        cost_estimate=pl.CostEstimate(flops=flops, bytes_accessed=moved, transcendentals=0),
        name=name,
    )


def shards(visibilities, uv_coords, w_terms, stations, tile_ids, owner_map, jones_gains):
    sub_count = visibilities.shape[1]
    samples = visibilities.shape[4] * visibilities.shape[5]
    half = sub_count // 2
    grid_size = lax.axis_size("grid")
    tiles_dev = owner_map.shape[0] // grid_size
    section_index = lax.axis_index("section").astype(jnp.int32)
    section = section_index.reshape(1)
    swap = [(0, 1), (1, 0)]
    shape_f32 = lambda *shape: jax.ShapeDtypeStruct(shape, jnp.float32)
    shape_i32 = lambda *shape: jax.ShapeDtypeStruct(shape, jnp.int32)

    peers, start = [], 0
    for size in CHUNKS:
        part = lax.dynamic_slice_in_dim(visibilities[0], (1 - section_index) * half + start, size, 0)
        peers.append(lax.ppermute(part, "section", swap))
        start += size
    passed = [jnp.asarray(table) for table in tables(samples)]
    passed += [uv_coords.reshape(2 * sub_count, uv_coords.shape[2]), owner_map.reshape(-1, 128)]
    coefs, *constants, uv_rows, owner_rows = call(
        prep_kernel,
        "prep",
        (shape_f32(16, 16, 128),) + tuple(jax.ShapeDtypeStruct(x.shape, x.dtype) for x in passed),
        [SMEM, SMEM, VMEM] + [VMEM] * len(passed),
        (VMEM,) * (1 + len(passed)),
        [pltpu.VMEM((128, 128), jnp.float32)] * 3,
    )(section, stations, jones_gains, *passed)
    mine, theirs, start = [], [], 0
    for chunk, size in enumerate(CHUNKS):
        placing = chunk == len(CHUNKS) - 1
        results = call(
            lambda *refs, start=start, placing=placing: grid_kernel(start, placing, *refs),
            "grid_chunk",
            (shape_f32(size, 16, 128),) * 2 + ((shape_i32(sub_count), shape_i32(2 * grid_size)) if placing else ()),
            [SMEM, SMEM] + [VMEM] * 7 + ([SMEM, HBM] if placing else []),
            (VMEM, VMEM) + ((SMEM, SMEM) if placing else ()),
            [
                pltpu.VMEM((2, GROUP, 64, 128), jnp.float32),
                pltpu.VMEM((2, 16, 16, 128), jnp.float32),
                pltpu.VMEM((2, 56, 128), jnp.float32),
                pltpu.VMEM((2, GROUP, 32, 128), jnp.float32),
                pltpu.VMEM((2, GROUP, 32, 128), jnp.float32),
            ]
            + ([pltpu.SMEM(owner_rows.shape, jnp.int32), pltpu.SemaphoreType.DMA] if placing else []),
            flops=size * 300_000_000,
            moved=size * 100_000,
            mib=12,
        )(
            section, w_terms, coefs, visibilities[0], peers[chunk], uv_rows, *constants,
            *((tile_ids, owner_rows) if placing else ()),
        )
        mine.append(results[0])
        theirs.append(lax.ppermute(results[1], "section", swap))
        start += size
    row_index, slots = results[2:]

    packed_shape = shape_f32(33 * grid_size, 128)
    packed = call(
        pack_kernel, "pack", packed_shape, [SMEM] * 3 + [VMEM] * (2 * len(CHUNKS) - 1), VMEM, flops=100_000_000
    )(section, row_index, slots, *mine, *theirs[:-1])
    packed = call(pack_more_kernel, "pack_more", packed_shape, [SMEM] * 2 + [VMEM] * 2, VMEM)(
        section, row_index, packed, theirs[-1]
    )
    received = lax.all_to_all(
        packed.reshape(grid_size, 1, 33 * 128), "grid", split_axis=0, concat_axis=0, tiled=True
    ).reshape(33 * grid_size, 128)
    tiles = call(unpack_kernel, "unpack", shape_f32(tiles_dev, 2048), [VMEM], VMEM)(received)
    return tiles[None]


def solution(mesh):
    in_specs = (
        P("section", "grid", None, None, None, None),
        P("grid", None, None),
        P("grid"),
        P(None, "grid"),
        P("grid"),
        P(),
        P(),
    )
    out_specs = P("section", "grid", None)
    return jax.shard_map(shards, mesh=mesh, in_specs=in_specs, out_specs=out_specs, check_vma=False)
```

```python
import math

import numpy as np
import jax
import jax.numpy as jnp
from jax import lax
from jax.experimental import pallas as pl
from jax.experimental.pallas import tpu as pltpu
from jax.sharding import PartitionSpec as P

SIDE = 32
CHUNKS = (48,)
GROUP = 4

PIXELS = np.concatenate([np.arange(16), -1 - np.arange(16)]).astype(np.float64)


def fit_even(function, reach, terms):
    nodes = np.cos(np.pi * (np.arange(64) + 0.5) / 64)
    square = (nodes + 1.0) / 2.0 * reach * reach
    cheb = np.polynomial.chebyshev.chebfit(nodes, function(np.sqrt(square)), terms - 1)
    poly = np.polynomial.chebyshev.cheb2poly(cheb)
    shift = np.polynomial.polynomial.Polynomial(poly)(
        np.polynomial.polynomial.Polynomial([-1.0, 2.0 / (reach * reach)])
    )
    return [float(np.float32(value)) for value in shift.coef]


def sinc_turns(scale):
    return lambda x: np.where(x > 0, np.sin(scale * x) / np.maximum(x, 1e-30), scale)


HALF_SIN = fit_even(sinc_turns(np.pi), 0.5, 5)
HALF_COS = fit_even(lambda x: np.cos(np.pi * x), 0.5, 6)
STEP_SIN = fit_even(sinc_turns(2 * np.pi), 0.0625, 3)
STEP_COS = fit_even(lambda x: np.cos(2 * np.pi * x), 0.0625, 4)


def horner(coefs, square):
    total = square * coefs[-1] + coefs[-2]
    for value in coefs[-3::-1]:
        total = total * square + value
    return total


def sincos_half(x):
    square = x * x
    half_sin = x * horner(HALF_SIN, square)
    half_cos = horner(HALF_COS, square)
    twice = half_sin + half_sin
    return twice * half_cos, 1.0 - twice * half_sin


def sincos_turns(x):
    return sincos_half(x - jnp.round(x))


def sincos_step(x):
    square = x * x
    return x * horner(STEP_SIN, square), horner(STEP_COS, square)


def spread(ref, row):
    return ref[pl.ds(row, 8, stride=0), :]


def split_hi_lo(values):
    high = values.astype(jnp.bfloat16)
    low = (values - high.astype(jnp.float32)).astype(jnp.bfloat16)
    return high, low


def np_split(values):
    high = np.asarray(values, np.float32).astype(jnp.bfloat16)
    low = (np.asarray(values, np.float32) - high.astype(np.float32)).astype(jnp.bfloat16)
    return high, low


def tables(samples):
    row_p = PIXELS[:, None]
    lane_p = np.tile(PIXELS, GROUP)[None, :]
    sine_row, sine_lane = 0.6 * row_p / SIDE, 0.6 * lane_p / SIDE
    n_term = np.sqrt(1.0 - sine_row**2 - sine_lane**2) - 1.0
    taper = np.cos(np.pi * row_p / (SIDE + 4.0)) * np.cos(np.pi * lane_p / (SIDE + 4.0))
    pixel_tables = np.stack([n_term, taper / math.sqrt(samples) / SIDE]).astype(np.float32)

    freq = np.arange(SIDE) - SIDE // 2
    angle = 2.0 * np.pi / SIDE * PIXELS[:, None] * freq[None, :]
    cos_t = np.kron(np.eye(GROUP), np.cos(angle))
    sin_t = np.kron(np.eye(GROUP), np.sin(angle))
    high, low = np_split(np.block([[cos_t, -sin_t], [sin_t, cos_t]]))
    right_all = np.concatenate([high, high, low], 0)

    order = np.arange(SIDE).reshape(8, 4).T.reshape(-1)
    angle = 2.0 * np.pi / SIDE * freq[order][:, None] * PIXELS[None, :]
    high, low = np_split(np.block([[np.cos(angle), np.sin(angle)], [-np.sin(angle), np.cos(angle)]]))
    left_all = np.concatenate([high, high, low], 1)
    return pixel_tables, right_all, left_all


def swap_groups(parts, low_half, odd_quarter):
    a0 = jnp.where(low_half, parts[0], pltpu.roll(parts[2], 64, 1))
    a2 = jnp.where(low_half, pltpu.roll(parts[0], 64, 1), parts[2])
    a1 = jnp.where(low_half, parts[1], pltpu.roll(parts[3], 64, 1))
    a3 = jnp.where(low_half, pltpu.roll(parts[1], 64, 1), parts[3])
    return [
        jnp.where(odd_quarter, pltpu.roll(a1, 32, 1), a0),
        jnp.where(odd_quarter, a1, pltpu.roll(a0, 96, 1)),
        jnp.where(odd_quarter, pltpu.roll(a3, 32, 1), a2),
        jnp.where(odd_quarter, a3, pltpu.roll(a2, 96, 1)),
    ]


def prep_kernel(section_ref, stations_ref, jones_ref, coef_ref, p_rows, q_rows, turned):
    section = section_ref[0]
    half = stations_ref.shape[1] // 2

    p_rows[...] = jnp.zeros_like(p_rows)
    q_rows[...] = jnp.zeros_like(q_rows)

    def fetch(step, carry):
        for k in range(8):
            item = section * half + step * 8 + k
            p_rows[pl.ds(step * 8 + k, 1), :] = jones_ref[pl.ds(stations_ref[0, item], 1), :]
            q_rows[pl.ds(step * 8 + k, 1), :] = jones_ref[pl.ds(stations_ref[1, item], 1), :]
        return carry

    lax.fori_loop(0, half // 8, fetch, 0)
    lane = lax.broadcasted_iota(jnp.int32, (128, 128), 1)
    odd = (lane & 1) == 1
    high_pair = (lane & 2) == 2

    def swap_one(x):
        return jnp.where(odd, pltpu.roll(x, 1, 1), pltpu.roll(x, 127, 1))

    def swap_two(x):
        return jnp.where(high_pair, pltpu.roll(x, 2, 1), pltpu.roll(x, 126, 1))

    gain_p = p_rows[...]
    gain_p_turned = swap_one(gain_p)
    for kind in range(2):
        gain_q = q_rows[...] if kind == 0 else swap_two(q_rows[...])
        straight = gain_p * gain_q
        crossed = gain_p_turned * gain_q
        real = straight + swap_one(straight)
        imag = swap_one(crossed) - crossed
        turned[...] = jnp.where(odd, imag, real).T
        for place in range(8):
            coef_ref[kind * 8 + place] = turned[pl.ds(place, 16, stride=8), :]


def clear_slots(slot_ref):
    for target in range(slot_ref.shape[0]):
        slot_ref[target] = -1


def place_items(first, count, tile_ref, owner_ref, row_ref, slot_ref):
    tiles_dev = owner_ref.shape[0] // (slot_ref.shape[0] // 2)
    shift = tiles_dev.bit_length() - 1
    assert tiles_dev == 1 << shift
    for k in range(count):
        item = jnp.minimum(first + k, tile_ref.shape[0] - 1)
        position = owner_ref[tile_ref[item]]
        target = 2 * (position >> shift)
        slot = position & (tiles_dev - 1)
        known = slot_ref[target]
        row = target + jnp.where((known == -1) | (known == slot), 0, 1)
        slot_ref[row] = slot
        row_ref[item] = row


def grid_kernel(chunk_start, placing, section_ref, w_ref, coef_ref, own_ref, peer_ref, uv_ref, pixel_ref, right_ref,
                left_ref, *refs):
    if placing:
        tile_ref, owner_any, mine_ref, other_ref, row_ref, slot_ref = refs[:6]
        owner_ref, owner_sem = refs[-2:]
        owner_copy = pltpu.make_async_copy(owner_any, owner_ref, owner_sem)
        owner_copy.start()
        clear_slots(slot_ref)
    else:
        mine_ref, other_ref = refs[:2]
    start = 6 if placing else 2
    bcast_all, rolled_all, rows_all, totals, finished = refs[start : start + 5]
    section = section_ref[0]
    groups = mine_ref.shape[0] // GROUP
    half = w_ref.shape[0] // 2
    lane = lax.broadcasted_iota(jnp.int32, (8, 128), 1)
    sub_lane = lax.broadcasted_iota(jnp.int32, (8, 128), 0).astype(jnp.float32)

    def gridding(group, side):
        first = group * GROUP
        bcast, rolled, wave_rows = bcast_all.at[side], rolled_all.at[side], rows_all.at[side]
        shift = lax.rem(128 - (chunk_start + first), 128)
        for place in range(16):
            rolled[place] = pltpu.roll(coef_ref[place], shift, 1)
        cells = uv_ref[pl.ds(pl.multiple_of(section * (2 * half) + 2 * (chunk_start + first), 8), 8), :]
        wave_rows[0:8], wave_rows[8:16] = sincos_turns(cells * (8.0 / SIDE))
        wave_rows[16:24], wave_rows[24:32] = sincos_step(cells * (8.0 / (64.0 * SIDE)))
        sums = cells + pltpu.roll(cells, 7, 0)
        wave_rows[32:40], wave_rows[40:48] = sincos_step(sums * (8.0 / (128.0 * SIDE)))
        wave_rows[48:56] = cells
        for g in range(GROUP):
            corr = [None, None]
            for row in range(2):
                for kind in range(2):
                    column = (row ^ section) ^ kind
                    source = own_ref if row == 0 else peer_ref
                    at = first + g + (chunk_start if row == 0 else 0)
                    vis_real = source[at, column, 0]
                    vis_imag = source[at, column, 1]
                    for pol in range(2):
                        place = kind * 8 + (pol ^ section) * 4 + (row ^ section) * 2
                        cr = jnp.broadcast_to(rolled[place][:, g : g + 1], (16, 128))
                        ci = jnp.broadcast_to(rolled[place + 1][:, g : g + 1], (16, 128))
                        real = cr * vis_real - ci * vis_imag
                        imag = cr * vis_imag + ci * vis_real
                        if corr[pol] is None:
                            corr[pol] = [real, imag]
                        else:
                            corr[pol] = [corr[pol][0] + real, corr[pol][1] + imag]
            u_row = spread(wave_rows, 48 + 2 * g)
            v_row = spread(wave_rows, 49 + 2 * g)
            turn_sin, turn_cos = sincos_half((u_row + v_row) * ((1.0 + sub_lane / 64.0) / (2.0 * SIDE)))
            step_sin, step_cos = spread(wave_rows, 32 + 2 * g), spread(wave_rows, 40 + 2 * g)
            turn_sin, turn_cos = (
                jnp.concatenate([turn_sin, turn_sin * step_cos + turn_cos * step_sin], 0),
                jnp.concatenate([turn_cos, turn_cos * step_cos - turn_sin * step_sin], 0),
            )
            for pol in range(2):
                real, imag = corr[pol]
                bcast[g, pol * 16 : pol * 16 + 16] = real * turn_cos + imag * turn_sin
                bcast[g, 32 + pol * 16 : 48 + pol * 16] = imag * turn_cos - real * turn_sin
            yield

            waves = []
            for axis, cell in enumerate((u_row, v_row)):
                turns = cell * ((sub_lane + 0.5) / SIDE)
                sin_0, cos_0 = sincos_turns(turns)
                sin_d, cos_d = sincos_step(turns * (1.0 / 64.0))
                place = 2 * g + axis
                up_sin, up_cos = spread(wave_rows, place), spread(wave_rows, 8 + place)
                upd_sin, upd_cos = spread(wave_rows, 16 + place), spread(wave_rows, 24 + place)
                cos_0, sin_0, cos_d, sin_d = (
                    jnp.stack([cos_0, cos_0 * up_cos - sin_0 * up_sin]),
                    jnp.stack([sin_0, sin_0 * up_cos + cos_0 * up_sin]),
                    jnp.stack([cos_d, cos_d * upd_cos - sin_d * upd_sin]),
                    jnp.stack([sin_d, sin_d * upd_cos + cos_d * upd_sin]),
                )
                cos_1 = cos_0 * cos_d - sin_0 * sin_d
                sin_1 = sin_0 * cos_d + cos_0 * sin_d
                waves.append([cos_0, sin_0, cos_1, sin_1, cos_d + cos_d])
            yield
            total = None
            for pair in range(8):
                left_parts, right_parts = [], []
                for c in (2 * pair, 2 * pair + 1):
                    cos_u, sin_u = waves[0][0], waves[0][1]
                    cos_v, sin_v = waves[1][0], waves[1][1]
                    left_parts.append(jnp.concatenate([cos_u, sin_u], 0).reshape(32, 128))
                    pieces = []
                    for k in range(4):
                        line = spread(bcast.at[g], 16 * k + c)[None]
                        pieces.append((cos_v * line).reshape(16, 128))
                        pieces.append((sin_v * line).reshape(16, 128))
                    right_parts.append(jnp.concatenate(pieces, 0))
                    for wave in waves:
                        cos_0, sin_0, cos_1, sin_1, twice = wave
                        wave[0], wave[1] = cos_1, sin_1
                        if c < 14:
                            wave[2], wave[3] = twice * cos_1 - cos_0, twice * sin_1 - sin_0
                part = lax.dot_general(
                    jnp.concatenate(left_parts, 1).astype(jnp.bfloat16),
                    jnp.concatenate(right_parts, 1).astype(jnp.bfloat16),
                    (((1,), (1,)), ((), ())),
                    preferred_element_type=jnp.float32,
                )
                total = part if total is None else total + part
                yield
            totals[side, g] = total

    def imaging(group, side):
        first = group * GROUP
        lane16 = lax.broadcasted_iota(jnp.int32, (16, 128), 1)
        upper = (lane16 & 16) == 16
        sign = jnp.where(upper, -1.0, 1.0)
        low_half, odd_quarter = lane16 < 64, (lane16 & 32) == 32
        w_first = section * half + chunk_start + first
        w_row = jnp.where(
            lane < 64,
            jnp.where(lane < 32, w_ref[w_first], w_ref[w_first + 1]),
            jnp.where(lane < 96, w_ref[w_first + 2], w_ref[w_first + 3]),
        )
        w_row = jnp.concatenate([w_row, w_row], 0)
        turned = []
        for k in range(2):
            rows = slice(k * 16, k * 16 + 16)
            w_sin, w_cos = sincos_turns(pixel_ref[0, rows] * w_row)
            turned.append((w_sin * pixel_ref[1, rows], w_cos * pixel_ref[1, rows]))
            yield
        parts = []
        for k in range(2):
            sums = swap_groups(
                [finished[side, g, k * 16 : k * 16 + 16] for g in range(GROUP)], low_half, odd_quarter
            )
            yield
            for value in sums:
                parts.append(
                    (
                        jnp.where(upper, pltpu.roll(value, 16, 1), value),
                        sign * jnp.where(upper, value, pltpu.roll(value, 112, 1)),
                    )
                )
                yield
        fields = []
        for pol in range(2):
            xa, xb, ya, yb = parts[pol], parts[2 + pol], parts[4 + pol], parts[6 + pol]
            even_re, even_im = xa[0] - xb[1], xb[0] + xa[1]
            odd_re, odd_im = yb[0] + ya[1], ya[0] - yb[1]
            for k in range(2):
                w_sin, w_cos = turned[k]
                image_re = even_re - odd_re if k == 0 else even_re + odd_re
                image_im = even_im + odd_im if k == 0 else even_im - odd_im
                fields.append(
                    jnp.concatenate(
                        [image_re * w_cos - image_im * w_sin, image_re * w_sin + image_im * w_cos], 1
                    )
                )
                yield
        pieces = []
        for field in fields:
            high, low = split_hi_lo(field)
            pieces.append(jnp.concatenate([high, low, high], 1))
            yield
        rows = jnp.dot(jnp.concatenate(pieces, 0), right_ref[...], preferred_element_type=jnp.float32)
        yield
        for pol, out_ref in enumerate((mine_ref, other_ref)):
            high, low = split_hi_lo(rows[pol * 32 : pol * 32 + 32])
            stack = jnp.concatenate(
                [high[:, :128], high[:, 128:], low[:, :128], low[:, 128:], high[:, :128], high[:, 128:]], 0
            )
            yield
            uv = jnp.dot(left_ref[...], stack, preferred_element_type=jnp.float32)
            yield
            for part in range(2):
                outs = swap_groups(
                    [uv[part * 32 + k * 8 : part * 32 + k * 8 + 8] for k in range(4)], lane < 64, (lane & 32) == 32
                )
                for g in range(GROUP):
                    out_ref[first + g, part * 8 : part * 8 + 8, :] = outs[g]
                yield

    def run(work):
        for _ in work:
            pass

    def image_pair(pair):
        finished[...] = totals[...]
        second = imaging(2 * pair + 1, 1)
        for _ in imaging(2 * pair, 0):
            next(second)
        run(second)

    def grid_pair(pair):
        run(gridding(2 * pair, 0))
        run(gridding(2 * pair + 1, 1))

    pairs = groups // 2
    grid_pair(0)
    if placing:
        owner_copy.wait()
        each = -(-tile_ref.shape[0] // (pairs - 1))

    def both(pair, carry):
        if placing:
            place_items((pair - 1) * each, each, tile_ref, owner_ref, row_ref, slot_ref)
        image_pair(pair - 1)
        grid_pair(pair)
        return carry

    lax.fori_loop(1, pairs, both, 0)
    image_pair(pairs - 1)


def pack_kernel(section_ref, row_ref, slot_ref, *refs):
    packed = refs[-1]
    section = section_ref[0]
    half = row_ref.shape[0] // 2
    width = packed.shape[0] // (slot_ref.shape[0] // 2)
    packed[...] = jnp.zeros_like(packed)
    lane = lax.broadcasted_iota(jnp.int32, (1, 128), 1)

    def note(step, carry):
        for k in range(2):
            target = step * 2 + k
            slots = jnp.where(lane == 0, slot_ref[2 * target], slot_ref[2 * target + 1])
            packed[pl.ds(target * width + width - 1, 1), :] = slots.astype(jnp.float32)
        return carry

    lax.fori_loop(0, slot_ref.shape[0] // 4, note, 0)
    start = section * half
    for values in refs[: len(CHUNKS)]:
        add_rows(row_ref, start, width, values, packed)
        start = start + values.shape[0]
    start = (1 - section) * half
    for values in refs[len(CHUNKS) : -1]:
        add_rows(row_ref, start, width, values, packed)
        start = start + values.shape[0]


def pack_more_kernel(section_ref, row_ref, before_ref, values, packed):
    half = row_ref.shape[0] // 2
    packed[...] = before_ref[...]
    add_rows(row_ref, (2 - section_ref[0]) * half - values.shape[0], 33, values, packed)


def add_rows(row_ref, start, width, values, packed):
    def add(step, carry):
        for k in range(4):
            item = step * 4 + k
            row = row_ref[start + item]
            top = (row >> 1) * width + (row & 1) * 16
            packed[pl.ds(top, 16), :] = packed[pl.ds(top, 16), :] + values[item]
        return carry

    lax.fori_loop(0, values.shape[0] // 4, add, 0)


def unpack_kernel(received_ref, out_ref):
    tiles_dev = out_ref.shape[0]
    sources = received_ref.shape[0] // 33
    slots = received_ref[pl.ds(32, sources, stride=33), :].T
    row = jnp.concatenate([slots[0:1, :], slots[1:2, :]], 1)
    tile = lax.broadcasted_iota(jnp.int32, (tiles_dev, 2 * sources), 0).astype(jnp.float32)
    picked = jnp.where(tile == row, 1.0, 0.0).astype(jnp.bfloat16)
    picked = jnp.concatenate([picked, picked], 1)
    for pair in range(8):
        columns = []
        for column in (2 * pair, 2 * pair + 1):
            values = jnp.concatenate(
                [received_ref[pl.ds(16 * rank + column, sources, stride=33), :] for rank in range(2)], 0
            )
            columns.append(jnp.concatenate(split_hi_lo(values), 0))
        out_ref[:, pair * 256 : (pair + 1) * 256] = jnp.dot(
            picked, jnp.concatenate(columns, 1), preferred_element_type=jnp.float32
        )


SMEM = pl.BlockSpec(memory_space=pltpu.SMEM)
VMEM = pl.BlockSpec(memory_space=pltpu.VMEM)
HBM = pl.BlockSpec(memory_space=pltpu.HBM)


def call(kernel, name, out_shape, in_specs, out_specs, scratch=(), flops=1_000_000, moved=1_000_000, mib=8, flags=None):
    return pl.pallas_call(
        kernel,
        out_shape=out_shape,
        in_specs=in_specs,
        out_specs=out_specs,
        scratch_shapes=list(scratch),
        compiler_params=pltpu.CompilerParams(vmem_limit_bytes=mib * 1024 * 1024, flags=flags),
        cost_estimate=pl.CostEstimate(flops=flops, bytes_accessed=moved, transcendentals=0),
        name=name,
    )


def shards(visibilities, uv_coords, w_terms, stations, tile_ids, owner_map, jones_gains):
    sub_count = visibilities.shape[1]
    samples = visibilities.shape[4] * visibilities.shape[5]
    half = sub_count // 2
    grid_size = lax.axis_size("grid")
    tiles_dev = owner_map.shape[0] // grid_size
    section_index = lax.axis_index("section").astype(jnp.int32)
    section = section_index.reshape(1)
    swap = [(0, 1), (1, 0)]
    shape_f32 = lambda *shape: jax.ShapeDtypeStruct(shape, jnp.float32)
    shape_i32 = lambda *shape: jax.ShapeDtypeStruct(shape, jnp.int32)

    peers, start = [], 0
    for size in CHUNKS:
        part = lax.dynamic_slice_in_dim(visibilities[0], (1 - section_index) * half + start, size, 0)
        peers.append(lax.ppermute(part, "section", swap))
        start += size
    own = lax.dynamic_slice_in_dim(visibilities[0], section_index * half, half, 0)
    coefs = call(
        prep_kernel,
        "prep",
        shape_f32(16, 16, 128),
        [SMEM, SMEM, VMEM],
        VMEM,
        [pltpu.VMEM((128, 128), jnp.float32)] * 3,
    )(section, stations, jones_gains)

    constants = [jnp.asarray(table) for table in tables(samples)]
    uv_rows = uv_coords.reshape(2 * sub_count, uv_coords.shape[2])
    mine, theirs, start = [], [], 0
    for chunk, size in enumerate(CHUNKS):
        placing = chunk == len(CHUNKS) - 1
        results = call(
            lambda *refs, start=start, placing=placing: grid_kernel(start, placing, *refs),
            "grid_chunk",
            (shape_f32(size, 16, 128),) * 2 + ((shape_i32(sub_count), shape_i32(2 * grid_size)) if placing else ()),
            [SMEM, SMEM] + [VMEM] * 7 + ([SMEM, HBM] if placing else []),
            (VMEM, VMEM) + ((SMEM, SMEM) if placing else ()),
            [
                pltpu.VMEM((2, GROUP, 64, 128), jnp.float32),
                pltpu.VMEM((2, 16, 16, 128), jnp.float32),
                pltpu.VMEM((2, 56, 128), jnp.float32),
                pltpu.VMEM((2, GROUP, 32, 128), jnp.float32),
                pltpu.VMEM((2, GROUP, 32, 128), jnp.float32),
            ]
            + ([pltpu.SMEM(owner_map.shape, jnp.int32), pltpu.SemaphoreType.DMA] if placing else []),
            flops=size * 300_000_000,
            moved=size * 100_000,
            mib=12,
        )(
            section, w_terms, coefs, own, peers[chunk], uv_rows, *constants,
            *((tile_ids, owner_map) if placing else ()),
        )
        mine.append(results[0])
        theirs.append(lax.ppermute(results[1], "section", swap))
        start += size
    row_index, slots = results[2:]

    packed_shape = shape_f32(33 * grid_size, 128)
    packed = call(
        pack_kernel, "pack", packed_shape, [SMEM] * 3 + [VMEM] * (2 * len(CHUNKS) - 1), VMEM, flops=100_000_000
    )(section, row_index, slots, *mine, *theirs[:-1])
    packed = call(pack_more_kernel, "pack_more", packed_shape, [SMEM] * 2 + [VMEM] * 2, VMEM)(
        section, row_index, packed, theirs[-1]
    )
    received = lax.all_to_all(
        packed.reshape(grid_size, 1, 33 * 128), "grid", split_axis=0, concat_axis=0, tiled=True
    ).reshape(33 * grid_size, 128)
    tiles = call(unpack_kernel, "unpack", shape_f32(tiles_dev, 2048), [VMEM], VMEM)(received)
    return tiles[None]


def solution(mesh):
    in_specs = (
        P("section", "grid", None, None, None, None),
        P("grid", None, None),
        P("grid"),
        P(None, "grid"),
        P("grid"),
        P(),
        P(),
    )
    out_specs = P("section", "grid", None)
    return jax.shard_map(shards, mesh=mesh, in_specs=in_specs, out_specs=out_specs, check_vma=False)
```

```python
import math

import numpy as np
import jax
import jax.numpy as jnp
from jax import lax
from jax.experimental import pallas as pl
from jax.experimental.pallas import tpu as pltpu
from jax.sharding import PartitionSpec as P

SIDE = 32
CHUNKS = (48,)
GROUP = 4

PIXELS = np.concatenate([np.arange(16), -1 - np.arange(16)]).astype(np.float64)


def fit_even(function, reach, terms):
    nodes = np.cos(np.pi * (np.arange(64) + 0.5) / 64)
    square = (nodes + 1.0) / 2.0 * reach * reach
    cheb = np.polynomial.chebyshev.chebfit(nodes, function(np.sqrt(square)), terms - 1)
    poly = np.polynomial.chebyshev.cheb2poly(cheb)
    shift = np.polynomial.polynomial.Polynomial(poly)(
        np.polynomial.polynomial.Polynomial([-1.0, 2.0 / (reach * reach)])
    )
    return [float(np.float32(value)) for value in shift.coef]


def sinc_turns(scale):
    return lambda x: np.where(x > 0, np.sin(scale * x) / np.maximum(x, 1e-30), scale)


HALF_SIN = fit_even(sinc_turns(np.pi), 0.5, 5)
HALF_COS = fit_even(lambda x: np.cos(np.pi * x), 0.5, 6)
STEP_SIN = fit_even(sinc_turns(2 * np.pi), 0.0625, 3)
STEP_COS = fit_even(lambda x: np.cos(2 * np.pi * x), 0.0625, 4)


def horner(coefs, square):
    total = square * coefs[-1] + coefs[-2]
    for value in coefs[-3::-1]:
        total = total * square + value
    return total


def sincos_half(x):
    square = x * x
    half_sin = x * horner(HALF_SIN, square)
    half_cos = horner(HALF_COS, square)
    twice = half_sin + half_sin
    return twice * half_cos, 1.0 - twice * half_sin


def sincos_turns(x):
    return sincos_half(x - jnp.round(x))


def sincos_step(x):
    square = x * x
    return x * horner(STEP_SIN, square), horner(STEP_COS, square)


def spread(ref, row):
    return ref[pl.ds(row, 8, stride=0), :]


def split_hi_lo(values):
    high = values.astype(jnp.bfloat16)
    low = (values - high.astype(jnp.float32)).astype(jnp.bfloat16)
    return high, low


def np_split(values):
    high = np.asarray(values, np.float32).astype(jnp.bfloat16)
    low = (np.asarray(values, np.float32) - high.astype(np.float32)).astype(jnp.bfloat16)
    return high, low


def tables(samples):
    row_p = PIXELS[:, None]
    lane_p = np.tile(PIXELS, GROUP)[None, :]
    sine_row, sine_lane = 0.6 * row_p / SIDE, 0.6 * lane_p / SIDE
    n_term = np.sqrt(1.0 - sine_row**2 - sine_lane**2) - 1.0
    taper = np.cos(np.pi * row_p / (SIDE + 4.0)) * np.cos(np.pi * lane_p / (SIDE + 4.0))
    pixel_tables = np.stack([n_term, taper / math.sqrt(samples) / SIDE]).astype(np.float32)

    freq = np.arange(SIDE) - SIDE // 2
    angle = 2.0 * np.pi / SIDE * PIXELS[:, None] * freq[None, :]
    cos_t = np.kron(np.eye(GROUP), np.cos(angle))
    sin_t = np.kron(np.eye(GROUP), np.sin(angle))
    high, low = np_split(np.block([[cos_t, -sin_t], [sin_t, cos_t]]))
    right_all = np.concatenate([high, low], 0)

    order = np.arange(SIDE).reshape(8, 4).T.reshape(-1)
    angle = 2.0 * np.pi / SIDE * freq[order][:, None] * PIXELS[None, :]
    high, low = np_split(np.block([[np.cos(angle), np.sin(angle)], [-np.sin(angle), np.cos(angle)]]))
    left_all = np.concatenate([high, high, low], 1)
    return pixel_tables, right_all, left_all


def swap_groups(parts, low_half, odd_quarter):
    a0 = jnp.where(low_half, parts[0], pltpu.roll(parts[2], 64, 1))
    a2 = jnp.where(low_half, pltpu.roll(parts[0], 64, 1), parts[2])
    a1 = jnp.where(low_half, parts[1], pltpu.roll(parts[3], 64, 1))
    a3 = jnp.where(low_half, pltpu.roll(parts[1], 64, 1), parts[3])
    return [
        jnp.where(odd_quarter, pltpu.roll(a1, 32, 1), a0),
        jnp.where(odd_quarter, a1, pltpu.roll(a0, 96, 1)),
        jnp.where(odd_quarter, pltpu.roll(a3, 32, 1), a2),
        jnp.where(odd_quarter, a3, pltpu.roll(a2, 96, 1)),
    ]


def prep_kernel(section_ref, stations_ref, jones_ref, coef_ref, p_rows, q_rows, turned):
    section = section_ref[0]
    half = stations_ref.shape[1] // 2

    p_rows[...] = jnp.zeros_like(p_rows)
    q_rows[...] = jnp.zeros_like(q_rows)

    def fetch(step, carry):
        for k in range(8):
            item = section * half + step * 8 + k
            p_rows[pl.ds(step * 8 + k, 1), :] = jones_ref[pl.ds(stations_ref[0, item], 1), :]
            q_rows[pl.ds(step * 8 + k, 1), :] = jones_ref[pl.ds(stations_ref[1, item], 1), :]
        return carry

    lax.fori_loop(0, half // 8, fetch, 0)
    lane = lax.broadcasted_iota(jnp.int32, (128, 128), 1)
    odd = (lane & 1) == 1
    high_pair = (lane & 2) == 2

    def swap_one(x):
        return jnp.where(odd, pltpu.roll(x, 1, 1), pltpu.roll(x, 127, 1))

    def swap_two(x):
        return jnp.where(high_pair, pltpu.roll(x, 2, 1), pltpu.roll(x, 126, 1))

    gain_p = p_rows[...]
    gain_p_turned = swap_one(gain_p)
    for kind in range(2):
        gain_q = q_rows[...] if kind == 0 else swap_two(q_rows[...])
        straight = gain_p * gain_q
        crossed = gain_p_turned * gain_q
        real = straight + swap_one(straight)
        imag = swap_one(crossed) - crossed
        turned[...] = jnp.where(odd, imag, real).T
        for place in range(8):
            coef_ref[kind * 8 + place] = turned[pl.ds(place, 16, stride=8), :]


def clear_slots(slot_ref):
    for target in range(slot_ref.shape[0]):
        slot_ref[target] = -1


def place_items(first, count, tile_ref, owner_ref, row_ref, slot_ref):
    tiles_dev = owner_ref.shape[0] // (slot_ref.shape[0] // 2)
    shift = tiles_dev.bit_length() - 1
    assert tiles_dev == 1 << shift
    for k in range(count):
        item = jnp.minimum(first + k, tile_ref.shape[0] - 1)
        position = owner_ref[tile_ref[item]]
        target = 2 * (position >> shift)
        slot = position & (tiles_dev - 1)
        known = slot_ref[target]
        row = target + jnp.where((known == -1) | (known == slot), 0, 1)
        slot_ref[row] = slot
        row_ref[item] = row


def grid_kernel(chunk_start, placing, section_ref, w_ref, coef_ref, own_ref, peer_ref, uv_ref, pixel_ref, right_ref,
                left_ref, *refs):
    if placing:
        tile_ref, owner_any, mine_ref, other_ref, row_ref, slot_ref = refs[:6]
        owner_ref, owner_sem = refs[-2:]
        owner_copy = pltpu.make_async_copy(owner_any, owner_ref, owner_sem)
        owner_copy.start()
        clear_slots(slot_ref)
    else:
        mine_ref, other_ref = refs[:2]
    start = 6 if placing else 2
    bcast_all, rolled_all, rows_all, totals, finished = refs[start : start + 5]
    section = section_ref[0]
    groups = mine_ref.shape[0] // GROUP
    half = w_ref.shape[0] // 2
    lane = lax.broadcasted_iota(jnp.int32, (8, 128), 1)
    sub_lane = lax.broadcasted_iota(jnp.int32, (8, 128), 0).astype(jnp.float32)

    def gridding(group, side):
        first = group * GROUP
        bcast, rolled, wave_rows = bcast_all.at[side], rolled_all.at[side], rows_all.at[side]
        shift = lax.rem(128 - (chunk_start + first), 128)
        for place in range(16):
            rolled[place] = pltpu.roll(coef_ref[place], shift, 1)
        cells = uv_ref[pl.ds(pl.multiple_of(section * (2 * half) + 2 * (chunk_start + first), 8), 8), :]
        wave_rows[0:8], wave_rows[8:16] = sincos_turns(cells * (8.0 / SIDE))
        wave_rows[16:24], wave_rows[24:32] = sincos_step(cells * (8.0 / (64.0 * SIDE)))
        sums = cells + pltpu.roll(cells, 7, 0)
        wave_rows[32:40], wave_rows[40:48] = sincos_step(sums * (8.0 / (128.0 * SIDE)))
        wave_rows[48:56] = cells
        for g in range(GROUP):
            corr = [None, None]
            for row in range(2):
                for kind in range(2):
                    column = (row ^ section) ^ kind
                    source = own_ref if row == 0 else peer_ref
                    at = first + g + (chunk_start if row == 0 else 0)
                    vis_real = source[at, column, 0]
                    vis_imag = source[at, column, 1]
                    for pol in range(2):
                        place = kind * 8 + (pol ^ section) * 4 + (row ^ section) * 2
                        cr = jnp.broadcast_to(rolled[place][:, g : g + 1], (16, 128))
                        ci = jnp.broadcast_to(rolled[place + 1][:, g : g + 1], (16, 128))
                        real = cr * vis_real - ci * vis_imag
                        imag = cr * vis_imag + ci * vis_real
                        if corr[pol] is None:
                            corr[pol] = [real, imag]
                        else:
                            corr[pol] = [corr[pol][0] + real, corr[pol][1] + imag]
            u_row = spread(wave_rows, 48 + 2 * g)
            v_row = spread(wave_rows, 49 + 2 * g)
            turn_sin, turn_cos = sincos_half((u_row + v_row) * ((1.0 + sub_lane / 64.0) / (2.0 * SIDE)))
            step_sin, step_cos = spread(wave_rows, 32 + 2 * g), spread(wave_rows, 40 + 2 * g)
            turn_sin, turn_cos = (
                jnp.concatenate([turn_sin, turn_sin * step_cos + turn_cos * step_sin], 0),
                jnp.concatenate([turn_cos, turn_cos * step_cos - turn_sin * step_sin], 0),
            )
            for pol in range(2):
                real, imag = corr[pol]
                bcast[g, pol * 16 : pol * 16 + 16] = real * turn_cos + imag * turn_sin
                bcast[g, 32 + pol * 16 : 48 + pol * 16] = imag * turn_cos - real * turn_sin
            yield

            waves = []
            for axis, cell in enumerate((u_row, v_row)):
                turns = cell * ((sub_lane + 0.5) / SIDE)
                sin_0, cos_0 = sincos_turns(turns)
                sin_d, cos_d = sincos_step(turns * (1.0 / 64.0))
                place = 2 * g + axis
                up_sin, up_cos = spread(wave_rows, place), spread(wave_rows, 8 + place)
                upd_sin, upd_cos = spread(wave_rows, 16 + place), spread(wave_rows, 24 + place)
                cos_0, sin_0, cos_d, sin_d = (
                    jnp.stack([cos_0, cos_0 * up_cos - sin_0 * up_sin]),
                    jnp.stack([sin_0, sin_0 * up_cos + cos_0 * up_sin]),
                    jnp.stack([cos_d, cos_d * upd_cos - sin_d * upd_sin]),
                    jnp.stack([sin_d, sin_d * upd_cos + cos_d * upd_sin]),
                )
                cos_1 = cos_0 * cos_d - sin_0 * sin_d
                sin_1 = sin_0 * cos_d + cos_0 * sin_d
                waves.append([cos_0, sin_0, cos_1, sin_1, cos_d + cos_d])
            yield
            total = None
            for pair in range(8):
                left_parts, right_parts = [], []
                for c in (2 * pair, 2 * pair + 1):
                    cos_u, sin_u = waves[0][0], waves[0][1]
                    cos_v, sin_v = waves[1][0], waves[1][1]
                    left_parts.append(jnp.concatenate([cos_u, sin_u], 0).reshape(32, 128))
                    pieces = []
                    for k in range(4):
                        line = spread(bcast.at[g], 16 * k + c)[None]
                        pieces.append((cos_v * line).reshape(16, 128))
                        pieces.append((sin_v * line).reshape(16, 128))
                    right_parts.append(jnp.concatenate(pieces, 0))
                    for wave in waves:
                        cos_0, sin_0, cos_1, sin_1, twice = wave
                        wave[0], wave[1] = cos_1, sin_1
                        if c < 14:
                            wave[2], wave[3] = twice * cos_1 - cos_0, twice * sin_1 - sin_0
                part = lax.dot_general(
                    jnp.concatenate(left_parts, 1).astype(jnp.bfloat16),
                    jnp.concatenate(right_parts, 1).astype(jnp.bfloat16),
                    (((1,), (1,)), ((), ())),
                    preferred_element_type=jnp.float32,
                )
                total = part if total is None else total + part
                yield
            totals[side, g] = total

    def fields_of(group, side, fields):
        first = group * GROUP
        lane16 = lax.broadcasted_iota(jnp.int32, (16, 128), 1)
        upper = (lane16 & 16) == 16
        sign = jnp.where(upper, -1.0, 1.0)
        low_half, odd_quarter = lane16 < 64, (lane16 & 32) == 32
        w_first = section * half + chunk_start + first
        w_row = jnp.where(
            lane < 64,
            jnp.where(lane < 32, w_ref[w_first], w_ref[w_first + 1]),
            jnp.where(lane < 96, w_ref[w_first + 2], w_ref[w_first + 3]),
        )
        w_row = jnp.concatenate([w_row, w_row], 0)
        turned = []
        for k in range(2):
            rows = slice(k * 16, k * 16 + 16)
            w_sin, w_cos = sincos_turns(pixel_ref[0, rows] * w_row)
            turned.append((w_sin * pixel_ref[1, rows], w_cos * pixel_ref[1, rows]))
            yield
        parts = []
        for k in range(2):
            sums = swap_groups(
                [finished[side, g, k * 16 : k * 16 + 16] for g in range(GROUP)], low_half, odd_quarter
            )
            yield
            for value in sums:
                parts.append(
                    (
                        jnp.where(upper, pltpu.roll(value, 16, 1), value),
                        sign * jnp.where(upper, value, pltpu.roll(value, 112, 1)),
                    )
                )
                yield
        for pol in range(2):
            xa, xb, ya, yb = parts[pol], parts[2 + pol], parts[4 + pol], parts[6 + pol]
            even_re, even_im = xa[0] - xb[1], xb[0] + xa[1]
            odd_re, odd_im = yb[0] + ya[1], ya[0] - yb[1]
            for k in range(2):
                w_sin, w_cos = turned[k]
                image_re = even_re - odd_re if k == 0 else even_re + odd_re
                image_im = even_im + odd_im if k == 0 else even_im - odd_im
                fields.append(
                    jnp.concatenate(
                        [image_re * w_cos - image_im * w_sin, image_re * w_sin + image_im * w_cos], 1
                    )
                )
                yield

    def imaging(pair):
        finished[...] = totals[...]
        fields = [], []
        second = fields_of(2 * pair + 1, 1, fields[1])
        for _ in fields_of(2 * pair, 0, fields[0]):
            next(second)
            yield
        run(second)
        pieces = [split_hi_lo(field) for field in fields[0] + fields[1]]
        yield
        high = jnp.concatenate([piece[0] for piece in pieces], 0)
        low = jnp.concatenate([piece[1] for piece in pieces], 0)
        count = high.shape[0]
        both = jnp.dot(jnp.concatenate([high, low], 0), right_ref[0:256, :], preferred_element_type=jnp.float32)
        rows = jnp.dot(high, right_ref[256:512, :], preferred_element_type=jnp.float32)
        yield
        rows = rows + (both[:count] + both[count:])
        for index in range(4):
            side, pol = index // 2, index % 2
            first = (2 * pair + side) * GROUP
            out_ref = (mine_ref, other_ref)[pol]
            high, low = split_hi_lo(rows[index * 32 : index * 32 + 32])
            stack = jnp.concatenate(
                [high[:, :128], high[:, 128:], low[:, :128], low[:, 128:], high[:, :128], high[:, 128:]], 0
            )
            yield
            uv = jnp.dot(left_ref[...], stack, preferred_element_type=jnp.float32)
            yield
            for part in range(2):
                outs = swap_groups(
                    [uv[part * 32 + k * 8 : part * 32 + k * 8 + 8] for k in range(4)], lane < 64, (lane & 32) == 32
                )
                for g in range(GROUP):
                    out_ref[first + g, part * 8 : part * 8 + 8, :] = outs[g]
                yield

    def run(work):
        for _ in work:
            pass

    pairs = groups // 2
    run(gridding(0, 0))
    run(gridding(1, 1))
    if placing:
        owner_copy.wait()
        each = -(-tile_ref.shape[0] // (pairs - 1))

    def both(pair, carry):
        if placing:
            place_items((pair - 1) * each, each, tile_ref, owner_ref, row_ref, slot_ref)
        work = imaging(pair - 1)
        next(work)
        for step, _ in enumerate(gridding(2 * pair, 0)):
            if step % 2 == 0:
                next(work, None)
        for step, _ in enumerate(gridding(2 * pair + 1, 1)):
            if step % 2 == 0:
                next(work, None)
        run(work)
        return carry

    lax.fori_loop(1, pairs, both, 0)
    run(imaging(pairs - 1))


def pack_kernel(section_ref, row_ref, slot_ref, *refs):
    packed = refs[-1]
    section = section_ref[0]
    half = row_ref.shape[0] // 2
    width = packed.shape[0] // (slot_ref.shape[0] // 2)
    packed[...] = jnp.zeros_like(packed)
    lane = lax.broadcasted_iota(jnp.int32, (1, 128), 1)

    def note(step, carry):
        for k in range(2):
            target = step * 2 + k
            slots = jnp.where(lane == 0, slot_ref[2 * target], slot_ref[2 * target + 1])
            packed[pl.ds(target * width + width - 1, 1), :] = slots.astype(jnp.float32)
        return carry

    lax.fori_loop(0, slot_ref.shape[0] // 4, note, 0)
    start = section * half
    for values in refs[: len(CHUNKS)]:
        add_rows(row_ref, start, width, values, packed)
        start = start + values.shape[0]
    start = (1 - section) * half
    for values in refs[len(CHUNKS) : -1]:
        add_rows(row_ref, start, width, values, packed)
        start = start + values.shape[0]


def pack_more_kernel(section_ref, row_ref, before_ref, values, packed):
    half = row_ref.shape[0] // 2
    packed[...] = before_ref[...]
    add_rows(row_ref, (2 - section_ref[0]) * half - values.shape[0], 33, values, packed)


def add_rows(row_ref, start, width, values, packed):
    def add(step, carry):
        for k in range(4):
            item = step * 4 + k
            row = row_ref[start + item]
            top = (row >> 1) * width + (row & 1) * 16
            packed[pl.ds(top, 16), :] = packed[pl.ds(top, 16), :] + values[item]
        return carry

    lax.fori_loop(0, values.shape[0] // 4, add, 0)


def unpack_kernel(received_ref, out_ref, picked_ref):
    tiles_dev, width = out_ref.shape
    sources = received_ref.shape[0] // 33
    block = pl.program_id(0)

    @pl.when(block == 0)
    def _():
        slots = received_ref[pl.ds(32, sources, stride=33), :].T
        row = jnp.concatenate([slots[0:1, :], slots[1:2, :]], 1)
        tile = lax.broadcasted_iota(jnp.int32, (tiles_dev, 2 * sources), 0).astype(jnp.float32)
        picked = jnp.where(tile == row, 1.0, 0.0).astype(jnp.bfloat16)
        picked_ref[...] = jnp.concatenate([picked, picked], 1)

    for pair in range(width // 256):
        columns = []
        for k in (2 * pair, 2 * pair + 1):
            column = block * (width // 128) + k
            values = jnp.concatenate(
                [received_ref[pl.ds(16 * rank + column, sources, stride=33), :] for rank in range(2)], 0
            )
            columns.append(jnp.concatenate(split_hi_lo(values), 0))
        out_ref[:, pair * 256 : (pair + 1) * 256] = jnp.dot(
            picked_ref[...], jnp.concatenate(columns, 1), preferred_element_type=jnp.float32
        )


SMEM = pl.BlockSpec(memory_space=pltpu.SMEM)
VMEM = pl.BlockSpec(memory_space=pltpu.VMEM)
HBM = pl.BlockSpec(memory_space=pltpu.HBM)


def call(kernel, name, out_shape, in_specs, out_specs, scratch=(), flops=1_000_000, moved=1_000_000, mib=8, flags=None):
    return pl.pallas_call(
        kernel,
        out_shape=out_shape,
        in_specs=in_specs,
        out_specs=out_specs,
        scratch_shapes=list(scratch),
        compiler_params=pltpu.CompilerParams(vmem_limit_bytes=mib * 1024 * 1024, flags=flags),
        cost_estimate=pl.CostEstimate(flops=flops, bytes_accessed=moved, transcendentals=0),
        name=name,
    )


def shards(visibilities, uv_coords, w_terms, stations, tile_ids, owner_map, jones_gains):
    sub_count = visibilities.shape[1]
    samples = visibilities.shape[4] * visibilities.shape[5]
    half = sub_count // 2
    grid_size = lax.axis_size("grid")
    tiles_dev = owner_map.shape[0] // grid_size
    section_index = lax.axis_index("section").astype(jnp.int32)
    section = section_index.reshape(1)
    swap = [(0, 1), (1, 0)]
    shape_f32 = lambda *shape: jax.ShapeDtypeStruct(shape, jnp.float32)
    shape_i32 = lambda *shape: jax.ShapeDtypeStruct(shape, jnp.int32)

    peers, start = [], 0
    for size in CHUNKS:
        part = lax.dynamic_slice_in_dim(visibilities[0], (1 - section_index) * half + start, size, 0)
        peers.append(lax.ppermute(part, "section", swap))
        start += size
    own = lax.dynamic_slice_in_dim(visibilities[0], section_index * half, half, 0)
    coefs = call(
        prep_kernel,
        "prep",
        shape_f32(16, 16, 128),
        [SMEM, SMEM, VMEM],
        VMEM,
        [pltpu.VMEM((128, 128), jnp.float32)] * 3,
    )(section, stations, jones_gains)

    constants = [jnp.asarray(table) for table in tables(samples)]
    uv_rows = uv_coords.reshape(2 * sub_count, uv_coords.shape[2])
    mine, theirs, start = [], [], 0
    for chunk, size in enumerate(CHUNKS):
        placing = chunk == len(CHUNKS) - 1
        results = call(
            lambda *refs, start=start, placing=placing: grid_kernel(start, placing, *refs),
            "grid_chunk",
            (shape_f32(size, 16, 128),) * 2 + ((shape_i32(sub_count), shape_i32(2 * grid_size)) if placing else ()),
            [SMEM, SMEM] + [VMEM] * 7 + ([SMEM, HBM] if placing else []),
            (VMEM, VMEM) + ((SMEM, SMEM) if placing else ()),
            [
                pltpu.VMEM((2, GROUP, 64, 128), jnp.float32),
                pltpu.VMEM((2, 16, 16, 128), jnp.float32),
                pltpu.VMEM((2, 56, 128), jnp.float32),
                pltpu.VMEM((2, GROUP, 32, 128), jnp.float32),
                pltpu.VMEM((2, GROUP, 32, 128), jnp.float32),
            ]
            + ([pltpu.SMEM(owner_map.shape, jnp.int32), pltpu.SemaphoreType.DMA] if placing else []),
            flops=size * 300_000_000,
            moved=size * 100_000,
            mib=12,
        )(
            section, w_terms, coefs, own, peers[chunk], uv_rows, *constants,
            *((tile_ids, owner_map) if placing else ()),
        )
        mine.append(results[0])
        theirs.append(lax.ppermute(results[1], "section", swap))
        start += size
    row_index, slots = results[2:]

    packed_shape = shape_f32(33 * grid_size, 128)
    packed = call(
        pack_kernel, "pack", packed_shape, [SMEM] * 3 + [VMEM] * (2 * len(CHUNKS) - 1), VMEM, flops=100_000_000
    )(section, row_index, slots, *mine, *theirs[:-1])
    packed = call(pack_more_kernel, "pack_more", packed_shape, [SMEM] * 2 + [VMEM] * 2, VMEM)(
        section, row_index, packed, theirs[-1]
    )
    received = lax.all_to_all(
        packed.reshape(grid_size, 1, 33 * 128), "grid", split_axis=0, concat_axis=0, tiled=True
    ).reshape(33 * grid_size, 128)
    blocks = 4
    tiles = pl.pallas_call(
        unpack_kernel,
        out_shape=shape_f32(tiles_dev, 2048),
        grid=(blocks,),
        in_specs=[VMEM],
        out_specs=pl.BlockSpec((tiles_dev, 2048 // blocks), lambda i: (0, i)),
        scratch_shapes=[pltpu.VMEM((tiles_dev, 4 * grid_size), jnp.bfloat16)],
        compiler_params=pltpu.CompilerParams(vmem_limit_bytes=8 * 1024 * 1024),
        name="unpack",
    )(received)
    return tiles[None]


def solution(mesh):
    in_specs = (
        P("section", "grid", None, None, None, None),
        P("grid", None, None),
        P("grid"),
        P(None, "grid"),
        P("grid"),
        P(),
        P(),
    )
    out_specs = P("section", "grid", None)
    return jax.shard_map(shards, mesh=mesh, in_specs=in_specs, out_specs=out_specs, check_vma=False)
```

```python
import math

import numpy as np
import jax
import jax.numpy as jnp
from jax import lax
from jax.experimental import pallas as pl
from jax.experimental.pallas import tpu as pltpu
from jax.sharding import PartitionSpec as P

SIDE = 32
CHUNKS = (48,)
GROUP = 4

PIXELS = np.concatenate([np.arange(16), -1 - np.arange(16)]).astype(np.float64)


def fit_even(function, reach, terms):
    nodes = np.cos(np.pi * (np.arange(64) + 0.5) / 64)
    square = (nodes + 1.0) / 2.0 * reach * reach
    cheb = np.polynomial.chebyshev.chebfit(nodes, function(np.sqrt(square)), terms - 1)
    poly = np.polynomial.chebyshev.cheb2poly(cheb)
    shift = np.polynomial.polynomial.Polynomial(poly)(
        np.polynomial.polynomial.Polynomial([-1.0, 2.0 / (reach * reach)])
    )
    return [float(np.float32(value)) for value in shift.coef]


def sinc_turns(scale):
    return lambda x: np.where(x > 0, np.sin(scale * x) / np.maximum(x, 1e-30), scale)


HALF_SIN = fit_even(sinc_turns(np.pi), 0.5, 5)
HALF_COS = fit_even(lambda x: np.cos(np.pi * x), 0.5, 6)
STEP_SIN = fit_even(sinc_turns(2 * np.pi), 0.0625, 3)
STEP_COS = fit_even(lambda x: np.cos(2 * np.pi * x), 0.0625, 4)


def horner(coefs, square):
    total = square * coefs[-1] + coefs[-2]
    for value in coefs[-3::-1]:
        total = total * square + value
    return total


def sincos_half(x):
    square = x * x
    half_sin = x * horner(HALF_SIN, square)
    half_cos = horner(HALF_COS, square)
    twice = half_sin + half_sin
    return twice * half_cos, 1.0 - twice * half_sin


def sincos_turns(x):
    return sincos_half(x - jnp.round(x))


def sincos_step(x):
    square = x * x
    return x * horner(STEP_SIN, square), horner(STEP_COS, square)


def spread(ref, row):
    return ref[pl.ds(row, 8, stride=0), :]


def split_hi_lo(values):
    high = values.astype(jnp.bfloat16)
    low = (values - high.astype(jnp.float32)).astype(jnp.bfloat16)
    return high, low


def np_split(values):
    high = np.asarray(values, np.float32).astype(jnp.bfloat16)
    low = (np.asarray(values, np.float32) - high.astype(np.float32)).astype(jnp.bfloat16)
    return high, low


def tables(samples):
    row_p = PIXELS[:, None]
    lane_p = np.tile(PIXELS, GROUP)[None, :]
    sine_row, sine_lane = 0.6 * row_p / SIDE, 0.6 * lane_p / SIDE
    n_term = np.sqrt(1.0 - sine_row**2 - sine_lane**2) - 1.0
    taper = np.cos(np.pi * row_p / (SIDE + 4.0)) * np.cos(np.pi * lane_p / (SIDE + 4.0))
    pixel_tables = np.stack([n_term, taper / math.sqrt(samples) / SIDE]).astype(np.float32)

    freq = np.arange(SIDE) - SIDE // 2
    angle = 2.0 * np.pi / SIDE * PIXELS[:, None] * freq[None, :]
    cos_t = np.kron(np.eye(GROUP), np.cos(angle))
    sin_t = np.kron(np.eye(GROUP), np.sin(angle))
    high, low = np_split(np.block([[cos_t, -sin_t], [sin_t, cos_t]]))
    right_all = np.concatenate([high, low], 0)

    order = np.arange(SIDE).reshape(8, 4).T.reshape(-1)
    angle = 2.0 * np.pi / SIDE * freq[order][:, None] * PIXELS[None, :]
    high, low = np_split(np.block([[np.cos(angle), np.sin(angle)], [-np.sin(angle), np.cos(angle)]]))
    left_all = np.concatenate([high, high, low], 1)
    return pixel_tables, right_all, left_all


def swap_groups(parts, low_half, odd_quarter):
    a0 = jnp.where(low_half, parts[0], pltpu.roll(parts[2], 64, 1))
    a2 = jnp.where(low_half, pltpu.roll(parts[0], 64, 1), parts[2])
    a1 = jnp.where(low_half, parts[1], pltpu.roll(parts[3], 64, 1))
    a3 = jnp.where(low_half, pltpu.roll(parts[1], 64, 1), parts[3])
    return [
        jnp.where(odd_quarter, pltpu.roll(a1, 32, 1), a0),
        jnp.where(odd_quarter, a1, pltpu.roll(a0, 96, 1)),
        jnp.where(odd_quarter, pltpu.roll(a3, 32, 1), a2),
        jnp.where(odd_quarter, a3, pltpu.roll(a2, 96, 1)),
    ]


def prep_kernel(section_ref, stations_ref, jones_ref, coef_ref, p_rows, q_rows, turned):
    section = section_ref[0]
    half = stations_ref.shape[1] // 2

    p_rows[...] = jnp.zeros_like(p_rows)
    q_rows[...] = jnp.zeros_like(q_rows)

    def fetch(step, carry):
        for k in range(8):
            item = section * half + step * 8 + k
            p_rows[pl.ds(step * 8 + k, 1), :] = jones_ref[pl.ds(stations_ref[0, item], 1), :]
            q_rows[pl.ds(step * 8 + k, 1), :] = jones_ref[pl.ds(stations_ref[1, item], 1), :]
        return carry

    lax.fori_loop(0, half // 8, fetch, 0)
    lane = lax.broadcasted_iota(jnp.int32, (128, 128), 1)
    odd = (lane & 1) == 1
    high_pair = (lane & 2) == 2

    def swap_one(x):
        return jnp.where(odd, pltpu.roll(x, 1, 1), pltpu.roll(x, 127, 1))

    def swap_two(x):
        return jnp.where(high_pair, pltpu.roll(x, 2, 1), pltpu.roll(x, 126, 1))

    gain_p = p_rows[...]
    gain_p_turned = swap_one(gain_p)
    for kind in range(2):
        gain_q = q_rows[...] if kind == 0 else swap_two(q_rows[...])
        straight = gain_p * gain_q
        crossed = gain_p_turned * gain_q
        real = straight + swap_one(straight)
        imag = swap_one(crossed) - crossed
        turned[...] = jnp.where(odd, imag, real).T
        for place in range(8):
            coef_ref[kind * 8 + place] = turned[pl.ds(place, 16, stride=8), :]


def clear_slots(slot_ref):
    for target in range(slot_ref.shape[0]):
        slot_ref[target] = -1


def place_items(first, count, tile_ref, owner_ref, row_ref, slot_ref):
    tiles_dev = owner_ref.shape[0] // (slot_ref.shape[0] // 2)
    shift = tiles_dev.bit_length() - 1
    assert tiles_dev == 1 << shift
    for k in range(count):
        item = jnp.minimum(first + k, tile_ref.shape[0] - 1)
        position = owner_ref[tile_ref[item]]
        target = 2 * (position >> shift)
        slot = position & (tiles_dev - 1)
        known = slot_ref[target]
        row = target + jnp.where((known == -1) | (known == slot), 0, 1)
        slot_ref[row] = slot
        row_ref[item] = row


def grid_kernel(chunk_start, placing, section_ref, w_ref, coef_ref, own_ref, peer_ref, uv_ref, pixel_ref, right_ref,
                left_ref, *refs):
    if placing:
        tile_ref, owner_any, mine_ref, other_ref, row_ref, slot_ref = refs[:6]
        owner_ref, owner_sem = refs[-2:]
        owner_copy = pltpu.make_async_copy(owner_any, owner_ref, owner_sem)
        owner_copy.start()
        clear_slots(slot_ref)
    else:
        mine_ref, other_ref = refs[:2]
    start = 6 if placing else 2
    bcast_all, rolled_all, rows_all, totals, finished = refs[start : start + 5]
    section = section_ref[0]
    groups = mine_ref.shape[0] // GROUP
    half = w_ref.shape[0] // 2
    lane = lax.broadcasted_iota(jnp.int32, (8, 128), 1)
    sub_lane = lax.broadcasted_iota(jnp.int32, (8, 128), 0).astype(jnp.float32)

    def gridding(group, side):
        first = group * GROUP
        bcast, rolled, wave_rows = bcast_all.at[side], rolled_all.at[side], rows_all.at[side]
        shift = lax.rem(128 - (chunk_start + first), 128)
        for place in range(16):
            rolled[place] = pltpu.roll(coef_ref[place], shift, 1)
        cells = uv_ref[pl.ds(pl.multiple_of(section * (2 * half) + 2 * (chunk_start + first), 8), 8), :]
        wave_rows[0:8], wave_rows[8:16] = sincos_turns(cells * (8.0 / SIDE))
        wave_rows[16:24], wave_rows[24:32] = sincos_step(cells * (8.0 / (64.0 * SIDE)))
        sums = cells + pltpu.roll(cells, 7, 0)
        wave_rows[32:40], wave_rows[40:48] = sincos_step(sums * (8.0 / (128.0 * SIDE)))
        wave_rows[48:56] = cells
        for g in range(GROUP):
            corr = [None, None]
            for row in range(2):
                for kind in range(2):
                    column = (row ^ section) ^ kind
                    source = own_ref if row == 0 else peer_ref
                    at = first + g + (chunk_start if row == 0 else 0)
                    vis_real = source[at, column, 0]
                    vis_imag = source[at, column, 1]
                    for pol in range(2):
                        place = kind * 8 + (pol ^ section) * 4 + (row ^ section) * 2
                        cr = jnp.broadcast_to(rolled[place][:, g : g + 1], (16, 128))
                        ci = jnp.broadcast_to(rolled[place + 1][:, g : g + 1], (16, 128))
                        real = cr * vis_real - ci * vis_imag
                        imag = cr * vis_imag + ci * vis_real
                        if corr[pol] is None:
                            corr[pol] = [real, imag]
                        else:
                            corr[pol] = [corr[pol][0] + real, corr[pol][1] + imag]
            u_row = spread(wave_rows, 48 + 2 * g)
            v_row = spread(wave_rows, 49 + 2 * g)
            turn_sin, turn_cos = sincos_half((u_row + v_row) * ((1.0 + sub_lane / 64.0) / (2.0 * SIDE)))
            step_sin, step_cos = spread(wave_rows, 32 + 2 * g), spread(wave_rows, 40 + 2 * g)
            turn_sin, turn_cos = (
                jnp.concatenate([turn_sin, turn_sin * step_cos + turn_cos * step_sin], 0),
                jnp.concatenate([turn_cos, turn_cos * step_cos - turn_sin * step_sin], 0),
            )
            for pol in range(2):
                real, imag = corr[pol]
                bcast[g, pol * 16 : pol * 16 + 16] = real * turn_cos + imag * turn_sin
                bcast[g, 32 + pol * 16 : 48 + pol * 16] = imag * turn_cos - real * turn_sin
            yield

            waves = []
            for axis, cell in enumerate((u_row, v_row)):
                turns = cell * ((sub_lane + 0.5) / SIDE)
                sin_0, cos_0 = sincos_turns(turns)
                sin_d, cos_d = sincos_step(turns * (1.0 / 64.0))
                place = 2 * g + axis
                up_sin, up_cos = spread(wave_rows, place), spread(wave_rows, 8 + place)
                upd_sin, upd_cos = spread(wave_rows, 16 + place), spread(wave_rows, 24 + place)
                cos_0, sin_0, cos_d, sin_d = (
                    jnp.stack([cos_0, cos_0 * up_cos - sin_0 * up_sin]),
                    jnp.stack([sin_0, sin_0 * up_cos + cos_0 * up_sin]),
                    jnp.stack([cos_d, cos_d * upd_cos - sin_d * upd_sin]),
                    jnp.stack([sin_d, sin_d * upd_cos + cos_d * upd_sin]),
                )
                cos_1 = cos_0 * cos_d - sin_0 * sin_d
                sin_1 = sin_0 * cos_d + cos_0 * sin_d
                waves.append([cos_0, sin_0, cos_1, sin_1, cos_d + cos_d])
            yield
            total = None
            for pair in range(8):
                left_parts, right_parts = [], []
                for c in (2 * pair, 2 * pair + 1):
                    cos_u, sin_u = waves[0][0], waves[0][1]
                    cos_v, sin_v = waves[1][0], waves[1][1]
                    left_parts.append(jnp.concatenate([cos_u, sin_u], 0).reshape(32, 128))
                    pieces = []
                    for k in range(4):
                        line = spread(bcast.at[g], 16 * k + c)[None]
                        pieces.append((cos_v * line).reshape(16, 128))
                        pieces.append((sin_v * line).reshape(16, 128))
                    right_parts.append(jnp.concatenate(pieces, 0))
                    for wave in waves:
                        cos_0, sin_0, cos_1, sin_1, twice = wave
                        wave[0], wave[1] = cos_1, sin_1
                        if c < 14:
                            wave[2], wave[3] = twice * cos_1 - cos_0, twice * sin_1 - sin_0
                part = lax.dot_general(
                    jnp.concatenate(left_parts, 1).astype(jnp.bfloat16),
                    jnp.concatenate(right_parts, 1).astype(jnp.bfloat16),
                    (((1,), (1,)), ((), ())),
                    preferred_element_type=jnp.float32,
                )
                total = part if total is None else total + part
                yield
            totals[side, g] = total

    def fields_of(group, side, fields):
        first = group * GROUP
        lane16 = lax.broadcasted_iota(jnp.int32, (16, 128), 1)
        upper = (lane16 & 16) == 16
        sign = jnp.where(upper, -1.0, 1.0)
        low_half, odd_quarter = lane16 < 64, (lane16 & 32) == 32
        w_first = section * half + chunk_start + first
        w_row = jnp.where(
            lane < 64,
            jnp.where(lane < 32, w_ref[w_first], w_ref[w_first + 1]),
            jnp.where(lane < 96, w_ref[w_first + 2], w_ref[w_first + 3]),
        )
        w_row = jnp.concatenate([w_row, w_row], 0)
        turned = []
        for k in range(2):
            rows = slice(k * 16, k * 16 + 16)
            w_sin, w_cos = sincos_turns(pixel_ref[0, rows] * w_row)
            turned.append((w_sin * pixel_ref[1, rows], w_cos * pixel_ref[1, rows]))
            yield
        parts = []
        for k in range(2):
            sums = swap_groups(
                [finished[side, g, k * 16 : k * 16 + 16] for g in range(GROUP)], low_half, odd_quarter
            )
            yield
            for value in sums:
                parts.append(
                    (
                        jnp.where(upper, pltpu.roll(value, 16, 1), value),
                        sign * jnp.where(upper, value, pltpu.roll(value, 112, 1)),
                    )
                )
                yield
        for pol in range(2):
            xa, xb, ya, yb = parts[pol], parts[2 + pol], parts[4 + pol], parts[6 + pol]
            even_re, even_im = xa[0] - xb[1], xb[0] + xa[1]
            odd_re, odd_im = yb[0] + ya[1], ya[0] - yb[1]
            for k in range(2):
                w_sin, w_cos = turned[k]
                image_re = even_re - odd_re if k == 0 else even_re + odd_re
                image_im = even_im + odd_im if k == 0 else even_im - odd_im
                fields.append(
                    jnp.concatenate(
                        [image_re * w_cos - image_im * w_sin, image_re * w_sin + image_im * w_cos], 1
                    )
                )
                yield

    def imaging(pair):
        finished[...] = totals[...]
        fields = [], []
        second = fields_of(2 * pair + 1, 1, fields[1])
        for _ in fields_of(2 * pair, 0, fields[0]):
            next(second)
            yield
        run(second)
        pieces = [split_hi_lo(field) for field in fields[0] + fields[1]]
        yield
        high = jnp.concatenate([piece[0] for piece in pieces], 0)
        low = jnp.concatenate([piece[1] for piece in pieces], 0)
        count = high.shape[0]
        both = jnp.dot(jnp.concatenate([high, low], 0), right_ref[0:256, :], preferred_element_type=jnp.float32)
        rows = jnp.dot(high, right_ref[256:512, :], preferred_element_type=jnp.float32)
        yield
        rows = rows + (both[:count] + both[count:])
        for index in range(4):
            side, pol = index // 2, index % 2
            first = (2 * pair + side) * GROUP
            out_ref = (mine_ref, other_ref)[pol]
            high, low = split_hi_lo(rows[index * 32 : index * 32 + 32])
            stack = jnp.concatenate(
                [high[:, :128], high[:, 128:], low[:, :128], low[:, 128:], high[:, :128], high[:, 128:]], 0
            )
            yield
            uv = jnp.dot(left_ref[...], stack, preferred_element_type=jnp.float32)
            yield
            for part in range(2):
                outs = swap_groups(
                    [uv[part * 32 + k * 8 : part * 32 + k * 8 + 8] for k in range(4)], lane < 64, (lane & 32) == 32
                )
                for g in range(GROUP):
                    out_ref[first + g, part * 8 : part * 8 + 8, :] = outs[g]
                yield

    def run(work):
        for _ in work:
            pass

    pairs = groups // 2
    run(gridding(0, 0))
    run(gridding(1, 1))
    if placing:
        owner_copy.wait()
        each = -(-tile_ref.shape[0] // (pairs - 1))

    def both(pair, carry):
        if placing:
            place_items((pair - 1) * each, each, tile_ref, owner_ref, row_ref, slot_ref)
        work = imaging(pair - 1)
        next(work)
        for step, _ in enumerate(gridding(2 * pair, 0)):
            if step % 2 == 0:
                next(work, None)
        for step, _ in enumerate(gridding(2 * pair + 1, 1)):
            if step % 2 == 0:
                next(work, None)
        run(work)
        return carry

    lax.fori_loop(1, pairs, both, 0)
    run(imaging(pairs - 1))


def pack_kernel(section_ref, row_ref, slot_ref, *refs):
    packed = refs[-1]
    section = section_ref[0]
    half = row_ref.shape[0] // 2
    width = packed.shape[0] // (slot_ref.shape[0] // 2)
    packed[...] = jnp.zeros_like(packed)
    lane = lax.broadcasted_iota(jnp.int32, (1, 128), 1)

    def note(step, carry):
        for k in range(2):
            target = step * 2 + k
            slots = jnp.where(lane == 0, slot_ref[2 * target], slot_ref[2 * target + 1])
            packed[pl.ds(target * width + width - 1, 1), :] = slots.astype(jnp.float32)
        return carry

    lax.fori_loop(0, slot_ref.shape[0] // 4, note, 0)
    start = section * half
    for values in refs[: len(CHUNKS)]:
        add_rows(row_ref, start, width, values, packed)
        start = start + values.shape[0]
    start = (1 - section) * half
    for values in refs[len(CHUNKS) : -1]:
        add_rows(row_ref, start, width, values, packed)
        start = start + values.shape[0]


def pack_more_kernel(section_ref, row_ref, before_ref, values, packed):
    half = row_ref.shape[0] // 2
    packed[...] = before_ref[...]
    add_rows(row_ref, (2 - section_ref[0]) * half - values.shape[0], 33, values, packed)


def add_rows(row_ref, start, width, values, packed):
    def add(step, carry):
        for k in range(16):
            item = step * 16 + k
            row = row_ref[start + item]
            top = (row >> 1) * width + (row & 1) * 16
            packed[pl.ds(top, 16), :] = packed[pl.ds(top, 16), :] + values[item]
        return carry

    lax.fori_loop(0, values.shape[0] // 16, add, 0)


def unpack_kernel(received_ref, out_ref):
    tiles_dev = out_ref.shape[0]
    sources = received_ref.shape[0] // 33
    slots = received_ref[pl.ds(32, sources, stride=33), :].T
    row = jnp.concatenate([slots[0:1, :], slots[1:2, :]], 1)
    tile = lax.broadcasted_iota(jnp.int32, (tiles_dev, 2 * sources), 0).astype(jnp.float32)
    picked = jnp.where(tile == row, 1.0, 0.0).astype(jnp.bfloat16)
    picked = jnp.concatenate([picked, picked], 1)
    for pair in range(8):
        columns = []
        for column in (2 * pair, 2 * pair + 1):
            values = jnp.concatenate(
                [received_ref[pl.ds(16 * rank + column, sources, stride=33), :] for rank in range(2)], 0
            )
            columns.append(jnp.concatenate(split_hi_lo(values), 0))
        out_ref[:, pair * 256 : (pair + 1) * 256] = jnp.dot(
            picked, jnp.concatenate(columns, 1), preferred_element_type=jnp.float32
        )


SMEM = pl.BlockSpec(memory_space=pltpu.SMEM)
VMEM = pl.BlockSpec(memory_space=pltpu.VMEM)
HBM = pl.BlockSpec(memory_space=pltpu.HBM)


def call(kernel, name, out_shape, in_specs, out_specs, scratch=(), flops=1_000_000, moved=1_000_000, mib=8, flags=None):
    return pl.pallas_call(
        kernel,
        out_shape=out_shape,
        in_specs=in_specs,
        out_specs=out_specs,
        scratch_shapes=list(scratch),
        compiler_params=pltpu.CompilerParams(vmem_limit_bytes=mib * 1024 * 1024, flags=flags),
        cost_estimate=pl.CostEstimate(flops=flops, bytes_accessed=moved, transcendentals=0),
        name=name,
    )


def shards(visibilities, uv_coords, w_terms, stations, tile_ids, owner_map, jones_gains):
    sub_count = visibilities.shape[1]
    samples = visibilities.shape[4] * visibilities.shape[5]
    half = sub_count // 2
    grid_size = lax.axis_size("grid")
    tiles_dev = owner_map.shape[0] // grid_size
    section_index = lax.axis_index("section").astype(jnp.int32)
    section = section_index.reshape(1)
    swap = [(0, 1), (1, 0)]
    shape_f32 = lambda *shape: jax.ShapeDtypeStruct(shape, jnp.float32)
    shape_i32 = lambda *shape: jax.ShapeDtypeStruct(shape, jnp.int32)

    peers, start = [], 0
    for size in CHUNKS:
        part = lax.dynamic_slice_in_dim(visibilities[0], (1 - section_index) * half + start, size, 0)
        peers.append(lax.ppermute(part, "section", swap))
        start += size
    own = lax.dynamic_slice_in_dim(visibilities[0], section_index * half, half, 0)
    coefs = call(
        prep_kernel,
        "prep",
        shape_f32(16, 16, 128),
        [SMEM, SMEM, VMEM],
        VMEM,
        [pltpu.VMEM((128, 128), jnp.float32)] * 3,
    )(section, stations, jones_gains)

    constants = [jnp.asarray(table) for table in tables(samples)]
    uv_rows = uv_coords.reshape(2 * sub_count, uv_coords.shape[2])
    mine, theirs, start = [], [], 0
    for chunk, size in enumerate(CHUNKS):
        placing = chunk == len(CHUNKS) - 1
        results = call(
            lambda *refs, start=start, placing=placing: grid_kernel(start, placing, *refs),
            "grid_chunk",
            (shape_f32(size, 16, 128),) * 2 + ((shape_i32(sub_count), shape_i32(2 * grid_size)) if placing else ()),
            [SMEM, SMEM] + [VMEM] * 7 + ([SMEM, HBM] if placing else []),
            (VMEM, VMEM) + ((SMEM, SMEM) if placing else ()),
            [
                pltpu.VMEM((2, GROUP, 64, 128), jnp.float32),
                pltpu.VMEM((2, 16, 16, 128), jnp.float32),
                pltpu.VMEM((2, 56, 128), jnp.float32),
                pltpu.VMEM((2, GROUP, 32, 128), jnp.float32),
                pltpu.VMEM((2, GROUP, 32, 128), jnp.float32),
            ]
            + ([pltpu.SMEM(owner_map.shape, jnp.int32), pltpu.SemaphoreType.DMA] if placing else []),
            flops=size * 300_000_000,
            moved=size * 100_000,
            mib=12,
        )(
            section, w_terms, coefs, own, peers[chunk], uv_rows, *constants,
            *((tile_ids, owner_map) if placing else ()),
        )
        mine.append(results[0])
        theirs.append(lax.ppermute(results[1], "section", swap))
        start += size
    row_index, slots = results[2:]

    packed_shape = shape_f32(33 * grid_size, 128)
    packed = call(
        pack_kernel, "pack", packed_shape, [SMEM] * 3 + [VMEM] * (2 * len(CHUNKS) - 1), VMEM, flops=100_000_000
    )(section, row_index, slots, *mine, *theirs[:-1])
    packed = call(pack_more_kernel, "pack_more", packed_shape, [SMEM] * 2 + [VMEM] * 2, VMEM)(
        section, row_index, packed, theirs[-1]
    )
    received = lax.all_to_all(
        packed.reshape(grid_size, 1, 33 * 128), "grid", split_axis=0, concat_axis=0, tiled=True
    ).reshape(33 * grid_size, 128)
    tiles = call(unpack_kernel, "unpack", shape_f32(tiles_dev, 2048), [VMEM], VMEM)(received)
    return tiles[None]


def solution(mesh):
    in_specs = (
        P("section", "grid", None, None, None, None),
        P("grid", None, None),
        P("grid"),
        P(None, "grid"),
        P("grid"),
        P(),
        P(),
    )
    out_specs = P("section", "grid", None)
    return jax.shard_map(shards, mesh=mesh, in_specs=in_specs, out_specs=out_specs, check_vma=False)
```

```python
import math

import numpy as np
import jax
import jax.numpy as jnp
from jax import lax
from jax.experimental import pallas as pl
from jax.experimental.pallas import tpu as pltpu
from jax.sharding import PartitionSpec as P


SIDE = 32
CHUNKS = (16, 32)
GROUP = 4

PIXELS = np.concatenate([np.arange(16), -1 - np.arange(16)]).astype(np.float64)


def fit_even(function, reach, terms):
    nodes = np.cos(np.pi * (np.arange(64) + 0.5) / 64)
    square = (nodes + 1.0) / 2.0 * reach * reach
    cheb = np.polynomial.chebyshev.chebfit(nodes, function(np.sqrt(square)), terms - 1)
    poly = np.polynomial.chebyshev.cheb2poly(cheb)
    shift = np.polynomial.polynomial.Polynomial(poly)(
        np.polynomial.polynomial.Polynomial([-1.0, 2.0 / (reach * reach)])
    )
    return [float(np.float32(value)) for value in shift.coef]


def sinc_turns(scale):
    return lambda x: np.where(x > 0, np.sin(scale * x) / np.maximum(x, 1e-30), scale)


HALF_SIN = fit_even(sinc_turns(np.pi), 0.5, 5)
HALF_COS = fit_even(lambda x: np.cos(np.pi * x), 0.5, 6)
STEP_SIN = fit_even(sinc_turns(2 * np.pi), 0.0625, 3)
STEP_COS = fit_even(lambda x: np.cos(2 * np.pi * x), 0.0625, 4)


def horner(coefs, square):
    total = square * coefs[-1] + coefs[-2]
    for value in coefs[-3::-1]:
        total = total * square + value
    return total


def sincos_half(x):
    square = x * x
    half_sin = x * horner(HALF_SIN, square)
    half_cos = horner(HALF_COS, square)
    twice = half_sin + half_sin
    return twice * half_cos, 1.0 - twice * half_sin


def sincos_turns(x):
    return sincos_half(x - jnp.round(x))


def sincos_step(x):
    square = x * x
    return x * horner(STEP_SIN, square), horner(STEP_COS, square)


def spread(ref, row):
    return ref[pl.ds(row, 8, stride=0), :]


def split_hi_lo(values):
    high = values.astype(jnp.bfloat16)
    low = (values - high.astype(jnp.float32)).astype(jnp.bfloat16)
    return high, low


def np_split(values):
    high = np.asarray(values, np.float32).astype(jnp.bfloat16)
    low = (np.asarray(values, np.float32) - high.astype(np.float32)).astype(jnp.bfloat16)
    return high, low


def tables(samples):
    row_p = PIXELS[:, None]
    lane_p = np.tile(PIXELS, GROUP)[None, :]
    sine_row, sine_lane = 0.6 * row_p / SIDE, 0.6 * lane_p / SIDE
    n_term = np.sqrt(1.0 - sine_row**2 - sine_lane**2) - 1.0
    taper = np.cos(np.pi * row_p / (SIDE + 4.0)) * np.cos(np.pi * lane_p / (SIDE + 4.0))
    pixel_tables = np.stack([n_term, taper / math.sqrt(samples) / SIDE]).astype(np.float32)

    freq = np.arange(SIDE) - SIDE // 2
    angle = 2.0 * np.pi / SIDE * PIXELS[:, None] * freq[None, :]
    cos_t = np.kron(np.eye(GROUP), np.cos(angle))
    sin_t = np.kron(np.eye(GROUP), np.sin(angle))
    high, low = np_split(np.block([[cos_t, -sin_t], [sin_t, cos_t]]))
    right_all = np.concatenate([high, low], 0)

    order = np.arange(SIDE).reshape(8, 4).T.reshape(-1)
    angle = 2.0 * np.pi / SIDE * freq[order][:, None] * PIXELS[None, :]
    high, low = np_split(np.block([[np.cos(angle), np.sin(angle)], [-np.sin(angle), np.cos(angle)]]))
    left_all = np.concatenate([high, high, low], 1)
    return pixel_tables, right_all, left_all


def swap_groups(parts, low_half, odd_quarter):
    a0 = jnp.where(low_half, parts[0], pltpu.roll(parts[2], 64, 1))
    a2 = jnp.where(low_half, pltpu.roll(parts[0], 64, 1), parts[2])
    a1 = jnp.where(low_half, parts[1], pltpu.roll(parts[3], 64, 1))
    a3 = jnp.where(low_half, pltpu.roll(parts[1], 64, 1), parts[3])
    return [
        jnp.where(odd_quarter, pltpu.roll(a1, 32, 1), a0),
        jnp.where(odd_quarter, a1, pltpu.roll(a0, 96, 1)),
        jnp.where(odd_quarter, pltpu.roll(a3, 32, 1), a2),
        jnp.where(odd_quarter, a3, pltpu.roll(a2, 96, 1)),
    ]


def prep_kernel(section_ref, stations_ref, jones_ref, coef_ref, p_rows, q_rows, turned):
    section = section_ref[0]
    half = stations_ref.shape[1] // 2

    p_rows[...] = jnp.zeros_like(p_rows)
    q_rows[...] = jnp.zeros_like(q_rows)

    def fetch(step, carry):
        for k in range(8):
            item = section * half + step * 8 + k
            p_rows[pl.ds(step * 8 + k, 1), :] = jones_ref[pl.ds(stations_ref[0, item], 1), :]
            q_rows[pl.ds(step * 8 + k, 1), :] = jones_ref[pl.ds(stations_ref[1, item], 1), :]
        return carry

    lax.fori_loop(0, half // 8, fetch, 0)
    lane = lax.broadcasted_iota(jnp.int32, (128, 128), 1)
    odd = (lane & 1) == 1
    high_pair = (lane & 2) == 2

    def swap_one(x):
        return jnp.where(odd, pltpu.roll(x, 1, 1), pltpu.roll(x, 127, 1))

    def swap_two(x):
        return jnp.where(high_pair, pltpu.roll(x, 2, 1), pltpu.roll(x, 126, 1))

    gain_p = p_rows[...]
    gain_p_turned = swap_one(gain_p)
    for kind in range(2):
        gain_q = q_rows[...] if kind == 0 else swap_two(q_rows[...])
        straight = gain_p * gain_q
        crossed = gain_p_turned * gain_q
        real = straight + swap_one(straight)
        imag = swap_one(crossed) - crossed
        turned[...] = jnp.where(odd, imag, real).T
        for place in range(8):
            coef_ref[kind * 8 + place] = turned[pl.ds(place, 16, stride=8), :]


def clear_slots(slot_ref):
    for target in range(slot_ref.shape[0]):
        slot_ref[target] = -1


def place_items(first, count, tile_ref, owner_ref, row_ref, slot_ref):
    tiles_dev = owner_ref.shape[0] // (slot_ref.shape[0] // 2)
    shift = tiles_dev.bit_length() - 1
    assert tiles_dev == 1 << shift
    for k in range(count):
        item = jnp.minimum(first + k, tile_ref.shape[0] - 1)
        position = owner_ref[tile_ref[item]]
        target = 2 * (position >> shift)
        slot = position & (tiles_dev - 1)
        known = slot_ref[target]
        row = target + jnp.where((known == -1) | (known == slot), 0, 1)
        slot_ref[row] = slot
        row_ref[item] = row


def grid_kernel(chunk_start, placing, section_ref, w_ref, coef_ref, own_ref, peer_ref, uv_ref, pixel_ref, right_ref,
                left_ref, *refs):
    if placing:
        tile_ref, owner_any, mine_ref, other_ref, row_ref, slot_ref = refs[:6]
        owner_ref, owner_sem = refs[-2:]
        owner_copy = pltpu.make_async_copy(owner_any, owner_ref, owner_sem)
        owner_copy.start()
        clear_slots(slot_ref)
    else:
        mine_ref, other_ref = refs[:2]
    start = 6 if placing else 2
    bcast_all, rolled_all, rows_all, totals, finished = refs[start : start + 5]
    section = section_ref[0]
    groups = mine_ref.shape[0] // GROUP
    half = w_ref.shape[0] // 2
    lane = lax.broadcasted_iota(jnp.int32, (8, 128), 1)
    sub_lane = lax.broadcasted_iota(jnp.int32, (8, 128), 0).astype(jnp.float32)

    def gridding(group, side):
        first = group * GROUP
        bcast, rolled, wave_rows = bcast_all.at[side], rolled_all.at[side], rows_all.at[side]
        shift = lax.rem(128 - (chunk_start + first), 128)
        for place in range(16):
            rolled[place] = pltpu.roll(coef_ref[place], shift, 1)
        cells = uv_ref[pl.ds(pl.multiple_of(section * (2 * half) + 2 * (chunk_start + first), 8), 8), :]
        wave_rows[0:8], wave_rows[8:16] = sincos_turns(cells * (8.0 / SIDE))
        wave_rows[16:24], wave_rows[24:32] = sincos_step(cells * (8.0 / (64.0 * SIDE)))
        sums = cells + pltpu.roll(cells, 7, 0)
        wave_rows[32:40], wave_rows[40:48] = sincos_step(sums * (8.0 / (128.0 * SIDE)))
        wave_rows[48:56] = cells
        for g in range(GROUP):
            corr = [None, None]
            for row in range(2):
                for kind in range(2):
                    column = (row ^ section) ^ kind
                    source = own_ref if row == 0 else peer_ref
                    at = first + g + (chunk_start if row == 0 else 0)
                    vis_real = source[at, column, 0]
                    vis_imag = source[at, column, 1]
                    for pol in range(2):
                        place = kind * 8 + (pol ^ section) * 4 + (row ^ section) * 2
                        cr = jnp.broadcast_to(rolled[place][:, g : g + 1], (16, 128))
                        ci = jnp.broadcast_to(rolled[place + 1][:, g : g + 1], (16, 128))
                        real = cr * vis_real - ci * vis_imag
                        imag = cr * vis_imag + ci * vis_real
                        if corr[pol] is None:
                            corr[pol] = [real, imag]
                        else:
                            corr[pol] = [corr[pol][0] + real, corr[pol][1] + imag]
            u_row = spread(wave_rows, 48 + 2 * g)
            v_row = spread(wave_rows, 49 + 2 * g)
            turn_sin, turn_cos = sincos_half((u_row + v_row) * ((1.0 + sub_lane / 64.0) / (2.0 * SIDE)))
            step_sin, step_cos = spread(wave_rows, 32 + 2 * g), spread(wave_rows, 40 + 2 * g)
            turn_sin, turn_cos = (
                jnp.concatenate([turn_sin, turn_sin * step_cos + turn_cos * step_sin], 0),
                jnp.concatenate([turn_cos, turn_cos * step_cos - turn_sin * step_sin], 0),
            )
            for pol in range(2):
                real, imag = corr[pol]
                bcast[g, pol * 16 : pol * 16 + 16] = real * turn_cos + imag * turn_sin
                bcast[g, 32 + pol * 16 : 48 + pol * 16] = imag * turn_cos - real * turn_sin
            yield

            waves = []
            for axis, cell in enumerate((u_row, v_row)):
                turns = cell * ((sub_lane + 0.5) / SIDE)
                sin_0, cos_0 = sincos_turns(turns)
                sin_d, cos_d = sincos_step(turns * (1.0 / 64.0))
                place = 2 * g + axis
                up_sin, up_cos = spread(wave_rows, place), spread(wave_rows, 8 + place)
                upd_sin, upd_cos = spread(wave_rows, 16 + place), spread(wave_rows, 24 + place)
                cos_0, sin_0, cos_d, sin_d = (
                    jnp.stack([cos_0, cos_0 * up_cos - sin_0 * up_sin]),
                    jnp.stack([sin_0, sin_0 * up_cos + cos_0 * up_sin]),
                    jnp.stack([cos_d, cos_d * upd_cos - sin_d * upd_sin]),
                    jnp.stack([sin_d, sin_d * upd_cos + cos_d * upd_sin]),
                )
                cos_1 = cos_0 * cos_d - sin_0 * sin_d
                sin_1 = sin_0 * cos_d + cos_0 * sin_d
                waves.append([cos_0, sin_0, cos_1, sin_1, cos_d + cos_d])
            yield
            total = None
            for pair in range(8):
                left_parts, right_parts = [], []
                for c in (2 * pair, 2 * pair + 1):
                    cos_u, sin_u = waves[0][0], waves[0][1]
                    cos_v, sin_v = waves[1][0], waves[1][1]
                    left_parts.append(jnp.concatenate([cos_u, sin_u], 0).reshape(32, 128))
                    pieces = []
                    for k in range(4):
                        line = spread(bcast.at[g], 16 * k + c)[None]
                        pieces.append((cos_v * line).reshape(16, 128))
                        pieces.append((sin_v * line).reshape(16, 128))
                    right_parts.append(jnp.concatenate(pieces, 0))
                    for wave in waves:
                        cos_0, sin_0, cos_1, sin_1, twice = wave
                        wave[0], wave[1] = cos_1, sin_1
                        if c < 14:
                            wave[2], wave[3] = twice * cos_1 - cos_0, twice * sin_1 - sin_0
                part = lax.dot_general(
                    jnp.concatenate(left_parts, 1).astype(jnp.bfloat16),
                    jnp.concatenate(right_parts, 1).astype(jnp.bfloat16),
                    (((1,), (1,)), ((), ())),
                    preferred_element_type=jnp.float32,
                )
                total = part if total is None else total + part
                yield
            totals[side, g] = total

    def fields_of(group, side, fields):
        first = group * GROUP
        lane16 = lax.broadcasted_iota(jnp.int32, (16, 128), 1)
        upper = (lane16 & 16) == 16
        sign = jnp.where(upper, -1.0, 1.0)
        low_half, odd_quarter = lane16 < 64, (lane16 & 32) == 32
        w_first = section * half + chunk_start + first
        w_row = jnp.where(
            lane < 64,
            jnp.where(lane < 32, w_ref[w_first], w_ref[w_first + 1]),
            jnp.where(lane < 96, w_ref[w_first + 2], w_ref[w_first + 3]),
        )
        w_row = jnp.concatenate([w_row, w_row], 0)
        turned = []
        for k in range(2):
            rows = slice(k * 16, k * 16 + 16)
            w_sin, w_cos = sincos_turns(pixel_ref[0, rows] * w_row)
            turned.append((w_sin * pixel_ref[1, rows], w_cos * pixel_ref[1, rows]))
            yield
        parts = []
        for k in range(2):
            sums = swap_groups(
                [finished[side, g, k * 16 : k * 16 + 16] for g in range(GROUP)], low_half, odd_quarter
            )
            yield
            for value in sums:
                parts.append(
                    (
                        jnp.where(upper, pltpu.roll(value, 16, 1), value),
                        sign * jnp.where(upper, value, pltpu.roll(value, 112, 1)),
                    )
                )
                yield
        for pol in range(2):
            xa, xb, ya, yb = parts[pol], parts[2 + pol], parts[4 + pol], parts[6 + pol]
            even_re, even_im = xa[0] - xb[1], xb[0] + xa[1]
            odd_re, odd_im = yb[0] + ya[1], ya[0] - yb[1]
            for k in range(2):
                w_sin, w_cos = turned[k]
                image_re = even_re - odd_re if k == 0 else even_re + odd_re
                image_im = even_im + odd_im if k == 0 else even_im - odd_im
                fields.append(
                    jnp.concatenate(
                        [image_re * w_cos - image_im * w_sin, image_re * w_sin + image_im * w_cos], 1
                    )
                )
                yield

    def imaging(pair):
        finished[...] = totals[...]
        fields = [], []
        second = fields_of(2 * pair + 1, 1, fields[1])
        for _ in fields_of(2 * pair, 0, fields[0]):
            next(second)
            yield
        run(second)
        pieces = [split_hi_lo(field) for field in fields[0] + fields[1]]
        yield
        high = jnp.concatenate([piece[0] for piece in pieces], 0)
        low = jnp.concatenate([piece[1] for piece in pieces], 0)
        count = high.shape[0]
        both = jnp.dot(jnp.concatenate([high, low], 0), right_ref[0:256, :], preferred_element_type=jnp.float32)
        rows = jnp.dot(high, right_ref[256:512, :], preferred_element_type=jnp.float32)
        yield
        rows = rows + (both[:count] + both[count:])
        for index in range(4):
            side, pol = index // 2, index % 2
            first = (2 * pair + side) * GROUP
            out_ref = (mine_ref, other_ref)[pol]
            high, low = split_hi_lo(rows[index * 32 : index * 32 + 32])
            stack = jnp.concatenate(
                [high[:, :128], high[:, 128:], low[:, :128], low[:, 128:], high[:, :128], high[:, 128:]], 0
            )
            yield
            uv = jnp.dot(left_ref[...], stack, preferred_element_type=jnp.float32)
            yield
            for part in range(2):
                outs = swap_groups(
                    [uv[part * 32 + k * 8 : part * 32 + k * 8 + 8] for k in range(4)], lane < 64, (lane & 32) == 32
                )
                for g in range(GROUP):
                    out_ref[first + g, part * 8 : part * 8 + 8, :] = outs[g]
                yield

    def run(work):
        for _ in work:
            pass

    pairs = groups // 2
    run(gridding(0, 0))
    run(gridding(1, 1))
    if placing:
        owner_copy.wait()
        each = -(-tile_ref.shape[0] // (pairs - 1))

    def both(pair, carry):
        if placing:
            place_items((pair - 1) * each, each, tile_ref, owner_ref, row_ref, slot_ref)
        work = imaging(pair - 1)
        next(work)
        for step, _ in enumerate(gridding(2 * pair, 0)):
            if step % 2 == 0:
                next(work, None)
        for step, _ in enumerate(gridding(2 * pair + 1, 1)):
            if step % 2 == 0:
                next(work, None)
        run(work)
        return carry

    lax.fori_loop(1, pairs, both, 0)
    run(imaging(pairs - 1))


def pack_kernel(section_ref, row_ref, slot_ref, *refs):
    packed = refs[-1]
    section = section_ref[0]
    half = row_ref.shape[0] // 2
    width = packed.shape[0] // (slot_ref.shape[0] // 2)
    packed[...] = jnp.zeros_like(packed)
    lane = lax.broadcasted_iota(jnp.int32, (1, 128), 1)

    def note(step, carry):
        for k in range(2):
            target = step * 2 + k
            slots = jnp.where(lane == 0, slot_ref[2 * target], slot_ref[2 * target + 1])
            packed[pl.ds(target * width + width - 1, 1), :] = slots.astype(jnp.float32)
        return carry

    lax.fori_loop(0, slot_ref.shape[0] // 4, note, 0)
    start = section * half
    for values in refs[: len(CHUNKS)]:
        add_rows(row_ref, start, width, values, packed)
        start = start + values.shape[0]
    start = (1 - section) * half
    for values in refs[len(CHUNKS) : -1]:
        add_rows(row_ref, start, width, values, packed)
        start = start + values.shape[0]


def pack_more_kernel(section_ref, row_ref, before_ref, values, packed):
    half = row_ref.shape[0] // 2
    packed[...] = before_ref[...]
    add_rows(row_ref, (2 - section_ref[0]) * half - values.shape[0], 33, values, packed)


def add_rows(row_ref, start, width, values, packed):
    def add(step, carry):
        for k in range(16):
            item = step * 16 + k
            row = row_ref[start + item]
            top = (row >> 1) * width + (row & 1) * 16
            packed[pl.ds(top, 16), :] = packed[pl.ds(top, 16), :] + values[item]
        return carry

    lax.fori_loop(0, values.shape[0] // 16, add, 0)


def unpack_kernel(received_ref, out_ref):
    tiles_dev = out_ref.shape[0]
    sources = received_ref.shape[0] // 33
    slots = received_ref[pl.ds(32, sources, stride=33), :].T
    row = jnp.concatenate([slots[0:1, :], slots[1:2, :]], 1)
    tile = lax.broadcasted_iota(jnp.int32, (tiles_dev, 2 * sources), 0).astype(jnp.float32)
    picked = jnp.where(tile == row, 1.0, 0.0).astype(jnp.bfloat16)
    picked = jnp.concatenate([picked, picked], 1)
    for pair in range(8):
        columns = []
        for column in (2 * pair, 2 * pair + 1):
            values = jnp.concatenate(
                [received_ref[pl.ds(16 * rank + column, sources, stride=33), :] for rank in range(2)], 0
            )
            columns.append(jnp.concatenate(split_hi_lo(values), 0))
        out_ref[:, pair * 256 : (pair + 1) * 256] = jnp.dot(
            picked, jnp.concatenate(columns, 1), preferred_element_type=jnp.float32
        )


SMEM = pl.BlockSpec(memory_space=pltpu.SMEM)
VMEM = pl.BlockSpec(memory_space=pltpu.VMEM)
HBM = pl.BlockSpec(memory_space=pltpu.HBM)


def call(kernel, out_shape, in_specs, out_specs, scratch=(), flops=1_000_000, moved=1_000_000, mib=8):
    return pl.pallas_call(
        kernel,
        out_shape=out_shape,
        in_specs=in_specs,
        out_specs=out_specs,
        scratch_shapes=list(scratch),
        compiler_params=pltpu.CompilerParams(vmem_limit_bytes=mib * 1024 * 1024),
        cost_estimate=pl.CostEstimate(flops=flops, bytes_accessed=moved, transcendentals=0),
    )


def device_program(visibilities, uv_coords, w_terms, stations, tile_ids, owner_map, jones_gains):
    sub_count = visibilities.shape[1]
    samples = visibilities.shape[4] * visibilities.shape[5]
    half = sub_count // 2
    grid_size = lax.axis_size("grid")
    tiles_dev = owner_map.shape[0] // grid_size
    section_index = lax.axis_index("section").astype(jnp.int32)
    section = section_index.reshape(1)
    swap = [(0, 1), (1, 0)]
    shape_f32 = lambda *shape: jax.ShapeDtypeStruct(shape, jnp.float32)
    shape_i32 = lambda *shape: jax.ShapeDtypeStruct(shape, jnp.int32)

    peers, start = [], 0
    for size in CHUNKS:
        part = lax.dynamic_slice_in_dim(visibilities[0], (1 - section_index) * half + start, size, 0)
        peers.append(lax.ppermute(part, "section", swap))
        start += size
    own = lax.dynamic_slice_in_dim(visibilities[0], section_index * half, half, 0)
    coefs = call(
        prep_kernel, shape_f32(16, 16, 128), [SMEM, SMEM, VMEM], VMEM, [pltpu.VMEM((128, 128), jnp.float32)] * 3
    )(section, stations, jones_gains)

    constants = [jnp.asarray(table) for table in tables(samples)]
    uv_rows = uv_coords.reshape(2 * sub_count, uv_coords.shape[2])
    mine, theirs, start = [], [], 0
    for chunk, size in enumerate(CHUNKS):
        placing = chunk == len(CHUNKS) - 1
        results = call(
            lambda *refs, start=start, placing=placing: grid_kernel(start, placing, *refs),
            (shape_f32(size, 16, 128),) * 2 + ((shape_i32(sub_count), shape_i32(2 * grid_size)) if placing else ()),
            [SMEM, SMEM] + [VMEM] * 7 + ([SMEM, HBM] if placing else []),
            (VMEM, VMEM) + ((SMEM, SMEM) if placing else ()),
            [
                pltpu.VMEM((2, GROUP, 64, 128), jnp.float32),
                pltpu.VMEM((2, 16, 16, 128), jnp.float32),
                pltpu.VMEM((2, 56, 128), jnp.float32),
                pltpu.VMEM((2, GROUP, 32, 128), jnp.float32),
                pltpu.VMEM((2, GROUP, 32, 128), jnp.float32),
            ]
            + ([pltpu.SMEM(owner_map.shape, jnp.int32), pltpu.SemaphoreType.DMA] if placing else []),
            flops=size * 300_000_000,
            moved=size * 100_000,
            mib=12,
        )(
            section, w_terms, coefs, own, peers[chunk], uv_rows, *constants,
            *((tile_ids, owner_map) if placing else ()),
        )
        coefs = lax.optimization_barrier((coefs, results[0]))[0]
        mine.append(results[0])
        theirs.append(lax.ppermute(results[1], "section", swap))
        start += size
    row_index, slots = results[2:]

    packed_shape = shape_f32(33 * grid_size, 128)
    packed = call(
        pack_kernel, packed_shape, [SMEM] * 3 + [VMEM] * (2 * len(CHUNKS) - 1), VMEM, flops=100_000_000
    )(section, row_index, slots, *mine, *theirs[:-1])
    packed = call(pack_more_kernel, packed_shape, [SMEM] * 2 + [VMEM] * 2, VMEM)(section, row_index, packed, theirs[-1])
    received = lax.all_to_all(
        packed.reshape(grid_size, 1, 33 * 128), "grid", split_axis=0, concat_axis=0, tiled=True
    ).reshape(33 * grid_size, 128)
    tiles = call(unpack_kernel, shape_f32(tiles_dev, 2048), [VMEM], VMEM)(received)
    return tiles[None]


def solution(mesh):
    in_specs = (
        P("section", "grid", None, None, None, None),
        P("grid", None, None),
        P("grid"),
        P(None, "grid"),
        P("grid"),
        P(),
        P(),
    )
    out_specs = P("section", "grid", None)
    return jax.shard_map(device_program, mesh=mesh, in_specs=in_specs, out_specs=out_specs, check_vma=False)
```

```python
import math

import numpy as np
import jax
import jax.numpy as jnp
from jax import lax
from jax.experimental import pallas as pl
from jax.experimental.pallas import tpu as pltpu
from jax.sharding import PartitionSpec as P

SIDE = 32
CHUNKS = (48,)
GROUP = 4

PIXELS = np.concatenate([np.arange(16), -1 - np.arange(16)]).astype(np.float64)


def fit_even(function, reach, terms):
    nodes = np.cos(np.pi * (np.arange(64) + 0.5) / 64)
    square = (nodes + 1.0) / 2.0 * reach * reach
    cheb = np.polynomial.chebyshev.chebfit(nodes, function(np.sqrt(square)), terms - 1)
    poly = np.polynomial.chebyshev.cheb2poly(cheb)
    shift = np.polynomial.polynomial.Polynomial(poly)(
        np.polynomial.polynomial.Polynomial([-1.0, 2.0 / (reach * reach)])
    )
    return [float(np.float32(value)) for value in shift.coef]


def sinc_turns(scale):
    return lambda x: np.where(x > 0, np.sin(scale * x) / np.maximum(x, 1e-30), scale)


HALF_SIN = fit_even(sinc_turns(np.pi), 0.5, 5)
HALF_COS = fit_even(lambda x: np.cos(np.pi * x), 0.5, 5)
STEP_SIN = fit_even(sinc_turns(2 * np.pi), 0.0625, 3)
STEP_COS = fit_even(lambda x: np.cos(2 * np.pi * x), 0.0625, 4)


def horner(coefs, square):
    total = square * coefs[-1] + coefs[-2]
    for value in coefs[-3::-1]:
        total = total * square + value
    return total


def sincos_half(x):
    square = x * x
    half_sin = x * horner(HALF_SIN, square)
    half_cos = horner(HALF_COS, square)
    twice = half_sin + half_sin
    return twice * half_cos, 1.0 - twice * half_sin


def sincos_turns(x):
    return sincos_half(x - jnp.round(x))


def sincos_step(x):
    square = x * x
    return x * horner(STEP_SIN, square), horner(STEP_COS, square)


def spread(ref, row):
    return ref[pl.ds(row, 8, stride=0), :]


def split_hi_lo(values):
    high = values.astype(jnp.bfloat16)
    low = (values - high.astype(jnp.float32)).astype(jnp.bfloat16)
    return high, low


def np_split(values):
    high = np.asarray(values, np.float32).astype(jnp.bfloat16)
    low = (np.asarray(values, np.float32) - high.astype(np.float32)).astype(jnp.bfloat16)
    return high, low


def tables(samples):
    row_p = PIXELS[:, None]
    lane_p = np.tile(PIXELS, GROUP)[None, :]
    sine_row, sine_lane = 0.6 * row_p / SIDE, 0.6 * lane_p / SIDE
    n_term = np.sqrt(1.0 - sine_row**2 - sine_lane**2) - 1.0
    taper = np.cos(np.pi * row_p / (SIDE + 4.0)) * np.cos(np.pi * lane_p / (SIDE + 4.0))
    pixel_tables = np.stack([n_term, taper / math.sqrt(samples) / SIDE]).astype(np.float32)

    freq = np.arange(SIDE) - SIDE // 2
    angle = 2.0 * np.pi / SIDE * PIXELS[:, None] * freq[None, :]
    cos_t = np.kron(np.eye(GROUP), np.cos(angle))
    sin_t = np.kron(np.eye(GROUP), np.sin(angle))
    high, low = np_split(np.block([[cos_t, -sin_t], [sin_t, cos_t]]))
    right_all = np.concatenate([high, low], 0)

    order = np.arange(SIDE).reshape(8, 4).T.reshape(-1)
    angle = 2.0 * np.pi / SIDE * freq[order][:, None] * PIXELS[None, :]
    high, low = np_split(np.block([[np.cos(angle), np.sin(angle)], [-np.sin(angle), np.cos(angle)]]))
    left_all = np.concatenate([high, high, low], 1)
    return pixel_tables, right_all, left_all


def swap_groups(parts, low_half, odd_quarter):
    a0 = jnp.where(low_half, parts[0], pltpu.roll(parts[2], 64, 1))
    a2 = jnp.where(low_half, pltpu.roll(parts[0], 64, 1), parts[2])
    a1 = jnp.where(low_half, parts[1], pltpu.roll(parts[3], 64, 1))
    a3 = jnp.where(low_half, pltpu.roll(parts[1], 64, 1), parts[3])
    return [
        jnp.where(odd_quarter, pltpu.roll(a1, 32, 1), a0),
        jnp.where(odd_quarter, a1, pltpu.roll(a0, 96, 1)),
        jnp.where(odd_quarter, pltpu.roll(a3, 32, 1), a2),
        jnp.where(odd_quarter, a3, pltpu.roll(a2, 96, 1)),
    ]


def prep_kernel(section_ref, stations_ref, jones_ref, coef_ref, p_rows, q_rows, turned):
    section = section_ref[0]
    half = stations_ref.shape[1] // 2

    p_rows[...] = jnp.zeros_like(p_rows)
    q_rows[...] = jnp.zeros_like(q_rows)

    def fetch(step, carry):
        for k in range(8):
            item = section * half + step * 8 + k
            p_rows[pl.ds(step * 8 + k, 1), :] = jones_ref[pl.ds(stations_ref[0, item], 1), :]
            q_rows[pl.ds(step * 8 + k, 1), :] = jones_ref[pl.ds(stations_ref[1, item], 1), :]
        return carry

    lax.fori_loop(0, half // 8, fetch, 0)
    lane = lax.broadcasted_iota(jnp.int32, (128, 128), 1)
    odd = (lane & 1) == 1
    high_pair = (lane & 2) == 2

    def swap_one(x):
        return jnp.where(odd, pltpu.roll(x, 1, 1), pltpu.roll(x, 127, 1))

    def swap_two(x):
        return jnp.where(high_pair, pltpu.roll(x, 2, 1), pltpu.roll(x, 126, 1))

    gain_p = p_rows[...]
    gain_p_turned = swap_one(gain_p)
    for kind in range(2):
        gain_q = q_rows[...] if kind == 0 else swap_two(q_rows[...])
        straight = gain_p * gain_q
        crossed = gain_p_turned * gain_q
        real = straight + swap_one(straight)
        imag = swap_one(crossed) - crossed
        turned[...] = jnp.where(odd, imag, real).T
        for place in range(8):
            coef_ref[kind * 8 + place] = turned[pl.ds(place, 16, stride=8), :]


def clear_slots(slot_ref):
    for target in range(slot_ref.shape[0]):
        slot_ref[target] = -1


def place_items(first, count, tile_ref, owner_ref, row_ref, slot_ref):
    tiles_dev = owner_ref.shape[0] // (slot_ref.shape[0] // 2)
    shift = tiles_dev.bit_length() - 1
    assert tiles_dev == 1 << shift
    for k in range(count):
        item = jnp.minimum(first + k, tile_ref.shape[0] - 1)
        position = owner_ref[tile_ref[item]]
        target = 2 * (position >> shift)
        slot = position & (tiles_dev - 1)
        known = slot_ref[target]
        row = target + jnp.where((known == -1) | (known == slot), 0, 1)
        slot_ref[row] = slot
        row_ref[item] = row


def grid_kernel(chunk_start, placing, section_ref, w_ref, coef_ref, own_ref, peer_ref, uv_ref, pixel_ref, right_ref,
                left_ref, *refs):
    if placing:
        tile_ref, owner_any, mine_ref, other_ref, row_ref, slot_ref = refs[:6]
        owner_ref, owner_sem = refs[-2:]
        owner_copy = pltpu.make_async_copy(owner_any, owner_ref, owner_sem)
        owner_copy.start()
        clear_slots(slot_ref)
    else:
        mine_ref, other_ref = refs[:2]
    start = 6 if placing else 2
    bcast_all, rolled_all, rows_all, totals, finished = refs[start : start + 5]
    section = section_ref[0]
    groups = mine_ref.shape[0] // GROUP
    half = w_ref.shape[0] // 2
    lane = lax.broadcasted_iota(jnp.int32, (8, 128), 1)
    sub_lane = lax.broadcasted_iota(jnp.int32, (8, 128), 0).astype(jnp.float32)

    def gridding(group, side):
        first = group * GROUP
        bcast, rolled, wave_rows = bcast_all.at[side], rolled_all.at[side], rows_all.at[side]
        shift = lax.rem(128 - (chunk_start + first), 128)
        for place in range(16):
            rolled[place] = pltpu.roll(coef_ref[place], shift, 1)
        cells = uv_ref[pl.ds(pl.multiple_of(section * (2 * half) + 2 * (chunk_start + first), 8), 8), :]
        wave_rows[0:8], wave_rows[8:16] = sincos_turns(cells * (8.0 / SIDE))
        wave_rows[16:24], wave_rows[24:32] = sincos_step(cells * (8.0 / (64.0 * SIDE)))
        sums = cells + pltpu.roll(cells, 7, 0)
        wave_rows[32:40], wave_rows[40:48] = sincos_step(sums * (8.0 / (128.0 * SIDE)))
        wave_rows[48:56] = cells
        for g in range(GROUP):
            corr = [None, None]
            for row in range(2):
                for kind in range(2):
                    column = (row ^ section) ^ kind
                    source = own_ref if row == 0 else peer_ref
                    at = first + g + (chunk_start if row == 0 else 0)
                    vis_real = source[at, column, 0]
                    vis_imag = source[at, column, 1]
                    for pol in range(2):
                        place = kind * 8 + (pol ^ section) * 4 + (row ^ section) * 2
                        cr = jnp.broadcast_to(rolled[place][:, g : g + 1], (16, 128))
                        ci = jnp.broadcast_to(rolled[place + 1][:, g : g + 1], (16, 128))
                        real = cr * vis_real - ci * vis_imag
                        imag = cr * vis_imag + ci * vis_real
                        if corr[pol] is None:
                            corr[pol] = [real, imag]
                        else:
                            corr[pol] = [corr[pol][0] + real, corr[pol][1] + imag]
            u_row = spread(wave_rows, 48 + 2 * g)
            v_row = spread(wave_rows, 49 + 2 * g)
            turn_sin, turn_cos = sincos_half((u_row + v_row) * ((1.0 + sub_lane / 64.0) / (2.0 * SIDE)))
            step_sin, step_cos = spread(wave_rows, 32 + 2 * g), spread(wave_rows, 40 + 2 * g)
            turn_sin, turn_cos = (
                jnp.concatenate([turn_sin, turn_sin * step_cos + turn_cos * step_sin], 0),
                jnp.concatenate([turn_cos, turn_cos * step_cos - turn_sin * step_sin], 0),
            )
            for pol in range(2):
                real, imag = corr[pol]
                bcast[g, pol * 16 : pol * 16 + 16] = real * turn_cos + imag * turn_sin
                bcast[g, 32 + pol * 16 : 48 + pol * 16] = imag * turn_cos - real * turn_sin
            yield

            waves = []
            for axis, cell in enumerate((u_row, v_row)):
                turns = cell * ((sub_lane + 0.5) / SIDE)
                sin_0, cos_0 = sincos_turns(turns)
                sin_d, cos_d = sincos_step(turns * (1.0 / 64.0))
                place = 2 * g + axis
                up_sin, up_cos = spread(wave_rows, place), spread(wave_rows, 8 + place)
                upd_sin, upd_cos = spread(wave_rows, 16 + place), spread(wave_rows, 24 + place)
                cos_0, sin_0, cos_d, sin_d = (
                    jnp.stack([cos_0, cos_0 * up_cos - sin_0 * up_sin]),
                    jnp.stack([sin_0, sin_0 * up_cos + cos_0 * up_sin]),
                    jnp.stack([cos_d, cos_d * upd_cos - sin_d * upd_sin]),
                    jnp.stack([sin_d, sin_d * upd_cos + cos_d * upd_sin]),
                )
                cos_1 = cos_0 * cos_d - sin_0 * sin_d
                sin_1 = sin_0 * cos_d + cos_0 * sin_d
                waves.append([cos_0, sin_0, cos_1, sin_1, cos_d + cos_d])
            yield
            total = None
            for pair in range(8):
                left_parts, right_parts = [], []
                for c in (2 * pair, 2 * pair + 1):
                    cos_u, sin_u = waves[0][0], waves[0][1]
                    cos_v, sin_v = waves[1][0], waves[1][1]
                    left_parts.append(jnp.concatenate([cos_u, sin_u], 0).reshape(32, 128))
                    pieces = []
                    for k in range(4):
                        line = spread(bcast.at[g], 16 * k + c)[None]
                        pieces.append((cos_v * line).reshape(16, 128))
                        pieces.append((sin_v * line).reshape(16, 128))
                    right_parts.append(jnp.concatenate(pieces, 0))
                    for wave in waves:
                        cos_0, sin_0, cos_1, sin_1, twice = wave
                        wave[0], wave[1] = cos_1, sin_1
                        if c < 14:
                            wave[2], wave[3] = twice * cos_1 - cos_0, twice * sin_1 - sin_0
                part = lax.dot_general(
                    jnp.concatenate(left_parts, 1),
                    jnp.concatenate(right_parts, 1),
                    (((1,), (1,)), ((), ())),
                    preferred_element_type=jnp.float32,
                )
                total = part if total is None else total + part
                yield
            totals[side, g] = total

    def fields_of(group, side, fields):
        first = group * GROUP
        lane16 = lax.broadcasted_iota(jnp.int32, (16, 128), 1)
        upper = (lane16 & 16) == 16
        sign = jnp.where(upper, -1.0, 1.0)
        low_half, odd_quarter = lane16 < 64, (lane16 & 32) == 32
        w_first = section * half + chunk_start + first
        w_row = jnp.where(
            lane < 64,
            jnp.where(lane < 32, w_ref[w_first], w_ref[w_first + 1]),
            jnp.where(lane < 96, w_ref[w_first + 2], w_ref[w_first + 3]),
        )
        w_row = jnp.concatenate([w_row, w_row], 0)
        turned = []
        for k in range(2):
            rows = slice(k * 16, k * 16 + 16)
            w_sin, w_cos = sincos_turns(pixel_ref[0, rows] * w_row)
            turned.append((w_sin * pixel_ref[1, rows], w_cos * pixel_ref[1, rows]))
            yield
        parts = []
        for k in range(2):
            sums = swap_groups(
                [finished[side, g, k * 16 : k * 16 + 16] for g in range(GROUP)], low_half, odd_quarter
            )
            yield
            for value in sums:
                parts.append(
                    (
                        jnp.where(upper, pltpu.roll(value, 16, 1), value),
                        sign * jnp.where(upper, value, pltpu.roll(value, 112, 1)),
                    )
                )
                yield
        for pol in range(2):
            xa, xb, ya, yb = parts[pol], parts[2 + pol], parts[4 + pol], parts[6 + pol]
            even_re, even_im = xa[0] - xb[1], xb[0] + xa[1]
            odd_re, odd_im = yb[0] + ya[1], ya[0] - yb[1]
            for k in range(2):
                w_sin, w_cos = turned[k]
                image_re = even_re - odd_re if k == 0 else even_re + odd_re
                image_im = even_im + odd_im if k == 0 else even_im - odd_im
                fields.append(
                    jnp.concatenate(
                        [image_re * w_cos - image_im * w_sin, image_re * w_sin + image_im * w_cos], 1
                    )
                )
                yield

    def imaging(pair):
        finished[...] = totals[...]
        fields = [], []
        second = fields_of(2 * pair + 1, 1, fields[1])
        for _ in fields_of(2 * pair, 0, fields[0]):
            next(second)
            yield
        run(second)
        pieces = [split_hi_lo(field) for field in fields[0] + fields[1]]
        yield
        high = jnp.concatenate([piece[0] for piece in pieces], 0)
        low = jnp.concatenate([piece[1] for piece in pieces], 0)
        count = high.shape[0]
        both = jnp.dot(jnp.concatenate([high, low], 0), right_ref[0:256, :], preferred_element_type=jnp.float32)
        rows = jnp.dot(high, right_ref[256:512, :], preferred_element_type=jnp.float32)
        yield
        rows = rows + (both[:count] + both[count:])
        for index in range(4):
            side, pol = index // 2, index % 2
            first = (2 * pair + side) * GROUP
            out_ref = (mine_ref, other_ref)[pol]
            high, low = split_hi_lo(rows[index * 32 : index * 32 + 32])
            stack = jnp.concatenate(
                [high[:, :128], high[:, 128:], low[:, :128], low[:, 128:], high[:, :128], high[:, 128:]], 0
            )
            yield
            uv = jnp.dot(left_ref[...], stack, preferred_element_type=jnp.float32)
            yield
            for part in range(2):
                outs = swap_groups(
                    [uv[part * 32 + k * 8 : part * 32 + k * 8 + 8] for k in range(4)], lane < 64, (lane & 32) == 32
                )
                for g in range(GROUP):
                    out_ref[first + g, part * 8 : part * 8 + 8, :] = outs[g]
                yield

    def run(work):
        for _ in work:
            pass

    pairs = groups // 2
    run(gridding(0, 0))
    run(gridding(1, 1))
    if placing:
        owner_copy.wait()
        each = -(-tile_ref.shape[0] // (pairs - 1))

    def both(pair, carry):
        if placing:
            place_items((pair - 1) * each, each, tile_ref, owner_ref, row_ref, slot_ref)
        work = imaging(pair - 1)
        next(work)
        for step, _ in enumerate(gridding(2 * pair, 0)):
            if step % 2 == 0:
                next(work, None)
        for step, _ in enumerate(gridding(2 * pair + 1, 1)):
            if step % 2 == 0:
                next(work, None)
        run(work)
        return carry

    lax.fori_loop(1, pairs, both, 0)
    run(imaging(pairs - 1))


def pack_kernel(section_ref, row_ref, slot_ref, *refs):
    packed = refs[-1]
    section = section_ref[0]
    half = row_ref.shape[0] // 2
    width = packed.shape[0] // (slot_ref.shape[0] // 2)
    packed[...] = jnp.zeros_like(packed)
    lane = lax.broadcasted_iota(jnp.int32, (1, 128), 1)

    def note(step, carry):
        for k in range(2):
            target = step * 2 + k
            slots = jnp.where(lane == 0, slot_ref[2 * target], slot_ref[2 * target + 1])
            packed[pl.ds(target * width + width - 1, 1), :] = slots.astype(jnp.float32)
        return carry

    lax.fori_loop(0, slot_ref.shape[0] // 4, note, 0)
    start = section * half
    for values in refs[: len(CHUNKS)]:
        add_rows(row_ref, start, width, values, packed)
        start = start + values.shape[0]
    start = (1 - section) * half
    for values in refs[len(CHUNKS) : -1]:
        add_rows(row_ref, start, width, values, packed)
        start = start + values.shape[0]


def pack_more_kernel(section_ref, row_ref, before_ref, values, packed):
    half = row_ref.shape[0] // 2
    packed[...] = before_ref[...]
    add_rows(row_ref, (2 - section_ref[0]) * half - values.shape[0], 33, values, packed)


def add_rows(row_ref, start, width, values, packed):
    def add(step, carry):
        for k in range(16):
            item = step * 16 + k
            row = row_ref[start + item]
            top = (row >> 1) * width + (row & 1) * 16
            packed[pl.ds(top, 16), :] = packed[pl.ds(top, 16), :] + values[item]
        return carry

    lax.fori_loop(0, values.shape[0] // 16, add, 0)


def unpack_kernel(received_ref, out_ref):
    tiles_dev = out_ref.shape[0]
    sources = received_ref.shape[0] // 33
    slots = received_ref[pl.ds(32, sources, stride=33), :].T
    row = jnp.concatenate([slots[0:1, :], slots[1:2, :]], 1)
    tile = lax.broadcasted_iota(jnp.int32, (tiles_dev, 2 * sources), 0).astype(jnp.float32)
    picked = jnp.where(tile == row, 1.0, 0.0).astype(jnp.bfloat16)
    picked = jnp.concatenate([picked, picked], 1)
    for pair in range(8):
        columns = []
        for column in (2 * pair, 2 * pair + 1):
            values = jnp.concatenate(
                [received_ref[pl.ds(16 * rank + column, sources, stride=33), :] for rank in range(2)], 0
            )
            columns.append(jnp.concatenate(split_hi_lo(values), 0))
        out_ref[:, pair * 256 : (pair + 1) * 256] = jnp.dot(
            picked, jnp.concatenate(columns, 1), preferred_element_type=jnp.float32
        )


SMEM = pl.BlockSpec(memory_space=pltpu.SMEM)
VMEM = pl.BlockSpec(memory_space=pltpu.VMEM)
HBM = pl.BlockSpec(memory_space=pltpu.HBM)


def call(kernel, name, out_shape, in_specs, out_specs, scratch=(), flops=1_000_000, moved=1_000_000, mib=8, flags=None):
    return pl.pallas_call(
        kernel,
        out_shape=out_shape,
        in_specs=in_specs,
        out_specs=out_specs,
        scratch_shapes=list(scratch),
        compiler_params=pltpu.CompilerParams(vmem_limit_bytes=mib * 1024 * 1024, flags=flags),
        cost_estimate=pl.CostEstimate(flops=flops, bytes_accessed=moved, transcendentals=0),
        name=name,
    )


def shards(visibilities, uv_coords, w_terms, stations, tile_ids, owner_map, jones_gains):
    sub_count = visibilities.shape[1]
    samples = visibilities.shape[4] * visibilities.shape[5]
    half = sub_count // 2
    grid_size = lax.axis_size("grid")
    tiles_dev = owner_map.shape[0] // grid_size
    section_index = lax.axis_index("section").astype(jnp.int32)
    section = section_index.reshape(1)
    swap = [(0, 1), (1, 0)]
    shape_f32 = lambda *shape: jax.ShapeDtypeStruct(shape, jnp.float32)
    shape_i32 = lambda *shape: jax.ShapeDtypeStruct(shape, jnp.int32)

    peers, start = [], 0
    for size in CHUNKS:
        part = lax.dynamic_slice_in_dim(visibilities[0], (1 - section_index) * half + start, size, 0)
        peers.append(lax.ppermute(part, "section", swap))
        start += size
    own = lax.dynamic_slice_in_dim(visibilities[0], section_index * half, half, 0)
    coefs = call(
        prep_kernel,
        "prep",
        shape_f32(16, 16, 128),
        [SMEM, SMEM, VMEM],
        VMEM,
        [pltpu.VMEM((128, 128), jnp.float32)] * 3,
    )(section, stations, jones_gains)

    constants = [jnp.asarray(table) for table in tables(samples)]
    uv_rows = uv_coords.reshape(2 * sub_count, uv_coords.shape[2])
    mine, theirs, start = [], [], 0
    for chunk, size in enumerate(CHUNKS):
        placing = chunk == len(CHUNKS) - 1
        results = call(
            lambda *refs, start=start, placing=placing: grid_kernel(start, placing, *refs),
            "grid_chunk",
            (shape_f32(size, 16, 128),) * 2 + ((shape_i32(sub_count), shape_i32(2 * grid_size)) if placing else ()),
            [SMEM, SMEM] + [VMEM] * 7 + ([SMEM, HBM] if placing else []),
            (VMEM, VMEM) + ((SMEM, SMEM) if placing else ()),
            [
                pltpu.VMEM((2, GROUP, 64, 128), jnp.float32),
                pltpu.VMEM((2, 16, 16, 128), jnp.float32),
                pltpu.VMEM((2, 56, 128), jnp.float32),
                pltpu.VMEM((2, GROUP, 32, 128), jnp.float32),
                pltpu.VMEM((2, GROUP, 32, 128), jnp.float32),
            ]
            + ([pltpu.SMEM(owner_map.shape, jnp.int32), pltpu.SemaphoreType.DMA] if placing else []),
            flops=size * 300_000_000,
            moved=size * 100_000,
            mib=12,
        )(
            section, w_terms, coefs, own, peers[chunk], uv_rows, *constants,
            *((tile_ids, owner_map) if placing else ()),
        )
        mine.append(results[0])
        theirs.append(lax.ppermute(results[1], "section", swap))
        start += size
    row_index, slots = results[2:]

    packed_shape = shape_f32(33 * grid_size, 128)
    packed = call(
        pack_kernel, "pack", packed_shape, [SMEM] * 3 + [VMEM] * (2 * len(CHUNKS) - 1), VMEM, flops=100_000_000
    )(section, row_index, slots, *mine, *theirs[:-1])
    packed = call(pack_more_kernel, "pack_more", packed_shape, [SMEM] * 2 + [VMEM] * 2, VMEM)(
        section, row_index, packed, theirs[-1]
    )
    received = lax.all_to_all(
        packed.reshape(grid_size, 1, 33 * 128), "grid", split_axis=0, concat_axis=0, tiled=True
    ).reshape(33 * grid_size, 128)
    tiles = call(unpack_kernel, "unpack", shape_f32(tiles_dev, 2048), [VMEM], VMEM)(received)
    return tiles[None]


def solution(mesh):
    in_specs = (
        P("section", "grid", None, None, None, None),
        P("grid", None, None),
        P("grid"),
        P(None, "grid"),
        P("grid"),
        P(),
        P(),
    )
    out_specs = P("section", "grid", None)
    return jax.shard_map(shards, mesh=mesh, in_specs=in_specs, out_specs=out_specs, check_vma=False)
```
